256 devices in a mesh: atom: 8 (over x, z_hi), slab: 32 (over y, z_lo, core).
Axes of the slice: x: 4, y: 4, z: 8 (z_hi: 2, z_lo: 4; z = z_hi * 4 + z_lo), core: 2. Of those that a mesh axis runs over, the one named last changes fastest.
Arguments:
- atom_log_density: float32 [8, 512, 64, 512], P('atom', 'slab'), may hold values from -123 to 121
- prior_log_scaling: float32 [8, 512, 64, 512], P('atom', 'slab'), may hold values from -5 to 115
- atom_cotangent_rows: float32 [8, 512, 64, 512], P('atom', 'slab'), may hold values from -6 to 6
- barycenter_cotangent: float32 [512, 64, 512], P('slab'), may hold values from -6 to 6
- weights: float32 [8], replicated, may hold values from 0.2 to 1
- band: int32 [3], replicated, may hold values from 1 to 8, as said below
- slot_atom_index: int32 [8], replicated, may hold values from 0 to 7, each once
Outputs:
- log_atom_gradient: float32 [8, 512, 64, 512], P('atom', 'slab')
- weight_grad: float32 [8], replicated
The draws below stay inside these ranges and needn't reach their ends.
Inputs may be any that keep to these rules, and one draw needn't show every extreme that they name: `band`: at least one entry equals 8. `slot_atom_index`: each atom is held in exactly one slot.
All inputs are finite; a program needn't handle non-finite values.
Results may differ from the reference program's by a relative error of at most 0.0003.
Values sent between devices are 32-bit elements; how exact they have to be, the bound alone decides.
No kernel may reach another device: no remote copies, remote signals or barrier semaphores. Data moves between devices by JAX's collectives and lax.ppermute only.
A program may use at most 64 MiB of HBM per device.

```python
import jax
import jax.numpy as jnp
from jax import lax

NX = 512
NY = 64
PLANES = 16
BAND_MAX = 8
ATOMS = 8
NZ = 512


def draw_atom_log_density(key, part):
    first_key, second_key, third_key = jax.random.split(jax.random.fold_in(key, 23), 3)
    rough = jax.random.uniform(first_key, (ATOMS, NZ, NY, NX), jnp.float32, -3.0, 1.0)
    ranks = jax.random.permutation(second_key, ATOMS).astype(jnp.float32)
    levels = -115.0 + 230.0 * ranks / max(ATOMS - 1, 1)
    slab_offset = jax.random.uniform(third_key, (ATOMS, NZ // PLANES, 1, 1), jnp.float32, -5.0, 5.0)
    slab_offset = jnp.repeat(slab_offset, PLANES, axis=1)
    return (rough + slab_offset + levels[:, None, None, None]).astype(jnp.float32)


def draw_prior_log_scaling(key, part):
    first_key, second_key, third_key = jax.random.split(jax.random.fold_in(key, 11), 3)
    rough = jax.random.uniform(first_key, (ATOMS, NZ, NY, NX), jnp.float32, -3.0, 3.0)
    slab_level = jax.random.uniform(third_key, (ATOMS, NZ // PLANES, 1, 1), jnp.float32, 0.0, 8.0)
    slab_level = jnp.repeat(slab_level, PLANES, axis=1)
    offset = jax.random.uniform(second_key, (ATOMS, 1, 1, 1), jnp.float32, -2.0, 2.0)
    return (rough + slab_level + offset).astype(jnp.float32)


def draw_band(key, part):
    raw_bits = jax.random.bits(key, (4,), jnp.uint32)
    widths = (raw_bits[:3] % BAND_MAX).astype(jnp.int32) + 1
    chosen = (raw_bits[3] % 3).astype(jnp.int32)
    return jnp.where(jnp.arange(3, dtype=jnp.int32) == chosen, jnp.int32(BAND_MAX), widths).astype(jnp.int32)


def shard_levels(own_key, dims, cuts, least, largest):
    def one(axis_at, parts):
        steps = jax.random.uniform(jax.random.fold_in(jax.random.fold_in(own_key, 6), axis_at), (parts,), jnp.float32, least / len(cuts), largest / len(cuts))
        return jnp.repeat(jnp.exp(steps), dims[axis_at] // parts).reshape((-1,) + (1,) * (len(dims) - axis_at - 1))

    factor_of = one(*cuts[0])
    for cut in cuts[1:]:
        factor_of = factor_of * one(*cut)
    return factor_of


def centred(key, extent, scale, most, cuts=(), held_as=jnp.bfloat16):
    result = scale * jax.random.normal(key, extent, jnp.float32)
    if cuts:
        result = result * shard_levels(key, extent, cuts, -0.22, 0.18)
    return jnp.clip(result, -most, most).astype(held_as)


def setup_inputs(seed: int = 0) -> dict:
    arg_keys = jax.random.split(jax.random.key(seed), 8)
    atom_log_density = draw_atom_log_density(jax.random.fold_in(arg_keys[7], 71), 0)
    prior_log_scaling = draw_prior_log_scaling(jax.random.fold_in(arg_keys[7], 71), 0)
    atom_cotangent_rows = centred(arg_keys[2], (ATOMS, NZ, NY, NX), 1.0, 6.0, ((0, 8), (1, 32)), jnp.float32)
    barycenter_cotangent = centred(arg_keys[3], (NZ, NY, NX), 1.0, 6.0, ((0, 32),), jnp.float32)
    weights = jnp.clip(jax.random.uniform(arg_keys[4], (ATOMS,), jnp.float32, 0.2, 1.0), 0.2, 1.0)
    band = draw_band(jax.random.fold_in(arg_keys[7], 71), 0)
    slot_atom_index = jax.random.permutation(arg_keys[6], ATOMS).astype(jnp.int32)
    return {"atom_log_density": atom_log_density, "prior_log_scaling": prior_log_scaling, "atom_cotangent_rows": atom_cotangent_rows, "barycenter_cotangent": barycenter_cotangent, "weights": weights, "band": band, "slot_atom_index": slot_atom_index}


def kernel_table(count, half):
    positions = jnp.arange(count, dtype=jnp.int32)
    offsets = positions[:, None] - positions[None, :]
    spread = offsets.astype(jnp.float32)
    values = jnp.exp(-2.0 * spread * spread / (BAND_MAX * BAND_MAX))
    return jnp.where(jnp.abs(offsets) <= half, values, jnp.float32(0.0))


def blur_three(field, kernel_columns, kernel_rows, kern_z):
    high = lax.Precision.HIGHEST
    section = jnp.einsum('zyx,xv->zyv', field, kernel_columns, precision=high)
    section = jnp.einsum('zyx,yv->zvx', section, kernel_rows, precision=high)
    return jnp.einsum('zyx,zw->wyx', section, kern_z, precision=high)


def reference(atom_log_density, prior_log_scaling, atom_cotangent_rows, barycenter_cotangent, weights, band, slot_atom_index):
    kernel_columns = kernel_table(NX, band[0])
    kernel_rows = kernel_table(NY, band[1])
    kern_z = kernel_table(NZ, band[2])
    summed = barycenter_cotangent + jnp.sum(atom_cotangent_rows, axis=0)
    slot_mixing_weight = weights[slot_atom_index]

    def single_entry(items):
        log_atom, log_scal, cot_atom, weight_one = items
        peak_gradient = jnp.max(log_scal)
        first_entry = blur_three(jnp.exp(log_scal - peak_gradient), kernel_columns, kernel_rows, kern_z)
        potential = log_atom - (jnp.log(first_entry) + peak_gradient)
        peak_f = jnp.max(potential)
        shifted = jnp.exp(potential - peak_f)
        second = blur_three(shifted, kernel_columns, kernel_rows, kern_z)
        mixed = jnp.log(second) + peak_f
        adjoint = weight_one * summed - cot_atom
        gradient = shifted * blur_three(adjoint / second, kernel_columns, kernel_rows, kern_z)
        total_one = jnp.sum(summed * mixed) / (NX * NY * NZ)
        return gradient, total_one

    log_atom_gradient, slot_sum_totals = lax.map(single_entry, (atom_log_density, prior_log_scaling, atom_cotangent_rows, slot_mixing_weight))
    weight_grad = jnp.zeros((ATOMS,), jnp.float32).at[slot_atom_index].set(slot_sum_totals)
    return log_atom_gradient, weight_grad
```

```python
import functools

import jax
import jax.numpy as jnp
from jax import lax
from jax.experimental import pallas as pl
from jax.experimental.pallas import tpu as pltpu
from jax.sharding import PartitionSpec as P

BAND_MAX = 8
GROUP = 4
F32 = jnp.float32
BF16 = jnp.bfloat16
VMEM_LIMIT = 40 * 1024 * 1024


def split(value):
    high = value.astype(BF16)
    return high, (value - high.astype(F32)).astype(BF16)


def dot(a, b):
    return jnp.dot(a, b, preferred_element_type=F32)


def dot3(ah, al, bh, bl):
    return dot(ah, bh) + (dot(al, bh) + dot(ah, bl))


def peak(value):
    return jnp.max(jnp.max(value, axis=0, keepdims=True), axis=1, keepdims=True)


def rows_of(values):
    return jnp.concatenate([jnp.broadcast_to(v, (1, 128)) for v in values], axis=0)


def tables_kernel(band, th, tl, kxh, kxl, *, ny):
    shift = ny.bit_length() - 1

    def entries(sq, ok):
        return jnp.where(ok, jnp.exp(sq.astype(F32) * (-2.0 / (BAND_MAX * BAND_MAX))), 0.0)

    shape = th.shape
    row = lax.broadcasted_iota(jnp.int32, shape, 0)
    col = lax.broadcasted_iota(jnp.int32, shape, 1)
    dz = (row >> shift) - (col >> shift) + BAND_MAX
    dy = (row & (ny - 1)) - (col & (ny - 1))
    ok = (jnp.abs(dz) <= band[2]) & (jnp.abs(dy) <= band[1])
    th[...], tl[...] = split(entries(dz * dz + dy * dy, ok))
    shape = kxh.shape
    dx = lax.broadcasted_iota(jnp.int32, shape, 0) - lax.broadcasted_iota(jnp.int32, shape, 1)
    kxh[...], kxl[...] = split(entries(dx * dx, jnp.abs(dx) <= band[0]))


def own_product(th, tl, eh, el, y):
    block = th.shape[0]
    count = y.shape[0] // block
    reach = th.shape[1] // block // 2
    for g in range(count):
        first, last = max(0, g - reach), min(count - 1, g + reach)
        rows = slice(first * block, (last + 1) * block)
        cols = slice((first - g + reach) * block, (last - g + reach + 1) * block)
        y[g * block : (g + 1) * block, :] = dot3(th[:, cols], tl[:, cols], eh[rows, :], el[rows, :])


def own_log_kernel(lo, hi, th, tl, y, stats, eh, el):
    half = lo.shape[0]
    m_lo, m_hi = peak(lo[...]), peak(hi[...])
    m = jnp.maximum(m_lo, m_hi)
    eh[:half, :], el[:half, :] = split(jnp.exp(lo[...] - m))
    eh[half:, :], el[half:, :] = split(jnp.exp(hi[...] - m))
    stats[...] = rows_of([m_lo, m_hi, m, m, m, m, m, m])
    own_product(th, tl, eh, el, y)


def own_linear_kernel(lo, hi, stats, th, tl, y, eh, el):
    half = lo.shape[0]
    c = stats[0:1, 0:1]
    f_lo = jnp.exp((c - stats[1:2, 0:1]) * 0.5)
    f_hi = jnp.exp((c - stats[2:3, 0:1]) * 0.5)
    eh[:half, :], el[:half, :] = split(lo[...] * f_lo * f_lo)
    eh[half:, :], el[half:, :] = split(hi[...] * f_hi * f_hi)
    own_product(th, tl, eh, el, y)


def halo_product(g, count, th, tl, eh, el, acc):
    block = th.shape[0]
    reach = th.shape[1] // block // 2
    for step in range(count):

        @pl.when(g == step)
        def _(step=step):
            parts = []
            left = reach - step
            if left > 0:
                rows = slice((reach - left) * block, reach * block)
                parts.append((slice(0, left * block), rows))
            right = step + reach - count + 1
            if right > 0:
                cols = slice((2 * reach + 1 - right) * block, (2 * reach + 1) * block)
                parts.append((cols, slice(reach * block, (reach + right) * block)))
            total = jnp.zeros(acc.shape, F32)
            for cols, rows in parts:
                total = total + dot3(th[:, cols], tl[:, cols], eh[rows, :], el[rows, :])
            acc[...] = total


def columns_product(value, kxh, kxl):
    vh, vl = split(value)
    return dot3(vh, vl, kxh[...], kxl[...])


def log_halos(where, left, right, stats, eh, el, scale):
    half = left.shape[0]
    has_left, has_right = where[0] > 0, where[1] > 0
    m_own = stats[2:3, 0:1]
    m_left = jnp.where(has_left, peak(left[...]), m_own)
    m_right = jnp.where(has_right, peak(right[...]), m_own)
    c = jnp.maximum(m_own, jnp.maximum(m_left, m_right))
    eh[:half, :], el[:half, :] = split(jnp.where(has_left, jnp.exp(left[...] - c), 0.0))
    eh[half:, :], el[half:, :] = split(jnp.where(has_right, jnp.exp(right[...] - c), 0.0))
    own = jnp.exp(m_own - c)
    scale[...] = rows_of([c, stats[0:1, 0:1], stats[1:2, 0:1], m_left, m_right, own, own, own])


def potential_kernel(
    where, left, right, y, stats, density, th, tl, kxh, kxl, lo, hi, eh, el, scale, acc, *, count
):
    g = pl.program_id(0)

    @pl.when(g == 0)
    def _():
        log_halos(where, left, right, stats, eh, el, scale)

    halo_product(g, count, th, tl, eh, el, acc)
    first = columns_product(y[...] * scale[5:6, 0:1] + acc[...], kxh, kxl)
    potential = density[...] - (jnp.log(first) + scale[0:1, 0:1])

    @pl.when(g < count // 2)
    def _():
        lo[...] = potential

    @pl.when(g >= count // 2)
    def _():
        hi[...] = potential


def ratio_kernel(
    where,
    weight,
    left,
    right,
    y,
    stats,
    bary,
    cot,
    sum0,
    sum1,
    sum2,
    sum3,
    th,
    tl,
    kxh,
    kxl,
    lo,
    hi,
    stats_out,
    total,
    eh,
    el,
    scale,
    acc,
    *,
    count,
):
    g = pl.program_id(0)

    @pl.when(g == 0)
    def _():
        log_halos(where, left, right, stats, eh, el, scale)
        stats_out[...] = scale[...]
        total[...] = jnp.zeros(total.shape, F32)

    halo_product(g, count, th, tl, eh, el, acc)
    c = scale[0:1, 0:1]
    second = columns_product(y[...] * scale[5:6, 0:1] + acc[...], kxh, kxl)
    mixed = jnp.log(second) + c
    away = lax.rem(g - where[2] + count, count)
    over_atoms = jnp.where(
        away == 0,
        sum0[...],
        jnp.where(away == 1, sum1[...], jnp.where(away == 2, sum2[...], sum3[...])),
    )
    summed = bary[...] + over_atoms
    share = summed * mixed
    share = jnp.sum(share.reshape(share.shape[0] // 8, 8, share.shape[1]), axis=0)
    for k in range(share.shape[1] // 128):
        total[...] += share[:, k * 128 : (k + 1) * 128]
    ratio = (weight[0] * summed - cot[...]) / second

    @pl.when(g < count // 2)
    def _():
        f = jnp.exp((scale[1:2, 0:1] - c) * 0.5)
        lo[...] = ratio * f * f

    @pl.when(g >= count // 2)
    def _():
        f = jnp.exp((scale[2:3, 0:1] - c) * 0.5)
        hi[...] = ratio * f * f


def gradient_kernel(where, left, right, y, stats, pot_lo, pot_hi, th, tl, kxh, kxl, out, eh, el, acc, *, count):
    g = pl.program_id(0)
    c = stats[0:1, 0:1]

    @pl.when(g == 0)
    def _():
        half = left.shape[0]
        f = jnp.exp((c - stats[3:4, 0:1]) * 0.5)
        eh[:half, :], el[:half, :] = split(jnp.where(where[0] > 0, left[...] * f * f, 0.0))
        f = jnp.exp((c - stats[4:5, 0:1]) * 0.5)
        eh[half:, :], el[half:, :] = split(jnp.where(where[1] > 0, right[...] * f * f, 0.0))

    halo_product(g, count, th, tl, eh, el, acc)
    blurred = columns_product(y[...] + acc[...], kxh, kxl)
    potential = jnp.where(g < count // 2, pot_lo[...], pot_hi[...])
    out[...] = jnp.exp(potential - c) * blurred


def body(
    atom_log_density,
    prior_log_scaling,
    atom_cotangent_rows,
    barycenter_cotangent,
    weights,
    band,
    slot_atom_index,
):
    planes, ny, nx = barycenter_cotangent.shape
    slabs, atoms = lax.axis_size("slab"), lax.axis_size("atom")
    rows = planes * ny
    half = rows // 2
    block = GROUP * ny
    count = planes // GROUP
    reach = BAND_MAX // GROUP
    slab_at, atom_at = lax.axis_index("slab"), lax.axis_index("atom")
    across = atoms // 2
    x_at = atom_at // 2

    smem = pl.BlockSpec(memory_space=pltpu.SMEM)
    params = pltpu.CompilerParams(vmem_limit_bytes=VMEM_LIMIT)

    def shape(*dims, dtype=F32):
        return jax.ShapeDtypeStruct(dims, dtype)

    def full(*dims):
        return pl.BlockSpec(dims, lambda g: (0,) * len(dims))

    def send(value, axis, pairs):
        return lax.ppermute(value, axis, pairs)

    to_right = [(i, i + 1) for i in range(slabs - 1)]
    to_left = [(i + 1, i) for i in range(slabs - 1)]
    ahead = {
        k: [(2 * x + z, 2 * ((x + k) % across) + z) for x in range(across) for z in range(2)]
        for k in range(1, across)
    }
    swap = [(i, i ^ 1) for i in range(atoms)]

    prior = prior_log_scaling.reshape(rows, nx)
    prior_lo, prior_hi = prior[:half], prior[half:]
    from_left = send(prior_hi, "slab", to_right)
    from_right = send(prior_lo, "slab", to_left)

    cot = atom_cotangent_rows.reshape(rows, nx)

    def block_of(k):
        return lax.dynamic_slice_in_dim(cot, lax.rem(x_at + k, count) * block, block)

    part = block_of(0)
    for k in range(1, across):
        part = part + send(block_of(k), "atom", ahead[k])
    both = part + send(part, "atom", swap)
    sums = [both] + [send(both, "atom", ahead[across - k]) for k in range(1, across)]

    where = jnp.stack([(slab_at > 0), (slab_at < slabs - 1), x_at, x_at]).astype(jnp.int32)
    slot = lax.dynamic_slice_in_dim(slot_atom_index, atom_at, 1)
    onehot = (slot[0] == jnp.arange(weights.shape[0], dtype=jnp.int32)).astype(F32)
    weight = jnp.sum(onehot * weights, keepdims=True)

    t_shape, k_shape = (block, (2 * reach + 1) * block), (nx, nx)
    tables = pl.pallas_call(
        functools.partial(tables_kernel, ny=ny),
        out_shape=[
            shape(*t_shape, dtype=BF16),
            shape(*t_shape, dtype=BF16),
            shape(*k_shape, dtype=BF16),
            shape(*k_shape, dtype=BF16),
        ],
        in_specs=[smem],
        compiler_params=params,
        name="tables",
    )(band)
    pair_scratch = [pltpu.VMEM((rows, nx), BF16), pltpu.VMEM((rows, nx), BF16)]
    own_out = [shape(rows, nx), shape(8, 128)]

    own_log = pl.pallas_call(
        own_log_kernel, out_shape=own_out, scratch_shapes=pair_scratch, compiler_params=params, name="own_log"
    )
    table_specs = [full(*t_shape), full(*t_shape), full(*k_shape), full(*k_shape)]
    halo_specs = [full(half, nx), full(half, nx)]
    one = pl.BlockSpec((block, nx), lambda g: (g, 0))
    lo_spec = pl.BlockSpec((block, nx), lambda g: (jnp.minimum(g, count // 2 - 1), 0))
    hi_spec = pl.BlockSpec((block, nx), lambda g: (jnp.maximum(g - count // 2, 0), 0))
    stat_spec = full(8, 128)
    scale_scratch = [pltpu.VMEM((8, 128), F32)]
    acc_scratch = [pltpu.VMEM((block, nx), F32)]

    y, stats = own_log(prior_lo, prior_hi, *tables[:2])
    pot_lo, pot_hi = pl.pallas_call(
        functools.partial(potential_kernel, count=count),
        grid=(count,),
        in_specs=[smem, *halo_specs, one, stat_spec, one, *table_specs],
        out_specs=[lo_spec, hi_spec],
        out_shape=[shape(half, nx), shape(half, nx)],
        scratch_shapes=pair_scratch + scale_scratch + acc_scratch,
        compiler_params=params,
        name="potential",
    )(where, from_left, from_right, y, stats, atom_log_density.reshape(rows, nx), *tables)

    from_left = send(pot_hi, "slab", to_right)
    from_right = send(pot_lo, "slab", to_left)
    y, stats = own_log(pot_lo, pot_hi, *tables[:2])
    ratio_lo, ratio_hi, stats, total = pl.pallas_call(
        functools.partial(ratio_kernel, count=count),
        grid=(count,),
        in_specs=[smem, smem, *halo_specs, one, stat_spec, one, one]
        + [full(block, nx)] * 4
        + table_specs,
        out_specs=[lo_spec, hi_spec, stat_spec, stat_spec],
        out_shape=[shape(half, nx), shape(half, nx), shape(8, 128), shape(8, 128)],
        scratch_shapes=pair_scratch + scale_scratch + acc_scratch,
        compiler_params=params,
        name="ratio",
    )(
        where,
        weight,
        from_left,
        from_right,
        y,
        stats,
        barycenter_cotangent.reshape(rows, nx),
        cot,
        *sums,
        *tables,
    )

    from_left = send(ratio_hi, "slab", to_right)
    from_right = send(ratio_lo, "slab", to_left)

    value = jnp.broadcast_to(jnp.sum(total), (8, 128))
    hop = 1
    while hop < slabs:
        value = value + send(value, "slab", [(i, i ^ hop) for i in range(slabs)])
        hop *= 2
    lanes = jnp.arange(128, dtype=jnp.int32)[None, :]
    value = jnp.where(lanes == slot[0], value, 0.0)
    hop = 1
    while hop < atoms:
        value = value + send(value, "atom", [(i, i ^ hop) for i in range(atoms)])
        hop *= 2
    weight_grad = value[0, : weights.shape[0]] / (rows * nx * slabs)

    (y,) = pl.pallas_call(
        own_linear_kernel,
        out_shape=[shape(rows, nx)],
        scratch_shapes=pair_scratch,
        compiler_params=params,
        name="own_linear",
    )(ratio_lo, ratio_hi, stats, *tables[:2])
    gradient = pl.pallas_call(
        functools.partial(gradient_kernel, count=count),
        grid=(count,),
        in_specs=[smem, *halo_specs, one, stat_spec, lo_spec, hi_spec, *table_specs],
        out_specs=one,
        out_shape=shape(rows, nx),
        scratch_shapes=pair_scratch + acc_scratch,
        compiler_params=params,
        name="gradient",
    )(where, from_left, from_right, y, stats, pot_lo, pot_hi, *tables)
    return gradient.reshape(atom_log_density.shape), weight_grad


def solution(mesh):
    return jax.shard_map(
        body,
        mesh=mesh,
        in_specs=(
            P("atom", "slab", None, None),
            P("atom", "slab", None, None),
            P("atom", "slab", None, None),
            P("slab", None, None),
            P(),
            P(),
            P(),
        ),
        out_specs=(P("atom", "slab", None, None), P()),
        check_vma=False,
    )
```

```python
import functools

import jax
import jax.numpy as jnp
from jax import lax
from jax.experimental import pallas as pl
from jax.experimental.pallas import tpu as pltpu
from jax.sharding import PartitionSpec as P

BAND_MAX = 8
GROUP = 4
F32 = jnp.float32
BF16 = jnp.bfloat16
VMEM_LIMIT = 40 * 1024 * 1024


def split(value):
    high = value.astype(BF16)
    return high, (value - high.astype(F32)).astype(BF16)


def dot(a, b):
    return jnp.dot(a, b, preferred_element_type=F32)


def dot3(ah, al, bh, bl):
    return dot(ah, bh) + (dot(al, bh) + dot(ah, bl))


def peak(value):
    return jnp.max(jnp.max(value, axis=0, keepdims=True), axis=1, keepdims=True)


def rows_of(values):
    return jnp.concatenate([jnp.broadcast_to(v, (1, 128)) for v in values], axis=0)


def tables_kernel(band, th, tl, kxh, kxl, *, ny):
    shift = ny.bit_length() - 1

    def entries(sq, ok):
        return jnp.where(ok, jnp.exp(sq.astype(F32) * (-2.0 / (BAND_MAX * BAND_MAX))), 0.0)

    shape = th.shape
    row = lax.broadcasted_iota(jnp.int32, shape, 0)
    col = lax.broadcasted_iota(jnp.int32, shape, 1)
    dz = (row >> shift) - (col >> shift) + BAND_MAX
    dy = (row & (ny - 1)) - (col & (ny - 1))
    ok = (jnp.abs(dz) <= band[2]) & (jnp.abs(dy) <= band[1])
    th[...], tl[...] = split(entries(dz * dz + dy * dy, ok))
    shape = kxh.shape
    dx = lax.broadcasted_iota(jnp.int32, shape, 0) - lax.broadcasted_iota(jnp.int32, shape, 1)
    kxh[...], kxl[...] = split(entries(dx * dx, jnp.abs(dx) <= band[0]))


def own_product(th, tl, eh, el, y):
    block = th.shape[0]
    count = y.shape[0] // block
    reach = th.shape[1] // block // 2
    for g in range(count):
        first, last = max(0, g - reach), min(count - 1, g + reach)
        rows = slice(first * block, (last + 1) * block)
        cols = slice((first - g + reach) * block, (last - g + reach + 1) * block)
        y[g * block : (g + 1) * block, :] = dot3(th[:, cols], tl[:, cols], eh[rows, :], el[rows, :])


def own_log_kernel(lo, hi, th, tl, y, stats, eh, el):
    half = lo.shape[0]
    m_lo, m_hi = peak(lo[...]), peak(hi[...])
    m = jnp.maximum(m_lo, m_hi)
    eh[:half, :], el[:half, :] = split(jnp.exp(lo[...] - m))
    eh[half:, :], el[half:, :] = split(jnp.exp(hi[...] - m))
    stats[...] = rows_of([m_lo, m_hi, m, m, m, m, m, m])
    own_product(th, tl, eh, el, y)


def own_linear_kernel(lo, hi, stats, th, tl, y, eh, el):
    half = lo.shape[0]
    c = stats[0:1, 0:1]
    f_lo = jnp.exp((c - stats[1:2, 0:1]) * 0.5)
    f_hi = jnp.exp((c - stats[2:3, 0:1]) * 0.5)
    eh[:half, :], el[:half, :] = split(lo[...] * f_lo * f_lo)
    eh[half:, :], el[half:, :] = split(hi[...] * f_hi * f_hi)
    own_product(th, tl, eh, el, y)


def halo_product(g, count, th, tl, eh, el, acc):
    block = th.shape[0]
    reach = th.shape[1] // block // 2
    for step in range(count):

        @pl.when(g == step)
        def _(step=step):
            parts = []
            left = reach - step
            if left > 0:
                rows = slice((reach - left) * block, reach * block)
                parts.append((slice(0, left * block), rows))
            right = step + reach - count + 1
            if right > 0:
                cols = slice((2 * reach + 1 - right) * block, (2 * reach + 1) * block)
                parts.append((cols, slice(reach * block, (reach + right) * block)))
            total = jnp.zeros(acc.shape, F32)
            for cols, rows in parts:
                total = total + dot3(th[:, cols], tl[:, cols], eh[rows, :], el[rows, :])
            acc[...] = total


def columns_product(value, kxh, kxl):
    vh, vl = split(value)
    return dot3(vh, vl, kxh[...], kxl[...])


def log_halos(where, left, right, stats, eh, el, scale):
    half = left.shape[0]
    has_left, has_right = where[0] > 0, where[1] > 0
    m_own = stats[2:3, 0:1]
    m_left = jnp.where(has_left, peak(left[...]), m_own)
    m_right = jnp.where(has_right, peak(right[...]), m_own)
    c = jnp.maximum(m_own, jnp.maximum(m_left, m_right))
    eh[:half, :], el[:half, :] = split(jnp.where(has_left, jnp.exp(left[...] - c), 0.0))
    eh[half:, :], el[half:, :] = split(jnp.where(has_right, jnp.exp(right[...] - c), 0.0))
    own = jnp.exp(m_own - c)
    scale[...] = rows_of([c, stats[0:1, 0:1], stats[1:2, 0:1], m_left, m_right, own, own, own])


def potential_kernel(
    where, left, right, y, stats, density, th, tl, kxh, kxl, lo, hi, eh, el, scale, acc, *, count
):
    g = pl.program_id(0)

    @pl.when(g == 0)
    def _():
        log_halos(where, left, right, stats, eh, el, scale)

    halo_product(g, count, th, tl, eh, el, acc)
    first = columns_product(y[...] * scale[5:6, 0:1] + acc[...], kxh, kxl)
    potential = density[...] - (jnp.log(first) + scale[0:1, 0:1])

    @pl.when(g < count // 2)
    def _():
        lo[...] = potential

    @pl.when(g >= count // 2)
    def _():
        hi[...] = potential


def ratio_kernel(
    where,
    weight,
    left,
    right,
    y,
    stats,
    bary,
    cot,
    sum0,
    sum1,
    sum2,
    sum3,
    th,
    tl,
    kxh,
    kxl,
    lo,
    hi,
    stats_out,
    total,
    eh,
    el,
    scale,
    acc,
    *,
    count,
):
    g = pl.program_id(0)

    @pl.when(g == 0)
    def _():
        log_halos(where, left, right, stats, eh, el, scale)
        stats_out[...] = scale[...]
        total[...] = jnp.zeros(total.shape, F32)

    halo_product(g, count, th, tl, eh, el, acc)
    c = scale[0:1, 0:1]
    second = columns_product(y[...] * scale[5:6, 0:1] + acc[...], kxh, kxl)
    mixed = jnp.log(second) + c
    away = lax.rem(g - where[2] + count, count)
    over_atoms = jnp.where(
        away == 0,
        sum0[...],
        jnp.where(away == 1, sum1[...], jnp.where(away == 2, sum2[...], sum3[...])),
    )
    summed = bary[...] + over_atoms
    share = summed * mixed
    share = jnp.sum(share.reshape(share.shape[0] // 8, 8, share.shape[1]), axis=0)
    for k in range(share.shape[1] // 128):
        total[...] += share[:, k * 128 : (k + 1) * 128]
    ratio = (weight[0] * summed - cot[...]) / second

    @pl.when(g < count // 2)
    def _():
        f = jnp.exp((scale[1:2, 0:1] - c) * 0.5)
        lo[...] = ratio * f * f

    @pl.when(g >= count // 2)
    def _():
        f = jnp.exp((scale[2:3, 0:1] - c) * 0.5)
        hi[...] = ratio * f * f


def gradient_kernel(where, left, right, y, stats, pot_lo, pot_hi, th, tl, kxh, kxl, out, eh, el, acc, *, count):
    g = pl.program_id(0)
    c = stats[0:1, 0:1]

    @pl.when(g == 0)
    def _():
        half = left.shape[0]
        f = jnp.exp((c - stats[3:4, 0:1]) * 0.5)
        eh[:half, :], el[:half, :] = split(jnp.where(where[0] > 0, left[...] * f * f, 0.0))
        f = jnp.exp((c - stats[4:5, 0:1]) * 0.5)
        eh[half:, :], el[half:, :] = split(jnp.where(where[1] > 0, right[...] * f * f, 0.0))

    halo_product(g, count, th, tl, eh, el, acc)
    blurred = columns_product(y[...] + acc[...], kxh, kxl)
    potential = jnp.where(g < count // 2, pot_lo[...], pot_hi[...])
    out[...] = jnp.exp(potential - c) * blurred


def body(
    atom_log_density,
    prior_log_scaling,
    atom_cotangent_rows,
    barycenter_cotangent,
    weights,
    band,
    slot_atom_index,
):
    planes, ny, nx = barycenter_cotangent.shape
    slabs, atoms = lax.axis_size("slab"), lax.axis_size("atom")
    rows = planes * ny
    half = rows // 2
    block = GROUP * ny
    count = planes // GROUP
    reach = BAND_MAX // GROUP
    slab_at, atom_at = lax.axis_index("slab"), lax.axis_index("atom")
    across = atoms // 2
    x_at = atom_at // 2

    smem = pl.BlockSpec(memory_space=pltpu.SMEM)
    params = pltpu.CompilerParams(vmem_limit_bytes=VMEM_LIMIT)

    def shape(*dims, dtype=F32):
        return jax.ShapeDtypeStruct(dims, dtype)

    def full(*dims):
        return pl.BlockSpec(dims, lambda g: (0,) * len(dims))

    def send(value, axis, pairs):
        return lax.ppermute(value, axis, pairs)

    in_order = lax.optimization_barrier
    to_right = [(i, i + 1) for i in range(slabs - 1)]
    to_left = [(i + 1, i) for i in range(slabs - 1)]
    ahead = {
        k: [(2 * x + z, 2 * ((x + k) % across) + z) for x in range(across) for z in range(2)]
        for k in range(1, across)
    }
    swap = [(i, i ^ 1) for i in range(atoms)]

    cot = atom_cotangent_rows.reshape(rows, nx)

    def block_of(k):
        return lax.dynamic_slice_in_dim(cot, lax.rem(x_at + k, count) * block, block)

    blocks = [block_of(k) for k in range(1, across)]
    blocks, prior_log_scaling = in_order((blocks, prior_log_scaling))
    part = block_of(0)
    for k in range(1, across):
        part = part + send(blocks[k - 1], "atom", ahead[k])

    prior = prior_log_scaling.reshape(rows, nx)
    prior_lo, prior_hi = prior[:half], prior[half:]
    from_left = send(prior_hi, "slab", to_right)
    from_right = send(prior_lo, "slab", to_left)
    from_left, from_right, part = in_order((from_left, from_right, part))
    swapped = send(part, "atom", swap)

    where = jnp.stack([(slab_at > 0), (slab_at < slabs - 1), x_at, x_at]).astype(jnp.int32)
    slot = lax.dynamic_slice_in_dim(slot_atom_index, atom_at, 1)
    onehot = (slot[0] == jnp.arange(weights.shape[0], dtype=jnp.int32)).astype(F32)
    weight = jnp.sum(onehot * weights, keepdims=True)

    t_shape, k_shape = (block, (2 * reach + 1) * block), (nx, nx)
    tables = pl.pallas_call(
        functools.partial(tables_kernel, ny=ny),
        out_shape=[
            shape(*t_shape, dtype=BF16),
            shape(*t_shape, dtype=BF16),
            shape(*k_shape, dtype=BF16),
            shape(*k_shape, dtype=BF16),
        ],
        in_specs=[smem],
        compiler_params=params,
        name="tables",
    )(band)
    pair_scratch = [pltpu.VMEM((rows, nx), BF16), pltpu.VMEM((rows, nx), BF16)]
    own_out = [shape(rows, nx), shape(8, 128)]

    own_log = pl.pallas_call(
        own_log_kernel, out_shape=own_out, scratch_shapes=pair_scratch, compiler_params=params, name="own_log"
    )
    table_specs = [full(*t_shape), full(*t_shape), full(*k_shape), full(*k_shape)]
    halo_specs = [full(half, nx), full(half, nx)]
    one = pl.BlockSpec((block, nx), lambda g: (g, 0))
    lo_spec = pl.BlockSpec((block, nx), lambda g: (jnp.minimum(g, count // 2 - 1), 0))
    hi_spec = pl.BlockSpec((block, nx), lambda g: (jnp.maximum(g - count // 2, 0), 0))
    stat_spec = full(8, 128)
    scale_scratch = [pltpu.VMEM((8, 128), F32)]
    acc_scratch = [pltpu.VMEM((block, nx), F32)]

    y, stats = own_log(prior_lo, prior_hi, *tables[:2])
    pot_lo, pot_hi = pl.pallas_call(
        functools.partial(potential_kernel, count=count),
        grid=(count,),
        in_specs=[smem, *halo_specs, one, stat_spec, one, *table_specs],
        out_specs=[lo_spec, hi_spec],
        out_shape=[shape(half, nx), shape(half, nx)],
        scratch_shapes=pair_scratch + scale_scratch + acc_scratch,
        compiler_params=params,
        name="potential",
    )(where, from_left, from_right, y, stats, atom_log_density.reshape(rows, nx), *tables)

    pot_lo, pot_hi, swapped = in_order((pot_lo, pot_hi, swapped))
    both = part + swapped
    sums = [both] + [send(both, "atom", ahead[across - k]) for k in range(1, across)]
    from_left = send(pot_hi, "slab", to_right)
    from_right = send(pot_lo, "slab", to_left)
    y, stats = own_log(pot_lo, pot_hi, *tables[:2])
    ratio_lo, ratio_hi, stats, total = pl.pallas_call(
        functools.partial(ratio_kernel, count=count),
        grid=(count,),
        in_specs=[smem, smem, *halo_specs, one, stat_spec, one, one]
        + [full(block, nx)] * 4
        + table_specs,
        out_specs=[lo_spec, hi_spec, stat_spec, stat_spec],
        out_shape=[shape(half, nx), shape(half, nx), shape(8, 128), shape(8, 128)],
        scratch_shapes=pair_scratch + scale_scratch + acc_scratch,
        compiler_params=params,
        name="ratio",
    )(
        where,
        weight,
        from_left,
        from_right,
        y,
        stats,
        barycenter_cotangent.reshape(rows, nx),
        cot,
        *sums,
        *tables,
    )

    from_left = send(ratio_hi, "slab", to_right)
    from_right = send(ratio_lo, "slab", to_left)

    (y,) = pl.pallas_call(
        own_linear_kernel,
        out_shape=[shape(rows, nx)],
        scratch_shapes=pair_scratch,
        compiler_params=params,
        name="own_linear",
    )(ratio_lo, ratio_hi, stats, *tables[:2])
    def add(value, axis, pairs):
        return value + send(value, axis, pairs)

    value = jnp.broadcast_to(jnp.sum(total), (8, 128))
    lanes = jnp.arange(128, dtype=jnp.int32)[None, :]
    value = jnp.where(lanes == slot[0], value, 0.0)
    value = add(value, "slab", [(i, i ^ 1) for i in range(slabs)])
    for k in (1, 2):
        value = add(value, "atom", ahead[k])
    value, y = in_order((value, y))
    for hop in (8, 16, 2, 4):
        value = add(value, "slab", [(i, i ^ hop) for i in range(slabs)])
    gradient = pl.pallas_call(
        functools.partial(gradient_kernel, count=count),
        grid=(count,),
        in_specs=[smem, *halo_specs, one, stat_spec, lo_spec, hi_spec, *table_specs],
        out_specs=one,
        out_shape=shape(rows, nx),
        scratch_shapes=pair_scratch + acc_scratch,
        compiler_params=params,
        name="gradient",
    )(where, from_left, from_right, y, stats, pot_lo, pot_hi, *tables)
    value, gradient = in_order((value, gradient))
    value = add(value, "atom", swap)
    weight_grad = value[0, : weights.shape[0]] / (rows * nx * slabs)
    return gradient.reshape(atom_log_density.shape), weight_grad


def solution(mesh):
    return jax.shard_map(
        body,
        mesh=mesh,
        in_specs=(
            P("atom", "slab", None, None),
            P("atom", "slab", None, None),
            P("atom", "slab", None, None),
            P("slab", None, None),
            P(),
            P(),
            P(),
        ),
        out_specs=(P("atom", "slab", None, None), P()),
        check_vma=False,
    )
```

```python
import functools

import jax
import jax.numpy as jnp
from jax import lax
from jax.experimental import pallas as pl
from jax.experimental.pallas import tpu as pltpu
from jax.sharding import PartitionSpec as P

BAND_MAX = 8
GROUP = 4
F32 = jnp.float32
BF16 = jnp.bfloat16
VMEM_LIMIT = 40 * 1024 * 1024


def split(value):
    high = value.astype(BF16)
    return high, (value - high.astype(F32)).astype(BF16)


def dot(a, b):
    return jnp.dot(a, b, preferred_element_type=F32)


def dot3(ah, al, bh, bl):
    return dot(ah, bh) + (dot(al, bh) + dot(ah, bl))


def peak(value):
    return jnp.max(jnp.max(value, axis=0, keepdims=True), axis=1, keepdims=True)


def rows_of(values):
    return jnp.concatenate([jnp.broadcast_to(v, (1, 128)) for v in values], axis=0)


def tables_kernel(band, kyh, kyl, kxh, kxl, *, ny):
    def entries(sq, ok):
        return jnp.where(ok, jnp.exp(sq.astype(F32) * (-2.0 / (BAND_MAX * BAND_MAX))), 0.0)

    def offsets(shape):
        return lax.broadcasted_iota(jnp.int32, shape, 0), lax.broadcasted_iota(jnp.int32, shape, 1)

    row, col = offsets(kyh.shape)
    shift = ny.bit_length() - 1
    dy = row - col
    kyh[...], kyl[...] = split(entries(dy * dy, ((row >> shift) == (col >> shift)) & (jnp.abs(dy) <= band[1])))
    row, col = offsets(kxh.shape)
    dx = row - col
    kxh[...], kxl[...] = split(entries(dx * dx, jnp.abs(dx) <= band[0]))


def tile_loop(ny, nx, step):
    across = nx // 128

    def body_of(i, carry):
        row = pl.multiple_of(lax.div(i, across) * 8, 8)
        column = pl.multiple_of(lax.rem(i, across) * 128, 128)
        step(row, pl.ds(column, 128))
        return carry

    lax.fori_loop(0, ny // 8 * across, body_of, 0)


def own_planes(lo, hi, kz, y, ny, entry_lo, entry_hi):
    side = lo.shape[0] // ny
    planes = 2 * side
    taps = [kz[d] for d in range(BAND_MAX + 1)]

    def step(row, columns):
        e = [entry_lo(lo[pl.ds(q * ny + row, 8), columns]) for q in range(side)]
        e += [entry_hi(hi[pl.ds(q * ny + row, 8), columns]) for q in range(side)]
        for p in range(planes):
            total = taps[0] * e[p]
            for d in range(1, BAND_MAX + 1):
                near = [e[q] for q in (p - d, p + d) if 0 <= q < planes]
                total += taps[d] * (near[0] if len(near) == 1 else near[0] + near[1])
            y[pl.ds(p * ny + row, 8), columns] = total

    tile_loop(ny, lo.shape[1], step)


def halo_planes(left, right, kz, y, z, ny, own, entry_left, entry_right):
    side = left.shape[0] // ny
    taps = [kz[d] for d in range(BAND_MAX + 1)]

    def step(row, columns):
        e = [entry_left(left[pl.ds(q * ny + row, 8), columns]) for q in range(side)]
        for p in range(side):
            rows = pl.ds(p * ny + row, 8)
            total = own(y[rows, columns])
            for q in range(max(0, p + side - BAND_MAX), side):
                total += taps[p + side - q] * e[q]
            z[rows, columns] = total
        e = [entry_right(right[pl.ds(q * ny + row, 8), columns]) for q in range(side)]
        for p in range(side):
            rows = pl.ds((side + p) * ny + row, 8)
            total = own(y[rows, columns])
            for q in range(min(side, p + BAND_MAX - side + 1)):
                total += taps[side + q - p] * e[q]
            z[rows, columns] = total

    tile_loop(ny, left.shape[1], step)


def tile(value):
    return jnp.broadcast_to(value, (8, 128))


def own_log_kernel(kz, lo, hi, y, stats, *, ny):
    m_lo, m_hi = peak(lo[...]), peak(hi[...])
    m = jnp.maximum(m_lo, m_hi)
    stats[...] = rows_of([m_lo, m_hi, m, m, m, m, m, m])
    m = tile(m)
    entry = lambda v: jnp.exp(v - m)
    own_planes(lo, hi, kz, y, ny, entry, entry)


def own_linear_kernel(kz, lo, hi, stats, y, *, ny):
    c = stats[0:1, 0:1]
    f_lo = tile(jnp.exp((c - stats[1:2, 0:1]) * 0.5))
    f_hi = tile(jnp.exp((c - stats[2:3, 0:1]) * 0.5))
    own_planes(lo, hi, kz, y, ny, lambda v: v * f_lo * f_lo, lambda v: v * f_hi * f_hi)


def rows_and_columns(z, g, kyh, kyl, kxh, kxl, mid):
    half, block = mid.shape[0], kyh.shape[0]
    for k in range(half // block):
        rows = pl.ds(pl.multiple_of(g * half + k * block, block), block)
        zh, zl = split(z[rows, :])
        mid[k * block : (k + 1) * block, :] = dot3(kyh[...], kyl[...], zh, zl)
    mh, ml = split(mid[...])
    return dot3(mh, ml, kxh[...], kxl[...])


def log_halos(where, kz, left, right, y, stats, z, scale, ny):
    has_left, has_right = where[0] > 0, where[1] > 0
    m_own = stats[2:3, 0:1]
    m_left = jnp.where(has_left, peak(left[...]), m_own)
    m_right = jnp.where(has_right, peak(right[...]), m_own)
    c = jnp.maximum(m_own, jnp.maximum(m_left, m_right))
    scale[...] = rows_of([c, stats[0:1, 0:1], stats[1:2, 0:1], m_left, m_right, c, c, c])
    own = tile(jnp.exp(m_own - c))
    c = tile(c)
    halo_planes(
        left,
        right,
        kz,
        y,
        z,
        ny,
        lambda v: v * own,
        lambda v: jnp.where(has_left, jnp.exp(v - c), 0.0),
        lambda v: jnp.where(has_right, jnp.exp(v - c), 0.0),
    )


def potential_kernel(
    where, kz, left, right, y, stats, density, kyh, kyl, kxh, kxl, lo, hi, z, mid, scale, *, ny
):
    g = pl.program_id(0)

    @pl.when(g == 0)
    def _():
        log_halos(where, kz, left, right, y, stats, z, scale, ny)

    first = rows_and_columns(z, g, kyh, kyl, kxh, kxl, mid)
    potential = density[...] - (jnp.log(first) + scale[0:1, 0:1])

    @pl.when(g == 0)
    def _():
        lo[...] = potential

    @pl.when(g == 1)
    def _():
        hi[...] = potential


def ratio_kernel(
    where,
    weight,
    kz,
    left,
    right,
    y,
    stats,
    bary,
    cot,
    sum0,
    sum1,
    sum2,
    sum3,
    kyh,
    kyl,
    kxh,
    kxl,
    lo,
    hi,
    stats_out,
    total,
    z,
    mid,
    scale,
    *,
    ny,
):
    g = pl.program_id(0)

    @pl.when(g == 0)
    def _():
        log_halos(where, kz, left, right, y, stats, z, scale, ny)
        stats_out[...] = scale[...]
        total[...] = jnp.zeros(total.shape, F32)

    c = scale[0:1, 0:1]
    second = rows_and_columns(z, g, kyh, kyl, kxh, kxl, mid)
    block = sum0.shape[0]
    per_step = mid.shape[0] // block
    count = 2 * per_step
    f = jnp.exp((jnp.where(g == 0, scale[1:2, 0:1], scale[2:3, 0:1]) - c) * 0.5)
    for k in range(per_step):
        rows = slice(k * block, (k + 1) * block)
        away = lax.rem(g * per_step + k - where[2] + count, count)
        over_atoms = jnp.where(
            away == 0,
            sum0[...],
            jnp.where(away == 1, sum1[...], jnp.where(away == 2, sum2[...], sum3[...])),
        )
        summed = bary[rows, :] + over_atoms
        share = summed * (jnp.log(second[rows, :]) + c)
        share = jnp.sum(share.reshape(block // 8, 8, share.shape[1]), axis=0)
        for m in range(share.shape[1] // 128):
            total[...] += share[:, m * 128 : (m + 1) * 128]
        ratio = (weight[0] * summed - cot[rows, :]) / second[rows, :] * f * f

        @pl.when(g == 0)
        def _():
            lo[rows, :] = ratio

        @pl.when(g == 1)
        def _():
            hi[rows, :] = ratio


def gradient_kernel(
    where, kz, left, right, y, stats, pot_lo, pot_hi, kyh, kyl, kxh, kxl, out, z, mid, *, ny
):
    g = pl.program_id(0)
    c = stats[0:1, 0:1]

    @pl.when(g == 0)
    def _():
        f_left = tile(jnp.exp((c - stats[3:4, 0:1]) * 0.5))
        f_right = tile(jnp.exp((c - stats[4:5, 0:1]) * 0.5))
        has_left, has_right = where[0] > 0, where[1] > 0
        halo_planes(
            left,
            right,
            kz,
            y,
            z,
            ny,
            lambda v: v,
            lambda v: jnp.where(has_left, v * f_left * f_left, 0.0),
            lambda v: jnp.where(has_right, v * f_right * f_right, 0.0),
        )

    blurred = rows_and_columns(z, g, kyh, kyl, kxh, kxl, mid)
    potential = jnp.where(g == 0, pot_lo[...], pot_hi[...])
    out[...] = jnp.exp(potential - c) * blurred


def body(
    atom_log_density,
    prior_log_scaling,
    atom_cotangent_rows,
    barycenter_cotangent,
    weights,
    band,
    slot_atom_index,
):
    planes, ny, nx = barycenter_cotangent.shape
    slabs, atoms = lax.axis_size("slab"), lax.axis_size("atom")
    rows = planes * ny
    half = rows // 2
    block = GROUP * ny
    count = planes // GROUP
    slab_at, atom_at = lax.axis_index("slab"), lax.axis_index("atom")
    across = atoms // 2
    x_at = atom_at // 2

    smem = pl.BlockSpec(memory_space=pltpu.SMEM)
    params = pltpu.CompilerParams(vmem_limit_bytes=VMEM_LIMIT)

    def shape(*dims, dtype=F32):
        return jax.ShapeDtypeStruct(dims, dtype)

    def full(*dims):
        return pl.BlockSpec(dims, lambda g: (0,) * len(dims))

    def send(value, axis, pairs):
        return lax.ppermute(value, axis, pairs)

    in_order = lax.optimization_barrier
    to_right = [(i, i + 1) for i in range(slabs - 1)]
    to_left = [(i + 1, i) for i in range(slabs - 1)]
    ahead = {
        k: [(2 * x + z, 2 * ((x + k) % across) + z) for x in range(across) for z in range(2)]
        for k in range(1, across)
    }
    swap = [(i, i ^ 1) for i in range(atoms)]

    cot = atom_cotangent_rows.reshape(rows, nx)

    def block_of(k):
        return lax.dynamic_slice_in_dim(cot, lax.rem(x_at + k, count) * block, block)

    blocks = [block_of(k) for k in range(1, across)]
    part = block_of(0)
    for k in range(1, across):
        part = part + send(blocks[k - 1], "atom", ahead[k])
    swapped = send(part, "atom", swap)

    y_shape, x_shape = (block, block), (nx, nx)
    distance = jnp.arange(BAND_MAX + 1, dtype=jnp.int32)
    kz = jnp.exp((distance * distance).astype(F32) * (-2.0 / (BAND_MAX * BAND_MAX)))
    kz = jnp.where(distance <= band[2], kz, 0.0)
    tables = pl.pallas_call(
        functools.partial(tables_kernel, ny=ny),
        out_shape=[shape(*dims, dtype=BF16) for dims in (y_shape, y_shape, x_shape, x_shape)],
        in_specs=[smem],
        compiler_params=params,
        name="tables",
    )(band)
    prior = prior_log_scaling.reshape(rows, nx)
    prior_lo, prior_hi = prior[:half], prior[half:]
    from_left = send(prior_hi, "slab", to_right)
    from_right = send(prior_lo, "slab", to_left)

    where = jnp.stack([(slab_at > 0), (slab_at < slabs - 1), x_at, x_at]).astype(jnp.int32)
    slot = lax.dynamic_slice_in_dim(slot_atom_index, atom_at, 1)
    onehot = (slot[0] == jnp.arange(weights.shape[0], dtype=jnp.int32)).astype(F32)
    weight = jnp.sum(onehot * weights, keepdims=True)

    vmem = pl.BlockSpec(memory_space=pltpu.VMEM)
    own_out = [shape(rows, nx), shape(8, 128)]
    own_log = pl.pallas_call(
        functools.partial(own_log_kernel, ny=ny),
        in_specs=[smem, vmem, vmem],
        out_shape=own_out,
        compiler_params=params,
        name="own_log",
    )
    halo_specs = [full(half, nx), full(half, nx), full(rows, nx), full(8, 128)]
    table_specs = [full(*y_shape), full(*y_shape), full(*x_shape), full(*x_shape)]
    one = pl.BlockSpec((half, nx), lambda g: (g, 0))
    whole_half = full(half, nx)
    scratch = [pltpu.VMEM((rows, nx), F32), pltpu.VMEM((half, nx), F32)]
    scale = pltpu.VMEM((8, 128), F32)

    y, stats = own_log(kz, prior_lo, prior_hi)
    pot_lo, pot_hi = pl.pallas_call(
        functools.partial(potential_kernel, ny=ny),
        grid=(2,),
        in_specs=[smem, smem, *halo_specs, one, *table_specs],
        out_specs=[whole_half, whole_half],
        out_shape=[shape(half, nx), shape(half, nx)],
        scratch_shapes=[*scratch, scale],
        compiler_params=params,
        name="potential",
    )(where, kz, from_left, from_right, y, stats, atom_log_density.reshape(rows, nx), *tables)

    from_left = send(pot_hi, "slab", to_right)
    from_right = send(pot_lo, "slab", to_left)
    both = part + swapped
    sums = [both] + [send(both, "atom", ahead[across - k]) for k in range(1, across)]
    y, stats = own_log(kz, pot_lo, pot_hi)
    ratio_lo, ratio_hi, stats, total = pl.pallas_call(
        functools.partial(ratio_kernel, ny=ny),
        grid=(2,),
        in_specs=[smem, smem, smem, *halo_specs, one, one] + [full(block, nx)] * 4 + table_specs,
        out_specs=[whole_half, whole_half, full(8, 128), full(8, 128)],
        out_shape=[shape(half, nx), shape(half, nx), shape(8, 128), shape(8, 128)],
        scratch_shapes=[*scratch, scale],
        compiler_params=params,
        name="ratio",
    )(
        where,
        weight,
        kz,
        from_left,
        from_right,
        y,
        stats,
        barycenter_cotangent.reshape(rows, nx),
        cot,
        *sums,
        *tables,
    )

    from_left = send(ratio_hi, "slab", to_right)
    from_right = send(ratio_lo, "slab", to_left)
    (y,) = pl.pallas_call(
        functools.partial(own_linear_kernel, ny=ny),
        in_specs=[smem, vmem, vmem, vmem],
        out_shape=[shape(rows, nx)],
        compiler_params=params,
        name="own_linear",
    )(kz, ratio_lo, ratio_hi, stats)

    total, y = in_order((total, y))
    value = jnp.broadcast_to(jnp.sum(total), (atoms * slabs, 128))
    value = lax.all_to_all(value, ("atom", "slab"), 0, 0, tiled=True)
    by_slot = jnp.sum(value[:, 0].reshape(atoms, slabs), axis=1)
    spread = slot_atom_index[:, None] == jnp.arange(atoms, dtype=jnp.int32)[None, :]
    weight_grad = jnp.sum(jnp.where(spread, by_slot[:, None], 0.0), axis=0) / (rows * nx * slabs)

    gradient = pl.pallas_call(
        functools.partial(gradient_kernel, ny=ny),
        grid=(2,),
        in_specs=[smem, smem, *halo_specs, whole_half, whole_half, *table_specs],
        out_specs=one,
        out_shape=shape(rows, nx),
        scratch_shapes=scratch,
        compiler_params=params,
        name="gradient",
    )(where, kz, from_left, from_right, y, stats, pot_lo, pot_hi, *tables)
    return gradient.reshape(atom_log_density.shape), weight_grad


def solution(mesh):
    return jax.shard_map(
        body,
        mesh=mesh,
        in_specs=(
            P("atom", "slab", None, None),
            P("atom", "slab", None, None),
            P("atom", "slab", None, None),
            P("slab", None, None),
            P(),
            P(),
            P(),
        ),
        out_specs=(P("atom", "slab", None, None), P()),
        check_vma=False,
    )
```

```python
import functools

import jax
import jax.numpy as jnp
from jax import lax
from jax.experimental import pallas as pl
from jax.experimental.pallas import tpu as pltpu
from jax.sharding import PartitionSpec as P

BAND_MAX = 8
GROUP = 4
F32 = jnp.float32
BF16 = jnp.bfloat16
VMEM_LIMIT = 12 * 1024 * 1024


def split(value):
    high = value.astype(BF16)
    return high, (value - high.astype(F32)).astype(BF16)


def dot(a, b):
    return jnp.dot(a, b, preferred_element_type=F32)


def dot3(ah, al, bh, bl):
    return dot(ah, bh) + (dot(al, bh) + dot(ah, bl))


def peak(value):
    return jnp.max(jnp.max(value, axis=0, keepdims=True), axis=1, keepdims=True)


def rows_of(values):
    return jnp.concatenate([jnp.broadcast_to(v, (1, 128)) for v in values], axis=0)


def tables_kernel(band, kyh, kyl, kxh, kxl, *, ny):
    def entries(sq, ok):
        return jnp.where(ok, jnp.exp(sq.astype(F32) * (-2.0 / (BAND_MAX * BAND_MAX))), 0.0)

    def offsets(shape):
        return lax.broadcasted_iota(jnp.int32, shape, 0), lax.broadcasted_iota(jnp.int32, shape, 1)

    row, col = offsets(kyh.shape)
    shift = ny.bit_length() - 1
    dy = row - col
    kyh[...], kyl[...] = split(entries(dy * dy, ((row >> shift) == (col >> shift)) & (jnp.abs(dy) <= band[1])))
    row, col = offsets(kxh.shape)
    dx = row - col
    kxh[...], kxl[...] = split(entries(dx * dx, jnp.abs(dx) <= band[0]))


def tile_loop(ny, nx, step):
    across = nx // 128

    def body_of(i, carry):
        row = pl.multiple_of(lax.div(i, across) * 8, 8)
        column = pl.multiple_of(lax.rem(i, across) * 128, 128)
        step(row, pl.ds(column, 128))
        return carry

    lax.fori_loop(0, ny // 8 * across, body_of, 0)


def own_planes(lo, hi, kz, y, ny, entry_lo, entry_hi):
    side = lo.shape[0] // ny
    planes = 2 * side
    taps = [kz[d] for d in range(BAND_MAX + 1)]

    def step(row, columns):
        e = [entry_lo(lo[pl.ds(q * ny + row, 8), columns]) for q in range(side)]
        e += [entry_hi(hi[pl.ds(q * ny + row, 8), columns]) for q in range(side)]
        for p in range(planes):
            total = taps[0] * e[p]
            for d in range(1, BAND_MAX + 1):
                near = [e[q] for q in (p - d, p + d) if 0 <= q < planes]
                total += taps[d] * (near[0] if len(near) == 1 else near[0] + near[1])
            y[pl.ds(p * ny + row, 8), columns] = total

    tile_loop(ny, lo.shape[1], step)


def halo_planes(left, right, kz, y, z, ny, own, entry_left, entry_right):
    side = left.shape[0] // ny
    taps = [kz[d] for d in range(BAND_MAX + 1)]

    def step(row, columns):
        e = [entry_left(left[pl.ds(q * ny + row, 8), columns]) for q in range(side)]
        for p in range(side):
            rows = pl.ds(p * ny + row, 8)
            total = own(y[rows, columns])
            for q in range(max(0, p + side - BAND_MAX), side):
                total += taps[p + side - q] * e[q]
            z[rows, columns] = total
        e = [entry_right(right[pl.ds(q * ny + row, 8), columns]) for q in range(side)]
        for p in range(side):
            rows = pl.ds((side + p) * ny + row, 8)
            total = own(y[rows, columns])
            for q in range(min(side, p + BAND_MAX - side + 1)):
                total += taps[side + q - p] * e[q]
            z[rows, columns] = total

    tile_loop(ny, left.shape[1], step)


def tile(value):
    return jnp.broadcast_to(value, (8, 128))


def own_log_kernel(kz, lo, hi, y, stats, *, ny):
    m_lo, m_hi = peak(lo[...]), peak(hi[...])
    m = jnp.maximum(m_lo, m_hi)
    stats[...] = rows_of([m_lo, m_hi, m, m, m, m, m, m])
    m = tile(m)
    entry = lambda v: jnp.exp(v - m)
    own_planes(lo, hi, kz, y, ny, entry, entry)


def own_linear_kernel(kz, lo, hi, stats, y, *, ny):
    c = stats[0:1, 0:1]
    f_lo = tile(jnp.exp((c - stats[1:2, 0:1]) * 0.5))
    f_hi = tile(jnp.exp((c - stats[2:3, 0:1]) * 0.5))
    own_planes(lo, hi, kz, y, ny, lambda v: v * f_lo * f_lo, lambda v: v * f_hi * f_hi)


def rows_and_columns(z, g, kyh, kyl, kxh, kxl, mid):
    half, block = mid.shape[0], kyh.shape[0]
    for k in range(half // block):
        rows = pl.ds(g * half + k * block, block)
        zh, zl = split(z[rows, :])
        mid[k * block : (k + 1) * block, :] = dot3(kyh[...], kyl[...], zh, zl)
    mh, ml = split(mid[...])
    return dot3(mh, ml, kxh[...], kxl[...])


def log_halos(where, kz, left, right, y, stats, z, scale, ny):
    has_left, has_right = where[0] > 0, where[1] > 0
    m_own = stats[2:3, 0:1]
    m_left = jnp.where(has_left, peak(left[...]), m_own)
    m_right = jnp.where(has_right, peak(right[...]), m_own)
    c = jnp.maximum(m_own, jnp.maximum(m_left, m_right))
    scale[...] = rows_of([c, stats[0:1, 0:1], stats[1:2, 0:1], m_left, m_right, c, c, c])
    own = tile(jnp.exp(m_own - c))
    c = tile(c)
    halo_planes(
        left,
        right,
        kz,
        y,
        z,
        ny,
        lambda v: v * own,
        lambda v: jnp.where(has_left, jnp.exp(v - c), 0.0),
        lambda v: jnp.where(has_right, jnp.exp(v - c), 0.0),
    )


def potential_kernel(
    where, kz, left, right, y, stats, density, kyh, kyl, kxh, kxl, lo, hi, z, mid, scale, *, ny
):
    log_halos(where, kz, left, right, y, stats, z, scale, ny)
    half = mid.shape[0]
    for g, out in enumerate((lo, hi)):
        first = rows_and_columns(z, g, kyh, kyl, kxh, kxl, mid)
        out[...] = density[g * half : (g + 1) * half, :] - (jnp.log(first) + scale[0:1, 0:1])


def second_kernel(where, kz, left, right, y, stats, kyh, kyl, kxh, kxl, out, scale, z, mid, *, ny):
    log_halos(where, kz, left, right, y, stats, z, scale, ny)
    half = mid.shape[0]
    for g in range(2):
        out[g * half : (g + 1) * half, :] = rows_and_columns(z, g, kyh, kyl, kxh, kxl, mid)


def ratio_kernel(at, weight, second, scale, bary, cot, sum0, sum1, sum2, sum3, lo, hi, total):
    c = scale[0:1, 0:1]
    block = sum0.shape[0]
    count = second.shape[0] // block
    partial = jnp.zeros(total.shape, F32)
    for g in range(count):
        rows = slice(g * block, (g + 1) * block)
        away = lax.rem(g - at[0] + count, count)
        over_atoms = jnp.where(
            away == 0,
            sum0[...],
            jnp.where(away == 1, sum1[...], jnp.where(away == 2, sum2[...], sum3[...])),
        )
        summed = bary[rows, :] + over_atoms
        share = summed * (jnp.log(second[rows, :]) + c)
        share = jnp.sum(share.reshape(block // 8, 8, share.shape[1]), axis=0)
        for m in range(share.shape[1] // 128):
            partial += share[:, m * 128 : (m + 1) * 128]
        low = 2 * g < count
        f = jnp.exp(((scale[1:2, 0:1] if low else scale[2:3, 0:1]) - c) * 0.5)
        ratio = (weight[0] * summed - cot[rows, :]) / second[rows, :] * f * f
        out, first = (lo, 0) if low else (hi, count // 2)
        out[(g - first) * block : (g - first + 1) * block, :] = ratio
    total[...] = partial


def gradient_kernel(
    where, kz, left, right, y, stats, pot_lo, pot_hi, kyh, kyl, kxh, kxl, out, z, mid, *, ny
):
    g = pl.program_id(0)
    c = stats[0:1, 0:1]

    @pl.when(g == 0)
    def _():
        f_left = tile(jnp.exp((c - stats[3:4, 0:1]) * 0.5))
        f_right = tile(jnp.exp((c - stats[4:5, 0:1]) * 0.5))
        has_left, has_right = where[0] > 0, where[1] > 0
        halo_planes(
            left,
            right,
            kz,
            y,
            z,
            ny,
            lambda v: v,
            lambda v: jnp.where(has_left, v * f_left * f_left, 0.0),
            lambda v: jnp.where(has_right, v * f_right * f_right, 0.0),
        )

    for step, pot in enumerate((pot_lo, pot_hi)):

        @pl.when(g == step)
        def _(step=step, pot=pot):
            blurred = rows_and_columns(z, step, kyh, kyl, kxh, kxl, mid)
            out[...] = jnp.exp(pot[...] - c) * blurred


def body(
    atom_log_density,
    prior_log_scaling,
    atom_cotangent_rows,
    barycenter_cotangent,
    weights,
    band,
    slot_atom_index,
):
    planes, ny, nx = barycenter_cotangent.shape
    slabs, atoms = lax.axis_size("slab"), lax.axis_size("atom")
    rows = planes * ny
    half = rows // 2
    block = GROUP * ny
    count = planes // GROUP
    slab_at, atom_at = lax.axis_index("slab"), lax.axis_index("atom")
    across = atoms // 2
    x_at = atom_at // 2

    smem = pl.BlockSpec(memory_space=pltpu.SMEM)
    vmem = pl.BlockSpec(memory_space=pltpu.VMEM)
    params = pltpu.CompilerParams(vmem_limit_bytes=VMEM_LIMIT)

    def shape(*dims, dtype=F32):
        return jax.ShapeDtypeStruct(dims, dtype)

    def send(value, axis, pairs):
        return lax.ppermute(value, axis, pairs)

    in_order = lax.optimization_barrier
    to_right = [(i, i + 1) for i in range(slabs - 1)]
    to_left = [(i + 1, i) for i in range(slabs - 1)]
    ahead = {
        k: [(2 * x + z, 2 * ((x + k) % across) + z) for x in range(across) for z in range(2)]
        for k in range(1, across)
    }
    swap = [(i, i ^ 1) for i in range(atoms)]

    cot = atom_cotangent_rows.reshape(rows, nx)

    def block_of(k):
        return lax.dynamic_slice_in_dim(cot, lax.rem(x_at + k, count) * block, block)

    blocks = [block_of(k) for k in range(1, across)]
    part = block_of(0)
    for k in range(1, across):
        part = part + send(blocks[k - 1], "atom", ahead[k])

    y_shape, x_shape = (block, block), (nx, nx)
    distance = jnp.arange(BAND_MAX + 1, dtype=jnp.int32)
    kz = jnp.exp((distance * distance).astype(F32) * (-2.0 / (BAND_MAX * BAND_MAX)))
    kz = jnp.where(distance <= band[2], kz, 0.0)
    tables = pl.pallas_call(
        functools.partial(tables_kernel, ny=ny),
        out_shape=[shape(*dims, dtype=BF16) for dims in (y_shape, y_shape, x_shape, x_shape)],
        in_specs=[smem],
        out_specs=[vmem] * 4,
        compiler_params=params,
        name="tables",
    )(band)
    prior = prior_log_scaling.reshape(rows, nx)
    prior_lo, prior_hi = prior[:half], prior[half:]
    from_left = send(prior_hi, "slab", to_right)
    from_right = send(prior_lo, "slab", to_left)

    where = jnp.stack([(slab_at > 0), (slab_at < slabs - 1), x_at, x_at]).astype(jnp.int32)
    slot = lax.dynamic_slice_in_dim(slot_atom_index, atom_at, 1)
    onehot = (slot[0] == jnp.arange(weights.shape[0], dtype=jnp.int32)).astype(F32)
    weight = jnp.sum(onehot * weights, keepdims=True)

    own_out = [shape(rows, nx), shape(8, 128)]
    own_log = pl.pallas_call(
        functools.partial(own_log_kernel, ny=ny),
        in_specs=[smem, vmem, vmem],
        out_specs=[vmem, vmem],
        out_shape=own_out,
        compiler_params=params,
        name="own_log",
    )
    one = pl.BlockSpec((half, nx), lambda g: (g, 0))
    scratch = [pltpu.VMEM((rows, nx), F32), pltpu.VMEM((half, nx), F32)]
    scale = pltpu.VMEM((8, 128), F32)

    y, stats = own_log(kz, prior_lo, prior_hi)
    y, part = in_order((y, part))
    swapped = send(part, "atom", swap)
    pot_lo, pot_hi = pl.pallas_call(
        functools.partial(potential_kernel, ny=ny),
        in_specs=[smem, smem] + [vmem] * 9,
        out_specs=[vmem, vmem],
        out_shape=[shape(half, nx), shape(half, nx)],
        scratch_shapes=[*scratch, scale],
        compiler_params=params,
        name="potential",
    )(where, kz, from_left, from_right, y, stats, atom_log_density.reshape(rows, nx), *tables)

    from_left = send(pot_hi, "slab", to_right)
    from_right = send(pot_lo, "slab", to_left)
    both = part + swapped
    sums = [both] + [send(both, "atom", ahead[across - k]) for k in range(1, across)]
    y, stats = own_log(kz, pot_lo, pot_hi)
    y, sums[1] = in_order((y, sums[1]))
    second, stats = pl.pallas_call(
        functools.partial(second_kernel, ny=ny),
        in_specs=[smem, smem] + [vmem] * 8,
        out_specs=[vmem, vmem],
        out_shape=[shape(rows, nx), shape(8, 128)],
        scratch_shapes=scratch,
        compiler_params=params,
        name="second",
    )(where, kz, from_left, from_right, y, stats, *tables)
    ratio_lo, ratio_hi, total = pl.pallas_call(
        ratio_kernel,
        in_specs=[smem, smem] + [vmem] * 8,
        out_specs=[vmem] * 3,
        out_shape=[shape(half, nx), shape(half, nx), shape(8, 128)],
        compiler_params=params,
        name="ratio",
    )(
        where[2:],
        weight,
        second,
        stats,
        barycenter_cotangent.reshape(rows, nx),
        cot,
        *sums,
    )

    from_left = send(ratio_hi, "slab", to_right)
    from_right = send(ratio_lo, "slab", to_left)
    (y,) = pl.pallas_call(
        functools.partial(own_linear_kernel, ny=ny),
        in_specs=[smem, vmem, vmem, vmem],
        out_specs=[vmem],
        out_shape=[shape(rows, nx)],
        compiler_params=params,
        name="own_linear",
    )(kz, ratio_lo, ratio_hi, stats)

    def add(value, axis, patterns):
        return sum([send(value, axis, pairs) for pairs in patterns], value)

    def flips(hop):
        return [(i, i ^ hop) for i in range(slabs)]

    value = jnp.broadcast_to(jnp.sum(total), (8, 128))
    lanes = jnp.arange(128, dtype=jnp.int32)[None, :]
    value = jnp.where(lanes == slot[0], value, 0.0)
    value = add(value, "slab", [flips(1)])
    value = add(value, "atom", [ahead[k] for k in range(1, across)])
    value, y = in_order((value, y))
    value = add(value, "slab", [[(i, (i + k) % slabs) for i in range(slabs)] for k in (8, 16, 24)])
    for hop in (2, 4):
        value = add(value, "slab", [flips(hop)])
    value, from_left, from_right = in_order((value, from_left, from_right))
    value = add(value, "atom", [swap])
    weight_grad = value[0, : weights.shape[0]] / (rows * nx * slabs)

    gradient = pl.pallas_call(
        functools.partial(gradient_kernel, ny=ny),
        grid=(2,),
        in_specs=[smem, smem] + [vmem] * 10,
        out_specs=one,
        out_shape=shape(rows, nx),
        scratch_shapes=scratch,
        compiler_params=params,
        name="gradient",
    )(where, kz, from_left, from_right, y, stats, pot_lo, pot_hi, *tables)
    return gradient.reshape(atom_log_density.shape), weight_grad


def solution(mesh):
    return jax.shard_map(
        body,
        mesh=mesh,
        in_specs=(
            P("atom", "slab", None, None),
            P("atom", "slab", None, None),
            P("atom", "slab", None, None),
            P("slab", None, None),
            P(),
            P(),
            P(),
        ),
        out_specs=(P("atom", "slab", None, None), P()),
        check_vma=False,
    )
```

```python
import functools

import jax
import jax.numpy as jnp
from jax import lax
from jax.experimental import pallas as pl
from jax.experimental.pallas import tpu as pltpu
from jax.sharding import PartitionSpec as P

BAND_MAX = 8
GROUP = 4
F32 = jnp.float32
BF16 = jnp.bfloat16
VMEM_LIMIT = 12 * 1024 * 1024


def split(value):
    high = value.astype(BF16)
    return high, (value - high.astype(F32)).astype(BF16)


def dot(a, b):
    return jnp.dot(a, b, preferred_element_type=F32)


def dot3(ah, al, bh, bl):
    return dot(ah, bh) + (dot(al, bh) + dot(ah, bl))


def peak(value):
    return jnp.max(jnp.max(value, axis=0, keepdims=True), axis=1, keepdims=True)


def rows_of(values):
    return jnp.concatenate([jnp.broadcast_to(v, (1, 128)) for v in values], axis=0)


def tables_kernel(band, kyh, kyl, kxh, kxl, *, ny):
    def entries(sq, ok):
        return jnp.where(ok, jnp.exp(sq.astype(F32) * (-2.0 / (BAND_MAX * BAND_MAX))), 0.0)

    def offsets(shape):
        return lax.broadcasted_iota(jnp.int32, shape, 0), lax.broadcasted_iota(jnp.int32, shape, 1)

    row, col = offsets(kyh.shape)
    shift = ny.bit_length() - 1
    dy = row - col
    kyh[...], kyl[...] = split(entries(dy * dy, ((row >> shift) == (col >> shift)) & (jnp.abs(dy) <= band[1])))
    row, col = offsets(kxh.shape)
    dx = row - col
    kxh[...], kxl[...] = split(entries(dx * dx, jnp.abs(dx) <= band[0]))


def tile_loop(ny, nx, step):
    across = nx // 128

    def body_of(i, carry):
        row = pl.multiple_of(lax.div(i, across) * 8, 8)
        column = pl.multiple_of(lax.rem(i, across) * 128, 128)
        step(row, pl.ds(column, 128))
        return carry

    lax.fori_loop(0, ny // 8 * across, body_of, 0)


def own_planes(lo, hi, kz, y, ny, entry_lo, entry_hi):
    side = lo.shape[0] // ny
    planes = 2 * side
    taps = [kz[d] for d in range(BAND_MAX + 1)]

    def step(row, columns):
        e = [entry_lo(lo[pl.ds(q * ny + row, 8), columns]) for q in range(side)]
        e += [entry_hi(hi[pl.ds(q * ny + row, 8), columns]) for q in range(side)]
        for p in range(planes):
            total = taps[0] * e[p]
            for d in range(1, BAND_MAX + 1):
                near = [e[q] for q in (p - d, p + d) if 0 <= q < planes]
                total += taps[d] * (near[0] if len(near) == 1 else near[0] + near[1])
            y[pl.ds(p * ny + row, 8), columns] = total

    tile_loop(ny, lo.shape[1], step)


def halo_planes(left, right, kz, y, z, ny, own, entry_left, entry_right):
    per = left[0].shape[0] // ny
    side = per * len(left)
    taps = [kz[d] for d in range(BAND_MAX + 1)]

    def step(row, columns):
        e = [entry_left(left[q // per][pl.ds(q % per * ny + row, 8), columns]) for q in range(side)]
        for p in range(side):
            rows = pl.ds(p * ny + row, 8)
            total = own(y[rows, columns])
            for q in range(max(0, p + side - BAND_MAX), side):
                total += taps[p + side - q] * e[q]
            z[rows, columns] = total
        e = [entry_right(right[q // per][pl.ds(q % per * ny + row, 8), columns]) for q in range(side)]
        for p in range(side):
            rows = pl.ds((side + p) * ny + row, 8)
            total = own(y[rows, columns])
            for q in range(min(side, p + BAND_MAX - side + 1)):
                total += taps[side + q - p] * e[q]
            z[rows, columns] = total

    tile_loop(ny, left[0].shape[1], step)


def tile(value):
    return jnp.broadcast_to(value, (8, 128))


def own_log_kernel(kz, lo, hi, y, stats, *, ny):
    m_lo, m_hi = peak(lo[...]), peak(hi[...])
    m = jnp.maximum(m_lo, m_hi)
    stats[...] = rows_of([m_lo, m_hi, m, m, m, m, m, m])
    m = tile(m)
    entry = lambda v: jnp.exp(v - m)
    own_planes(lo, hi, kz, y, ny, entry, entry)


def own_linear_kernel(kz, lo, hi, pot_lo, pot_hi, stats, y, shifted, *, ny):
    c = stats[0:1, 0:1]
    half = lo.shape[0]
    shifted[:half, :] = jnp.exp(pot_lo[...] - c)
    shifted[half:, :] = jnp.exp(pot_hi[...] - c)
    f_lo = tile(jnp.exp((c - stats[1:2, 0:1]) * 0.5))
    f_hi = tile(jnp.exp((c - stats[2:3, 0:1]) * 0.5))
    own_planes(lo, hi, kz, y, ny, lambda v: v * f_lo * f_lo, lambda v: v * f_hi * f_hi)


def rows_and_columns(z, g, kyh, kyl, kxh, kxl, mid):
    half, block = mid.shape[0], kyh.shape[0]
    for k in range(half // block):
        rows = pl.ds(g * half + k * block, block)
        zh, zl = split(z[rows, :])
        mid[k * block : (k + 1) * block, :] = dot3(kyh[...], kyl[...], zh, zl)
    mh, ml = split(mid[...])
    return dot3(mh, ml, kxh[...], kxl[...])


def log_halos(where, kz, left, right, y, stats, z, scale, ny):
    has_left, has_right = where[0] > 0, where[1] > 0
    m_own = stats[2:3, 0:1]
    m_left = jnp.where(has_left, functools.reduce(jnp.maximum, [peak(ref[...]) for ref in left]), m_own)
    m_right = jnp.where(has_right, functools.reduce(jnp.maximum, [peak(ref[...]) for ref in right]), m_own)
    c = jnp.maximum(m_own, jnp.maximum(m_left, m_right))
    scale[...] = rows_of([c, stats[0:1, 0:1], stats[1:2, 0:1], m_left, m_right, c, c, c])
    own = tile(jnp.exp(m_own - c))
    c = tile(c)
    halo_planes(
        left,
        right,
        kz,
        y,
        z,
        ny,
        lambda v: v * own,
        lambda v: jnp.where(has_left, jnp.exp(v - c), 0.0),
        lambda v: jnp.where(has_right, jnp.exp(v - c), 0.0),
    )


def potential_kernel(
    where, kz, left0, left1, right0, right1, y, stats, density, kyh, kyl, kxh, kxl, lo, hi, z, mid, scale, *, ny
):
    log_halos(where, kz, (left0, left1), (right0, right1), y, stats, z, scale, ny)
    half = mid.shape[0]
    for g, out in enumerate((lo, hi)):
        first = rows_and_columns(z, g, kyh, kyl, kxh, kxl, mid)
        out[...] = density[g * half : (g + 1) * half, :] - (jnp.log(first) + scale[0:1, 0:1])


def second_kernel(where, kz, left, right, y, stats, kyh, kyl, kxh, kxl, out, scale, z, mid, *, ny):
    log_halos(where, kz, (left,), (right,), y, stats, z, scale, ny)
    half = mid.shape[0]
    for g in range(2):
        out[g * half : (g + 1) * half, :] = rows_and_columns(z, g, kyh, kyl, kxh, kxl, mid)


def ratio_kernel(
    at, weight, second, scale, bary, cot, sum0, sum1, sum2, sum3, lo, hi, total, sums, out, sems
):
    c = scale[0:1, 0:1]
    block, columns = sums.shape[1:]
    count = sums.shape[0]
    half = out.shape[0] // 2
    arriving = [
        pltpu.make_async_copy(ref, sums.at[k], sems.at[k]) for k, ref in enumerate((sum0, sum1, sum2, sum3))
    ]
    for copy in arriving:
        copy.start()
    partial = jnp.zeros((8, 128), F32)
    f_lo = jnp.exp((scale[1:2, 0:1] - c) * 0.5)
    f_hi = jnp.exp((scale[2:3, 0:1] - c) * 0.5)
    for k, copy in enumerate(arriving):
        copy.wait()
        g = lax.rem(at[0] + k, count)
        rows = pl.ds(pl.multiple_of(g * block, block), block)
        summed = bary[rows, :] + sums[k]
        denominator = second[rows, :]
        share = summed * (jnp.log(denominator) + c)
        share = jnp.sum(share.reshape(block // 8, 8, columns), axis=0)
        for m in range(columns // 128):
            partial += share[:, m * 128 : (m + 1) * 128]
        f = jnp.where(2 * g < count, f_lo, f_hi)
        out[rows, :] = (weight[0] * summed - cot[rows, :]) / denominator * f * f
    leaving = [
        pltpu.make_async_copy(out.at[:half], lo, sems.at[0]),
        pltpu.make_async_copy(out.at[half:], hi, sems.at[1]),
    ]
    for copy in leaving:
        copy.start()
    lanes = lax.broadcasted_iota(jnp.int32, total.shape, 1)
    partial = jnp.sum(jnp.sum(partial, axis=0, keepdims=True), axis=1, keepdims=True)
    total[...] = jnp.where(lanes == at[1], partial, 0.0)
    for copy in leaving:
        copy.wait()


def gradient_kernel(
    where, kz, left, right, y, shifted, stats, kyh, kyl, kxh, kxl, out, z, mid, *, ny
):
    g = pl.program_id(0)
    c = stats[0:1, 0:1]

    @pl.when(g == 0)
    def _():
        f_left = tile(jnp.exp((c - stats[3:4, 0:1]) * 0.5))
        f_right = tile(jnp.exp((c - stats[4:5, 0:1]) * 0.5))
        has_left, has_right = where[0] > 0, where[1] > 0
        halo_planes(
            (left,),
            (right,),
            kz,
            y,
            z,
            ny,
            lambda v: v,
            lambda v: jnp.where(has_left, v * f_left * f_left, 0.0),
            lambda v: jnp.where(has_right, v * f_right * f_right, 0.0),
        )

    for step in range(2):

        @pl.when(g == step)
        def _(step=step):
            blurred = rows_and_columns(z, step, kyh, kyl, kxh, kxl, mid)
            half = out.shape[0]
            out[...] = shifted[step * half : (step + 1) * half, :] * blurred


def body(
    atom_log_density,
    prior_log_scaling,
    atom_cotangent_rows,
    barycenter_cotangent,
    weights,
    band,
    slot_atom_index,
):
    planes, ny, nx = barycenter_cotangent.shape
    slabs, atoms = lax.axis_size("slab"), lax.axis_size("atom")
    rows = planes * ny
    half = rows // 2
    block = GROUP * ny
    count = planes // GROUP
    slab_at, atom_at = lax.axis_index("slab"), lax.axis_index("atom")
    across = atoms // 2
    x_at = atom_at // 2

    smem = pl.BlockSpec(memory_space=pltpu.SMEM)
    vmem = pl.BlockSpec(memory_space=pltpu.VMEM)
    anywhere = pl.BlockSpec(memory_space=pl.ANY)
    params = pltpu.CompilerParams(vmem_limit_bytes=VMEM_LIMIT)

    def shape(*dims, dtype=F32):
        return jax.ShapeDtypeStruct(dims, dtype)

    def send(value, axis, pairs):
        return lax.ppermute(value, axis, pairs)

    in_order = lax.optimization_barrier
    to_right = [(i, i + 1) for i in range(slabs - 1)]
    to_left = [(i + 1, i) for i in range(slabs - 1)]
    ahead = {
        k: [(2 * x + z, 2 * ((x + k) % across) + z) for x in range(across) for z in range(2)]
        for k in range(1, across)
    }
    swap = [(i, i ^ 1) for i in range(atoms)]

    cot = atom_cotangent_rows.reshape(rows, nx)

    def block_of(k):
        return lax.dynamic_slice_in_dim(cot, lax.rem(x_at + k, count) * block, block)

    blocks = [block_of(k) for k in range(1, across)]
    part = block_of(0)
    for k in range(1, across):
        part = part + send(blocks[k - 1], "atom", ahead[k])

    y_shape, x_shape = (block, block), (nx, nx)
    distance = jnp.arange(BAND_MAX + 1, dtype=jnp.int32)
    kz = jnp.exp((distance * distance).astype(F32) * (-2.0 / (BAND_MAX * BAND_MAX)))
    kz = jnp.where(distance <= band[2], kz, 0.0)
    tables = pl.pallas_call(
        functools.partial(tables_kernel, ny=ny),
        out_shape=[shape(*dims, dtype=BF16) for dims in (y_shape, y_shape, x_shape, x_shape)],
        in_specs=[smem],
        out_specs=[vmem] * 4,
        compiler_params=params,
        name="tables",
    )(band)
    prior = prior_log_scaling.reshape(rows, nx)
    prior_lo, prior_hi = prior[:half], prior[half:]
    piece = half // 2
    from_left = [send(prior_hi[k * piece : (k + 1) * piece], "slab", to_right) for k in range(2)]
    from_right = [send(prior_lo[k * piece : (k + 1) * piece], "slab", to_left) for k in range(2)]

    where = jnp.stack([slab_at > 0, slab_at < slabs - 1]).astype(jnp.int32)
    slot = lax.dynamic_slice_in_dim(slot_atom_index, atom_at, 1)
    onehot = (slot[0] == jnp.arange(weights.shape[0], dtype=jnp.int32)).astype(F32)
    weight = jnp.sum(onehot * weights, keepdims=True)

    own_out = [shape(rows, nx), shape(8, 128)]
    own_log = pl.pallas_call(
        functools.partial(own_log_kernel, ny=ny),
        in_specs=[smem, vmem, vmem],
        out_specs=[vmem, vmem],
        out_shape=own_out,
        compiler_params=params,
        name="own_log",
    )
    one = pl.BlockSpec((half, nx), lambda g: (g, 0))
    scratch = [pltpu.VMEM((rows, nx), F32), pltpu.VMEM((half, nx), F32)]
    scale = pltpu.VMEM((8, 128), F32)

    y, stats = own_log(kz, prior_lo, prior_hi)
    y, part = in_order((y, part))
    swapped = send(part, "atom", swap)
    pot_lo, pot_hi = pl.pallas_call(
        functools.partial(potential_kernel, ny=ny),
        in_specs=[smem, smem] + [vmem] * 11,
        out_specs=[vmem, vmem],
        out_shape=[shape(half, nx), shape(half, nx)],
        scratch_shapes=[*scratch, scale],
        compiler_params=params,
        name="potential",
    )(where, kz, *from_left, *from_right, y, stats, atom_log_density.reshape(rows, nx), *tables)

    from_left = send(pot_hi, "slab", to_right)
    from_right = send(pot_lo, "slab", to_left)
    both = part + swapped
    sums = [both] + [send(both, "atom", ahead[across - k]) for k in range(1, across)]
    y, stats = own_log(kz, pot_lo, pot_hi)
    y, sums[1] = in_order((y, sums[1]))
    second, stats = pl.pallas_call(
        functools.partial(second_kernel, ny=ny),
        in_specs=[smem, smem] + [vmem] * 8,
        out_specs=[vmem, vmem],
        out_shape=[shape(rows, nx), shape(8, 128)],
        scratch_shapes=scratch,
        compiler_params=params,
        name="second",
    )(where, kz, from_left, from_right, y, stats, *tables)
    ratio_lo, ratio_hi, total = pl.pallas_call(
        ratio_kernel,
        in_specs=[smem, smem] + [vmem] * 4 + [anywhere] * 4,
        out_specs=[anywhere, anywhere, vmem],
        out_shape=[shape(half, nx), shape(half, nx), shape(8, 128)],
        scratch_shapes=[
            pltpu.VMEM((count, block, nx), F32),
            pltpu.VMEM((rows, nx), F32),
            pltpu.SemaphoreType.DMA((count,)),
        ],
        compiler_params=params,
        name="ratio",
    )(
        jnp.stack([x_at, slot[0]]),
        weight,
        second,
        stats,
        barycenter_cotangent.reshape(rows, nx),
        cot,
        *sums,
    )

    from_left = send(ratio_hi, "slab", to_right)
    from_right = send(ratio_lo, "slab", to_left)
    y, shifted = pl.pallas_call(
        functools.partial(own_linear_kernel, ny=ny),
        in_specs=[smem] + [vmem] * 5,
        out_specs=[vmem, vmem],
        out_shape=[shape(rows, nx), shape(rows, nx)],
        compiler_params=params,
        name="own_linear",
    )(kz, ratio_lo, ratio_hi, pot_lo, pot_hi, stats)

    def add(value, axis, patterns):
        return sum([send(value, axis, pairs) for pairs in patterns], value)

    def flips(hop):
        return [(i, i ^ hop) for i in range(slabs)]

    value = add(total, "slab", [flips(1)])
    value = add(value, "atom", [ahead[k] for k in range(1, across)])
    value, y = in_order((value, y))
    value = add(value, "slab", [[(i, (i + k) % slabs) for i in range(slabs)] for k in (8, 16, 24)])
    for hop in (2, 4):
        value = add(value, "slab", [flips(hop)])
    value, from_left, from_right = in_order((value, from_left, from_right))
    value = add(value, "atom", [swap])
    weight_grad = value[0, : weights.shape[0]] / (rows * nx * slabs)

    gradient = pl.pallas_call(
        functools.partial(gradient_kernel, ny=ny),
        grid=(2,),
        in_specs=[smem, smem] + [vmem] * 9,
        out_specs=one,
        out_shape=shape(rows, nx),
        scratch_shapes=scratch,
        compiler_params=params,
        name="gradient",
    )(where, kz, from_left, from_right, y, shifted, stats, *tables)
    return gradient.reshape(atom_log_density.shape), weight_grad


def solution(mesh):
    return jax.shard_map(
        body,
        mesh=mesh,
        in_specs=(
            P("atom", "slab", None, None),
            P("atom", "slab", None, None),
            P("atom", "slab", None, None),
            P("slab", None, None),
            P(),
            P(),
            P(),
        ),
        out_specs=(P("atom", "slab", None, None), P()),
        check_vma=False,
    )
```

```python
import functools

import jax
import jax.numpy as jnp
from jax import lax
from jax.experimental import pallas as pl
from jax.experimental.pallas import tpu as pltpu
from jax.sharding import PartitionSpec as P

BAND_MAX = 8
GROUP = 4
F32 = jnp.float32
BF16 = jnp.bfloat16
VMEM_LIMIT = 12 * 1024 * 1024


def split(value):
    high = value.astype(BF16)
    return high, (value - high.astype(F32)).astype(BF16)


def dot(a, b):
    return jnp.dot(a, b, preferred_element_type=F32)


def dot3(ah, al, bh, bl):
    return dot(ah, bh) + (dot(al, bh) + dot(ah, bl))


def peak(value):
    return jnp.max(jnp.max(value, axis=0, keepdims=True), axis=1, keepdims=True)


def rows_of(values):
    return jnp.concatenate([jnp.broadcast_to(v, (1, 128)) for v in values], axis=0)


def tables_kernel(band, kyh, kyl, kxh, kxl, *, ny):
    def entries(sq, ok):
        return jnp.where(ok, jnp.exp(sq.astype(F32) * (-2.0 / (BAND_MAX * BAND_MAX))), 0.0)

    def offsets(shape):
        return lax.broadcasted_iota(jnp.int32, shape, 0), lax.broadcasted_iota(jnp.int32, shape, 1)

    row, col = offsets(kyh.shape)
    shift = ny.bit_length() - 1
    dy = row - col
    kyh[...], kyl[...] = split(entries(dy * dy, ((row >> shift) == (col >> shift)) & (jnp.abs(dy) <= band[1])))
    row, col = offsets(kxh.shape)
    dx = row - col
    kxh[...], kxl[...] = split(entries(dx * dx, jnp.abs(dx) <= band[0]))


def tile_loop(ny, nx, step):
    across = nx // 128

    def body_of(i, carry):
        row = pl.multiple_of(lax.div(i, across) * 8, 8)
        column = pl.multiple_of(lax.rem(i, across) * 128, 128)
        step(row, pl.ds(column, 128))
        return carry

    lax.fori_loop(0, ny // 8 * across, body_of, 0)


def own_planes(lo, hi, kz, y, ny, entry_lo, entry_hi):
    side = lo.shape[0] // ny
    planes = 2 * side
    taps = [kz[d] for d in range(BAND_MAX + 1)]

    def step(row, columns):
        e = [entry_lo(lo[pl.ds(q * ny + row, 8), columns]) for q in range(side)]
        e += [entry_hi(hi[pl.ds(q * ny + row, 8), columns]) for q in range(side)]
        for p in range(planes):
            total = taps[0] * e[p]
            for d in range(1, BAND_MAX + 1):
                near = [e[q] for q in (p - d, p + d) if 0 <= q < planes]
                total += taps[d] * (near[0] if len(near) == 1 else near[0] + near[1])
            y[pl.ds(p * ny + row, 8), columns] = total

    tile_loop(ny, lo.shape[1], step)


def halo_planes(left, right, kz, y, z, ny, own, entry_left, entry_right):
    side = left.shape[0] // ny
    taps = [kz[d] for d in range(BAND_MAX + 1)]

    def step(row, columns):
        e = [entry_left(left[pl.ds(q * ny + row, 8), columns]) for q in range(side)]
        for p in range(side):
            rows = pl.ds(p * ny + row, 8)
            total = own(y[rows, columns])
            for q in range(max(0, p + side - BAND_MAX), side):
                total += taps[p + side - q] * e[q]
            z[rows, columns] = total
        e = [entry_right(right[pl.ds(q * ny + row, 8), columns]) for q in range(side)]
        for p in range(side):
            rows = pl.ds((side + p) * ny + row, 8)
            total = own(y[rows, columns])
            for q in range(min(side, p + BAND_MAX - side + 1)):
                total += taps[side + q - p] * e[q]
            z[rows, columns] = total

    tile_loop(ny, left.shape[1], step)


def tile(value):
    return jnp.broadcast_to(value, (8, 128))


def own_log_kernel(kz, lo, hi, y, stats, *, ny):
    m_lo, m_hi = peak(lo[...]), peak(hi[...])
    m = jnp.maximum(m_lo, m_hi)
    stats[...] = rows_of([m_lo, m_hi, m, m, m, m, m, m])
    m = tile(m)
    entry = lambda v: jnp.exp(v - m)
    own_planes(lo, hi, kz, y, ny, entry, entry)


def own_linear_kernel(kz, lo, hi, pot_lo, pot_hi, stats, y, shifted, *, ny):
    c = stats[0:1, 0:1]
    half = lo.shape[0]
    shifted[:half, :] = jnp.exp(pot_lo[...] - c)
    shifted[half:, :] = jnp.exp(pot_hi[...] - c)
    f_lo = tile(jnp.exp((c - stats[1:2, 0:1]) * 0.5))
    f_hi = tile(jnp.exp((c - stats[2:3, 0:1]) * 0.5))
    own_planes(lo, hi, kz, y, ny, lambda v: v * f_lo * f_lo, lambda v: v * f_hi * f_hi)


def rows_and_columns(z, g, kyh, kyl, kxh, kxl, mid):
    half, block = mid.shape[0], kyh.shape[0]
    for k in range(half // block):
        rows = pl.ds(g * half + k * block, block)
        zh, zl = split(z[rows, :])
        mid[k * block : (k + 1) * block, :] = dot3(kyh[...], kyl[...], zh, zl)
    mh, ml = split(mid[...])
    return dot3(mh, ml, kxh[...], kxl[...])


def log_halos(where, kz, left, right, y, stats, z, scale, ny):
    has_left, has_right = where[0] > 0, where[1] > 0
    m_own = stats[2:3, 0:1]
    m_left = jnp.where(has_left, peak(left[...]), m_own)
    m_right = jnp.where(has_right, peak(right[...]), m_own)
    c = jnp.maximum(m_own, jnp.maximum(m_left, m_right))
    scale[...] = rows_of([c, stats[0:1, 0:1], stats[1:2, 0:1], m_left, m_right, c, c, c])
    own = tile(jnp.exp(m_own - c))
    c = tile(c)
    halo_planes(
        left,
        right,
        kz,
        y,
        z,
        ny,
        lambda v: v * own,
        lambda v: jnp.where(has_left, jnp.exp(v - c), 0.0),
        lambda v: jnp.where(has_right, jnp.exp(v - c), 0.0),
    )


def potential_kernel(
    where, kz, left, right, y, stats, density, kyh, kyl, kxh, kxl, lo, hi, z, mid, scale, *, ny
):
    log_halos(where, kz, left, right, y, stats, z, scale, ny)
    half = mid.shape[0]
    for g, out in enumerate((lo, hi)):
        first = rows_and_columns(z, g, kyh, kyl, kxh, kxl, mid)
        out[...] = density[g * half : (g + 1) * half, :] - (jnp.log(first) + scale[0:1, 0:1])


def second_kernel(where, kz, left, right, y, stats, kyh, kyl, kxh, kxl, out, scale, z, mid, *, ny):
    log_halos(where, kz, left, right, y, stats, z, scale, ny)
    half = mid.shape[0]
    for g in range(2):
        out[g * half : (g + 1) * half, :] = rows_and_columns(z, g, kyh, kyl, kxh, kxl, mid)


def ratio_kernel(at, weight, second, scale, bary, cot, *refs):
    lo, hi, total, sums, out, sems = refs[-6:]
    c = scale[0:1, 0:1]
    pieces, block, columns = sums.shape
    count = pieces // 2
    half = out.shape[0] // 2
    arriving = [pltpu.make_async_copy(ref, sums.at[k], sems.at[k]) for k, ref in enumerate(refs[:-6])]
    for copy in arriving:
        copy.start()
    partial = jnp.zeros((8, 128), F32)
    f_lo = jnp.exp((scale[1:2, 0:1] - c) * 0.5)
    f_hi = jnp.exp((scale[2:3, 0:1] - c) * 0.5)
    for k, copy in enumerate(arriving):
        copy.wait()
        g = lax.rem(at[0] + k, count)
        rows = pl.ds(pl.multiple_of((2 * g + k // count) * block, block), block)
        summed = bary[rows, :] + sums[k]
        denominator = second[rows, :]
        share = summed * (jnp.log(denominator) + c)
        share = jnp.sum(share.reshape(block // 8, 8, columns), axis=0)
        for m in range(columns // 128):
            partial += share[:, m * 128 : (m + 1) * 128]
        f = jnp.where(2 * g < count, f_lo, f_hi)
        out[rows, :] = (weight[0] * summed - cot[rows, :]) / denominator * f * f
    leaving = [
        pltpu.make_async_copy(out.at[:half], lo, sems.at[0]),
        pltpu.make_async_copy(out.at[half:], hi, sems.at[1]),
    ]
    for copy in leaving:
        copy.start()
    lanes = lax.broadcasted_iota(jnp.int32, total.shape, 1)
    partial = jnp.sum(jnp.sum(partial, axis=0, keepdims=True), axis=1, keepdims=True)
    total[...] = jnp.where(lanes == at[1], partial, 0.0)
    for copy in leaving:
        copy.wait()


def gradient_kernel(
    where, kz, left, right, y, shifted, stats, kyh, kyl, kxh, kxl, out, z, mid, *, ny
):
    g = pl.program_id(0)
    c = stats[0:1, 0:1]

    @pl.when(g == 0)
    def _():
        f_left = tile(jnp.exp((c - stats[3:4, 0:1]) * 0.5))
        f_right = tile(jnp.exp((c - stats[4:5, 0:1]) * 0.5))
        has_left, has_right = where[0] > 0, where[1] > 0
        halo_planes(
            left,
            right,
            kz,
            y,
            z,
            ny,
            lambda v: v,
            lambda v: jnp.where(has_left, v * f_left * f_left, 0.0),
            lambda v: jnp.where(has_right, v * f_right * f_right, 0.0),
        )

    for step in range(2):

        @pl.when(g == step)
        def _(step=step):
            blurred = rows_and_columns(z, step, kyh, kyl, kxh, kxl, mid)
            half = out.shape[0]
            out[...] = shifted[step * half : (step + 1) * half, :] * blurred


def body(
    atom_log_density,
    prior_log_scaling,
    atom_cotangent_rows,
    barycenter_cotangent,
    weights,
    band,
    slot_atom_index,
):
    planes, ny, nx = barycenter_cotangent.shape
    slabs, atoms = lax.axis_size("slab"), lax.axis_size("atom")
    rows = planes * ny
    half = rows // 2
    block = GROUP * ny
    count = planes // GROUP
    slab_at, atom_at = lax.axis_index("slab"), lax.axis_index("atom")
    across = atoms // 2
    x_at = atom_at // 2

    smem = pl.BlockSpec(memory_space=pltpu.SMEM)
    vmem = pl.BlockSpec(memory_space=pltpu.VMEM)
    anywhere = pl.BlockSpec(memory_space=pl.ANY)
    params = pltpu.CompilerParams(vmem_limit_bytes=VMEM_LIMIT)

    def shape(*dims, dtype=F32):
        return jax.ShapeDtypeStruct(dims, dtype)

    def send(value, axis, pairs):
        return lax.ppermute(value, axis, pairs)

    in_order = lax.optimization_barrier
    to_right = [(i, i + 1) for i in range(slabs - 1)]
    to_left = [(i + 1, i) for i in range(slabs - 1)]
    ahead = {
        k: [(2 * x + z, 2 * ((x + k) % across) + z) for x in range(across) for z in range(2)]
        for k in range(1, across)
    }
    swap = [(i, i ^ 1) for i in range(atoms)]

    cot = atom_cotangent_rows.reshape(rows, nx)

    def block_of(k, h):
        return lax.dynamic_slice_in_dim(cot, lax.rem(x_at + k, count) * block + h * block // 2, block // 2)

    def over_x(h):
        return sum([send(block_of(k, h), "atom", ahead[k]) for k in range(1, across)], block_of(0, h))

    parts = [over_x(h) for h in range(2)]


    y_shape, x_shape = (block, block), (nx, nx)
    distance = jnp.arange(BAND_MAX + 1, dtype=jnp.int32)
    kz = jnp.exp((distance * distance).astype(F32) * (-2.0 / (BAND_MAX * BAND_MAX)))
    kz = jnp.where(distance <= band[2], kz, 0.0)
    tables = pl.pallas_call(
        functools.partial(tables_kernel, ny=ny),
        out_shape=[shape(*dims, dtype=BF16) for dims in (y_shape, y_shape, x_shape, x_shape)],
        in_specs=[smem],
        out_specs=[vmem] * 4,
        compiler_params=params,
        name="tables",
    )(band)
    prior = prior_log_scaling.reshape(rows, nx)
    prior_lo, prior_hi = prior[:half], prior[half:]
    from_left = send(prior_hi, "slab", to_right)
    from_right = send(prior_lo, "slab", to_left)

    where = jnp.stack([slab_at > 0, slab_at < slabs - 1]).astype(jnp.int32)
    slot = lax.dynamic_slice_in_dim(slot_atom_index, atom_at, 1)
    onehot = (slot[0] == jnp.arange(weights.shape[0], dtype=jnp.int32)).astype(F32)
    weight = jnp.sum(onehot * weights, keepdims=True)

    own_out = [shape(rows, nx), shape(8, 128)]
    own_log = pl.pallas_call(
        functools.partial(own_log_kernel, ny=ny),
        in_specs=[smem, vmem, vmem],
        out_specs=[vmem, vmem],
        out_shape=own_out,
        compiler_params=params,
        name="own_log",
    )
    one = pl.BlockSpec((half, nx), lambda g: (g, 0))
    scratch = [pltpu.VMEM((rows, nx), F32), pltpu.VMEM((half, nx), F32)]
    scale = pltpu.VMEM((8, 128), F32)

    y, stats = own_log(kz, prior_lo, prior_hi)
    swapped = [send(part, "atom", swap) for part in parts]
    y, swapped[0] = in_order((y, swapped[0]))
    pot_lo, pot_hi = pl.pallas_call(
        functools.partial(potential_kernel, ny=ny),
        in_specs=[smem, smem] + [vmem] * 9,
        out_specs=[vmem, vmem],
        out_shape=[shape(half, nx), shape(half, nx)],
        scratch_shapes=[*scratch, scale],
        compiler_params=params,
        name="potential",
    )(where, kz, from_left, from_right, y, stats, atom_log_density.reshape(rows, nx), *tables)

    from_left = send(pot_hi, "slab", to_right)
    from_right = send(pot_lo, "slab", to_left)
    both = [part + other for part, other in zip(parts, swapped)]
    sums = [[both[h]] + [send(both[h], "atom", ahead[across - k]) for k in range(1, across)] for h in range(2)]
    y, stats = own_log(kz, pot_lo, pot_hi)
    y, sums[0] = in_order((y, sums[0]))
    second, stats = pl.pallas_call(
        functools.partial(second_kernel, ny=ny),
        in_specs=[smem, smem] + [vmem] * 8,
        out_specs=[vmem, vmem],
        out_shape=[shape(rows, nx), shape(8, 128)],
        scratch_shapes=scratch,
        compiler_params=params,
        name="second",
    )(where, kz, from_left, from_right, y, stats, *tables)
    ratio_lo, ratio_hi, total = pl.pallas_call(
        ratio_kernel,
        in_specs=[smem, smem] + [vmem] * 4 + [anywhere] * (2 * count),
        out_specs=[anywhere, anywhere, vmem],
        out_shape=[shape(half, nx), shape(half, nx), shape(8, 128)],
        scratch_shapes=[
            pltpu.VMEM((2 * count, block // 2, nx), F32),
            pltpu.VMEM((rows, nx), F32),
            pltpu.SemaphoreType.DMA((2 * count,)),
        ],
        compiler_params=params,
        name="ratio",
    )(
        jnp.stack([x_at, slot[0]]),
        weight,
        second,
        stats,
        barycenter_cotangent.reshape(rows, nx),
        cot,
        *sums[0],
        *sums[1],
    )

    from_left = send(ratio_hi, "slab", to_right)
    from_right = send(ratio_lo, "slab", to_left)
    y, shifted = pl.pallas_call(
        functools.partial(own_linear_kernel, ny=ny),
        in_specs=[smem] + [vmem] * 5,
        out_specs=[vmem, vmem],
        out_shape=[shape(rows, nx), shape(rows, nx)],
        compiler_params=params,
        name="own_linear",
    )(kz, ratio_lo, ratio_hi, pot_lo, pot_hi, stats)

    total, y = in_order((total, y))
    value = jnp.broadcast_to(total[:1], (atoms * slabs, 128))
    value = lax.all_to_all(value, ("atom", "slab"), 0, 0, tiled=True)
    weight_grad = jnp.sum(value, axis=0)[: weights.shape[0]] / (rows * nx * slabs)

    gradient = pl.pallas_call(
        functools.partial(gradient_kernel, ny=ny),
        grid=(2,),
        in_specs=[smem, smem] + [vmem] * 9,
        out_specs=one,
        out_shape=shape(rows, nx),
        scratch_shapes=scratch,
        compiler_params=params,
        name="gradient",
    )(where, kz, from_left, from_right, y, shifted, stats, *tables)
    return gradient.reshape(atom_log_density.shape), weight_grad


def solution(mesh):
    return jax.shard_map(
        body,
        mesh=mesh,
        in_specs=(
            P("atom", "slab", None, None),
            P("atom", "slab", None, None),
            P("atom", "slab", None, None),
            P("slab", None, None),
            P(),
            P(),
            P(),
        ),
        out_specs=(P("atom", "slab", None, None), P()),
        check_vma=False,
    )
```

```python
import functools

import jax
import jax.numpy as jnp
from jax import lax
from jax.experimental import pallas as pl
from jax.experimental.pallas import tpu as pltpu
from jax.sharding import PartitionSpec as P

BAND_MAX = 8
GROUP = 4
F32 = jnp.float32
BF16 = jnp.bfloat16
VMEM_LIMIT = 12 * 1024 * 1024


def split(value):
    high = value.astype(BF16)
    return high, (value - high.astype(F32)).astype(BF16)


def dot(a, b):
    return jnp.dot(a, b, preferred_element_type=F32)


def dot3(ah, al, bh, bl):
    return dot(ah, bh) + (dot(al, bh) + dot(ah, bl))


def peak(value):
    return jnp.max(jnp.max(value, axis=0, keepdims=True), axis=1, keepdims=True)


def rows_of(values):
    return jnp.concatenate([jnp.broadcast_to(v, (1, 128)) for v in values], axis=0)


def tables_kernel(band, kyh, kyl, kxh, kxl, *, ny):
    def entries(sq, ok):
        return jnp.where(ok, jnp.exp(sq.astype(F32) * (-2.0 / (BAND_MAX * BAND_MAX))), 0.0)

    def offsets(shape):
        return lax.broadcasted_iota(jnp.int32, shape, 0), lax.broadcasted_iota(jnp.int32, shape, 1)

    row, col = offsets(kyh.shape)
    shift = ny.bit_length() - 1
    dy = row - col
    kyh[...], kyl[...] = split(entries(dy * dy, ((row >> shift) == (col >> shift)) & (jnp.abs(dy) <= band[1])))
    row, col = offsets(kxh.shape)
    dx = row - col
    kxh[...], kxl[...] = split(entries(dx * dx, jnp.abs(dx) <= band[0]))


def tile_loop(ny, nx, step):
    across = nx // 128

    def body_of(i, carry):
        row = pl.multiple_of(lax.div(i, across) * 8, 8)
        column = pl.multiple_of(lax.rem(i, across) * 128, 128)
        step(row, pl.ds(column, 128))
        return carry

    lax.fori_loop(0, ny // 8 * across, body_of, 0)


def own_planes(lo, hi, kz, y, ny, entry_lo, entry_hi):
    side = lo.shape[0] // ny
    planes = 2 * side
    taps = [kz[d] for d in range(BAND_MAX + 1)]

    def step(row, columns):
        e = [entry_lo(lo[pl.ds(q * ny + row, 8), columns]) for q in range(side)]
        e += [entry_hi(hi[pl.ds(q * ny + row, 8), columns]) for q in range(side)]
        for p in range(planes):
            total = taps[0] * e[p]
            for d in range(1, BAND_MAX + 1):
                near = [e[q] for q in (p - d, p + d) if 0 <= q < planes]
                total += taps[d] * (near[0] if len(near) == 1 else near[0] + near[1])
            y[pl.ds(p * ny + row, 8), columns] = total

    tile_loop(ny, lo.shape[1], step)


def halo_planes(left, right, kz, y, z, ny, own, entry_left, entry_right):
    side = left.shape[0] // ny
    taps = [kz[d] for d in range(BAND_MAX + 1)]

    def step(row, columns):
        e = [entry_left(left[pl.ds(q * ny + row, 8), columns]) for q in range(side)]
        for p in range(side):
            rows = pl.ds(p * ny + row, 8)
            total = own(y[rows, columns])
            for q in range(max(0, p + side - BAND_MAX), side):
                total += taps[p + side - q] * e[q]
            z[rows, columns] = total
        e = [entry_right(right[pl.ds(q * ny + row, 8), columns]) for q in range(side)]
        for p in range(side):
            rows = pl.ds((side + p) * ny + row, 8)
            total = own(y[rows, columns])
            for q in range(min(side, p + BAND_MAX - side + 1)):
                total += taps[side + q - p] * e[q]
            z[rows, columns] = total

    tile_loop(ny, left.shape[1], step)


def tile(value):
    return jnp.broadcast_to(value, (8, 128))


def own_log_kernel(kz, lo, hi, y, stats, *, ny):
    m_lo, m_hi = peak(lo[...]), peak(hi[...])
    m = jnp.maximum(m_lo, m_hi)
    stats[...] = rows_of([m_lo, m_hi, m, m, m, m, m, m])
    m = tile(m)
    entry = lambda v: jnp.exp(v - m)
    own_planes(lo, hi, kz, y, ny, entry, entry)


def own_linear_kernel(kz, lo, hi, pot_lo, pot_hi, stats, y, shifted, *, ny):
    c = stats[0:1, 0:1]
    half = lo.shape[0]
    shifted[:half, :] = jnp.exp(pot_lo[...] - c)
    shifted[half:, :] = jnp.exp(pot_hi[...] - c)
    f_lo = tile(jnp.exp((c - stats[1:2, 0:1]) * 0.5))
    f_hi = tile(jnp.exp((c - stats[2:3, 0:1]) * 0.5))
    own_planes(lo, hi, kz, y, ny, lambda v: v * f_lo * f_lo, lambda v: v * f_hi * f_hi)


def rows_and_columns(z, g, kyh, kyl, kxh, kxl, mid):
    half, block = mid.shape[0], kyh.shape[0]
    for k in range(half // block):
        rows = pl.ds(g * half + k * block, block)
        zh, zl = split(z[rows, :])
        mid[k * block : (k + 1) * block, :] = dot3(kyh[...], kyl[...], zh, zl)
    mh, ml = split(mid[...])
    return dot3(mh, ml, kxh[...], kxl[...])


def log_halos(where, kz, left, right, y, stats, z, scale, ny):
    has_left, has_right = where[0] > 0, where[1] > 0
    m_own = stats[2:3, 0:1]
    m_left = jnp.where(has_left, peak(left[...]), m_own)
    m_right = jnp.where(has_right, peak(right[...]), m_own)
    c = jnp.maximum(m_own, jnp.maximum(m_left, m_right))
    scale[...] = rows_of([c, stats[0:1, 0:1], stats[1:2, 0:1], m_left, m_right, c, c, c])
    own = tile(jnp.exp(m_own - c))
    c = tile(c)
    halo_planes(
        left,
        right,
        kz,
        y,
        z,
        ny,
        lambda v: v * own,
        lambda v: jnp.where(has_left, jnp.exp(v - c), 0.0),
        lambda v: jnp.where(has_right, jnp.exp(v - c), 0.0),
    )


def potential_kernel(
    where, kz, left, right, y, stats, density, kyh, kyl, kxh, kxl, lo, hi, z, mid, scale, *, ny
):
    log_halos(where, kz, left, right, y, stats, z, scale, ny)
    half = mid.shape[0]
    for g, out in enumerate((lo, hi)):
        first = rows_and_columns(z, g, kyh, kyl, kxh, kxl, mid)
        out[...] = density[g * half : (g + 1) * half, :] - (jnp.log(first) + scale[0:1, 0:1])


def second_kernel(where, kz, left, right, y, stats, kyh, kyl, kxh, kxl, out, scale, z, mid, *, ny):
    log_halos(where, kz, left, right, y, stats, z, scale, ny)
    half = mid.shape[0]
    for g in range(2):
        out[g * half : (g + 1) * half, :] = rows_and_columns(z, g, kyh, kyl, kxh, kxl, mid)


def ratio_kernel(
    at, weight, second, scale, bary, cot, sum0, sum1, sum2, sum3, lo, hi, total, sums, out, sems
):
    c = scale[0:1, 0:1]
    block, columns = sums.shape[1:]
    count = sums.shape[0]
    half = out.shape[0] // 2
    arriving = [
        pltpu.make_async_copy(ref, sums.at[k], sems.at[k]) for k, ref in enumerate((sum0, sum1, sum2, sum3))
    ]
    for copy in arriving:
        copy.start()
    partial = jnp.zeros((8, 128), F32)
    f_lo = jnp.exp((scale[1:2, 0:1] - c) * 0.5)
    f_hi = jnp.exp((scale[2:3, 0:1] - c) * 0.5)
    for k, copy in enumerate(arriving):
        copy.wait()
        g = lax.rem(at[0] + k, count)
        rows = pl.ds(pl.multiple_of(g * block, block), block)
        summed = bary[rows, :] + sums[k]
        denominator = second[rows, :]
        share = summed * (jnp.log(denominator) + c)
        share = jnp.sum(share.reshape(block // 8, 8, columns), axis=0)
        for m in range(columns // 128):
            partial += share[:, m * 128 : (m + 1) * 128]
        f = jnp.where(2 * g < count, f_lo, f_hi)
        out[rows, :] = (weight[0] * summed - cot[rows, :]) / denominator * f * f
    leaving = [
        pltpu.make_async_copy(out.at[:half], lo, sems.at[0]),
        pltpu.make_async_copy(out.at[half:], hi, sems.at[1]),
    ]
    for copy in leaving:
        copy.start()
    lanes = lax.broadcasted_iota(jnp.int32, total.shape, 1)
    partial = jnp.sum(jnp.sum(partial, axis=0, keepdims=True), axis=1, keepdims=True)
    total[...] = jnp.where(lanes == at[1], partial, 0.0)
    for copy in leaving:
        copy.wait()


def gradient_kernel(
    where, kz, left, right, y, shifted, stats, kyh, kyl, kxh, kxl, out, z, mid, *, ny
):
    g = pl.program_id(0)
    c = stats[0:1, 0:1]

    @pl.when(g == 0)
    def _():
        f_left = tile(jnp.exp((c - stats[3:4, 0:1]) * 0.5))
        f_right = tile(jnp.exp((c - stats[4:5, 0:1]) * 0.5))
        has_left, has_right = where[0] > 0, where[1] > 0
        halo_planes(
            left,
            right,
            kz,
            y,
            z,
            ny,
            lambda v: v,
            lambda v: jnp.where(has_left, v * f_left * f_left, 0.0),
            lambda v: jnp.where(has_right, v * f_right * f_right, 0.0),
        )

    for step in range(2):

        @pl.when(g == step)
        def _(step=step):
            blurred = rows_and_columns(z, step, kyh, kyl, kxh, kxl, mid)
            half = out.shape[0]
            out[...] = shifted[step * half : (step + 1) * half, :] * blurred


def body(
    atom_log_density,
    prior_log_scaling,
    atom_cotangent_rows,
    barycenter_cotangent,
    weights,
    band,
    slot_atom_index,
):
    planes, ny, nx = barycenter_cotangent.shape
    slabs, atoms = lax.axis_size("slab"), lax.axis_size("atom")
    rows = planes * ny
    half = rows // 2
    block = GROUP * ny
    count = planes // GROUP
    slab_at, atom_at = lax.axis_index("slab"), lax.axis_index("atom")
    across = atoms // 2
    x_at = atom_at // 2

    smem = pl.BlockSpec(memory_space=pltpu.SMEM)
    vmem = pl.BlockSpec(memory_space=pltpu.VMEM)
    anywhere = pl.BlockSpec(memory_space=pl.ANY)
    params = pltpu.CompilerParams(vmem_limit_bytes=VMEM_LIMIT)

    def shape(*dims, dtype=F32):
        return jax.ShapeDtypeStruct(dims, dtype)

    def send(value, axis, pairs):
        return lax.ppermute(value, axis, pairs)

    in_order = lax.optimization_barrier
    to_right = [(i, i + 1) for i in range(slabs - 1)]
    to_left = [(i + 1, i) for i in range(slabs - 1)]
    ahead = {
        k: [(2 * x + z, 2 * ((x + k) % across) + z) for x in range(across) for z in range(2)]
        for k in range(1, across)
    }
    swap = [(i, i ^ 1) for i in range(atoms)]

    cot = atom_cotangent_rows.reshape(rows, nx)

    def block_of(k):
        return lax.dynamic_slice_in_dim(cot, lax.rem(x_at + k, count) * block, block)

    blocks = [block_of(k) for k in range(1, across)]
    part = block_of(0)
    for k in range(1, across):
        part = part + send(blocks[k - 1], "atom", ahead[k])

    y_shape, x_shape = (block, block), (nx, nx)
    distance = jnp.arange(BAND_MAX + 1, dtype=jnp.int32)
    kz = jnp.exp((distance * distance).astype(F32) * (-2.0 / (BAND_MAX * BAND_MAX)))
    kz = jnp.where(distance <= band[2], kz, 0.0)
    tables = pl.pallas_call(
        functools.partial(tables_kernel, ny=ny),
        out_shape=[shape(*dims, dtype=BF16) for dims in (y_shape, y_shape, x_shape, x_shape)],
        in_specs=[smem],
        out_specs=[vmem] * 4,
        compiler_params=params,
        name="tables",
    )(band)
    prior = prior_log_scaling.reshape(rows, nx)
    prior_lo, prior_hi = prior[:half], prior[half:]
    from_left = send(prior_hi, "slab", to_right)
    from_right = send(prior_lo, "slab", to_left)

    where = jnp.stack([slab_at > 0, slab_at < slabs - 1]).astype(jnp.int32)
    slot = lax.dynamic_slice_in_dim(slot_atom_index, atom_at, 1)
    onehot = (slot[0] == jnp.arange(weights.shape[0], dtype=jnp.int32)).astype(F32)
    weight = jnp.sum(onehot * weights, keepdims=True)

    own_out = [shape(rows, nx), shape(8, 128)]
    own_log = pl.pallas_call(
        functools.partial(own_log_kernel, ny=ny),
        in_specs=[smem, vmem, vmem],
        out_specs=[vmem, vmem],
        out_shape=own_out,
        compiler_params=params,
        name="own_log",
    )
    one = pl.BlockSpec((half, nx), lambda g: (g, 0))
    scratch = [pltpu.VMEM((rows, nx), F32), pltpu.VMEM((half, nx), F32)]
    scale = pltpu.VMEM((8, 128), F32)

    y, stats = own_log(kz, prior_lo, prior_hi)
    y, part = in_order((y, part))
    swapped = send(part, "atom", swap)
    pot_lo, pot_hi = pl.pallas_call(
        functools.partial(potential_kernel, ny=ny),
        in_specs=[smem, smem] + [vmem] * 9,
        out_specs=[vmem, vmem],
        out_shape=[shape(half, nx), shape(half, nx)],
        scratch_shapes=[*scratch, scale],
        compiler_params=params,
        name="potential",
    )(where, kz, from_left, from_right, y, stats, atom_log_density.reshape(rows, nx), *tables)

    from_left = send(pot_hi, "slab", to_right)
    from_right = send(pot_lo, "slab", to_left)
    both = part + swapped
    own_at, both = in_order((pot_lo, both))
    sums = [both] + [send(both, "atom", ahead[across - k]) for k in range(1, across)]
    y, stats = own_log(kz, own_at, pot_hi)
    second, stats = pl.pallas_call(
        functools.partial(second_kernel, ny=ny),
        in_specs=[smem, smem] + [vmem] * 8,
        out_specs=[vmem, vmem],
        out_shape=[shape(rows, nx), shape(8, 128)],
        scratch_shapes=scratch,
        compiler_params=params,
        name="second",
    )(where, kz, from_left, from_right, y, stats, *tables)
    ratio_lo, ratio_hi, total = pl.pallas_call(
        ratio_kernel,
        in_specs=[smem, smem] + [vmem] * 4 + [anywhere] * 4,
        out_specs=[anywhere, anywhere, vmem],
        out_shape=[shape(half, nx), shape(half, nx), shape(8, 128)],
        scratch_shapes=[
            pltpu.VMEM((count, block, nx), F32),
            pltpu.VMEM((rows, nx), F32),
            pltpu.SemaphoreType.DMA((count,)),
        ],
        compiler_params=params,
        name="ratio",
    )(
        jnp.stack([x_at, slot[0]]),
        weight,
        second,
        stats,
        barycenter_cotangent.reshape(rows, nx),
        cot,
        *sums,
    )

    from_left = send(ratio_hi, "slab", to_right)
    from_right = send(ratio_lo, "slab", to_left)
    y, shifted = pl.pallas_call(
        functools.partial(own_linear_kernel, ny=ny),
        in_specs=[smem] + [vmem] * 5,
        out_specs=[vmem, vmem],
        out_shape=[shape(rows, nx), shape(rows, nx)],
        compiler_params=params,
        name="own_linear",
    )(kz, ratio_lo, ratio_hi, pot_lo, pot_hi, stats)

    def add(value, axis, patterns):
        return sum([send(value, axis, pairs) for pairs in patterns], value)

    def flips(hop):
        return [(i, i ^ hop) for i in range(slabs)]

    value = add(total, "slab", [flips(1)])
    value = add(value, "atom", [ahead[k] for k in range(1, across)])
    value, y = in_order((value, y))
    value = add(value, "slab", [[(i, (i + k) % slabs) for i in range(slabs)] for k in (8, 16, 24)])
    for hop in (2, 4):
        value = add(value, "slab", [flips(hop)])
    value, from_left, from_right = in_order((value, from_left, from_right))
    value = add(value, "atom", [swap])
    weight_grad = value[0, : weights.shape[0]] / (rows * nx * slabs)

    gradient = pl.pallas_call(
        functools.partial(gradient_kernel, ny=ny),
        grid=(2,),
        in_specs=[smem, smem] + [vmem] * 9,
        out_specs=one,
        out_shape=shape(rows, nx),
        scratch_shapes=scratch,
        compiler_params=params,
        name="gradient",
    )(where, kz, from_left, from_right, y, shifted, stats, *tables)
    return gradient.reshape(atom_log_density.shape), weight_grad


def solution(mesh):
    return jax.shard_map(
        body,
        mesh=mesh,
        in_specs=(
            P("atom", "slab", None, None),
            P("atom", "slab", None, None),
            P("atom", "slab", None, None),
            P("slab", None, None),
            P(),
            P(),
            P(),
        ),
        out_specs=(P("atom", "slab", None, None), P()),
        check_vma=False,
    )
```

```python
import functools

import jax
import jax.numpy as jnp
from jax import lax
from jax.experimental import pallas as pl
from jax.experimental.pallas import tpu as pltpu
from jax.sharding import PartitionSpec as P

BAND_MAX = 8
GROUP = 4
F32 = jnp.float32
BF16 = jnp.bfloat16
VMEM_LIMIT = 16 * 1024 * 1024


def split(value):
    high = value.astype(BF16)
    return high, (value - high.astype(F32)).astype(BF16)


def dot(a, b):
    return jnp.dot(a, b, preferred_element_type=F32)


def dot3(ah, al, bh, bl):
    return dot(ah, bh) + (dot(al, bh) + dot(ah, bl))


def peak(value):
    return jnp.max(jnp.max(value, axis=0, keepdims=True), axis=1, keepdims=True)


def rows_of(values):
    return jnp.concatenate([jnp.broadcast_to(v, (1, 128)) for v in values], axis=0)


def tables_kernel(band, kyh, kyl, kxh, kxl, *, ny):
    def entries(sq, ok):
        return jnp.where(ok, jnp.exp(sq.astype(F32) * (-2.0 / (BAND_MAX * BAND_MAX))), 0.0)

    def offsets(shape):
        return lax.broadcasted_iota(jnp.int32, shape, 0), lax.broadcasted_iota(jnp.int32, shape, 1)

    row, col = offsets(kyh.shape)
    shift = ny.bit_length() - 1
    dy = row - col
    kyh[...], kyl[...] = split(entries(dy * dy, ((row >> shift) == (col >> shift)) & (jnp.abs(dy) <= band[1])))
    row, col = offsets(kxh.shape)
    dx = row - col
    kxh[...], kxl[...] = split(entries(dx * dx, jnp.abs(dx) <= band[0]))


def tile_loop(ny, nx, step):
    across = nx // 128

    def body_of(i, carry):
        row = pl.multiple_of(lax.div(i, across) * 8, 8)
        column = pl.multiple_of(lax.rem(i, across) * 128, 128)
        step(row, pl.ds(column, 128))
        return carry

    lax.fori_loop(0, ny // 8 * across, body_of, 0)


def own_planes(field, kz, y, ny, entry_lo, entry_hi):
    planes = field.shape[0] // ny
    taps = [kz[d] for d in range(BAND_MAX + 1)]

    def step(row, columns):
        e = [
            (entry_lo if 2 * q < planes else entry_hi)(field[pl.ds(q * ny + row, 8), columns])
            for q in range(planes)
        ]
        for p in range(planes):
            total = taps[0] * e[p]
            for d in range(1, BAND_MAX + 1):
                near = [e[q] for q in (p - d, p + d) if 0 <= q < planes]
                total += taps[d] * (near[0] if len(near) == 1 else near[0] + near[1])
            y[pl.ds(p * ny + row, 8), columns] = total

    tile_loop(ny, field.shape[1], step)


def halo_copies(near, far, halo, sems, core):
    return [
        pltpu.make_async_copy(near, halo.at[1 - core], sems.at[0]),
        pltpu.make_async_copy(far, halo.at[core], sems.at[1]),
    ]


def edge_copies(field, near, far, sems, core):
    half = near.shape[0]

    def rows(k):
        return pl.ds(pl.multiple_of(k * half, half), half)

    return [
        pltpu.make_async_copy(field.at[rows(1 - core)], near, sems.at[0]),
        pltpu.make_async_copy(field.at[rows(core)], far, sems.at[1]),
    ]


def halo_planes(halo, kz, y, z, ny, own, entry_left, entry_right):
    side = halo.shape[1] // ny
    taps = [kz[d] for d in range(BAND_MAX + 1)]

    def step(row, columns):
        e = [entry_left(halo[0, pl.ds(q * ny + row, 8), columns]) for q in range(side)]
        for p in range(side):
            rows = pl.ds(p * ny + row, 8)
            total = own(y[rows, columns])
            for q in range(max(0, p + side - BAND_MAX), side):
                total += taps[p + side - q] * e[q]
            z[rows, columns] = total
        e = [entry_right(halo[1, pl.ds(q * ny + row, 8), columns]) for q in range(side)]
        for p in range(side):
            rows = pl.ds((side + p) * ny + row, 8)
            total = own(y[rows, columns])
            for q in range(min(side, p + BAND_MAX - side + 1)):
                total += taps[side + q - p] * e[q]
            z[rows, columns] = total

    tile_loop(ny, halo.shape[2], step)


def tile(value):
    return jnp.broadcast_to(value, (8, 128))


def own_log_kernel(kz, field, y, stats, *, ny):
    half = field.shape[0] // 2
    m_lo, m_hi = peak(field[:half, :]), peak(field[half:, :])
    m = jnp.maximum(m_lo, m_hi)
    stats[...] = rows_of([m_lo, m_hi, m, m, m, m, m, m])
    m = tile(m)
    entry = lambda v: jnp.exp(v - m)
    own_planes(field, kz, y, ny, entry, entry)


def own_linear_kernel(kz, field, potential, stats, y, shifted, *, ny):
    c = stats[0:1, 0:1]
    shifted[...] = jnp.exp(potential[...] - c)
    f_lo = tile(jnp.exp((c - stats[1:2, 0:1]) * 0.5))
    f_hi = tile(jnp.exp((c - stats[2:3, 0:1]) * 0.5))
    own_planes(field, kz, y, ny, lambda v: v * f_lo * f_lo, lambda v: v * f_hi * f_hi)


def rows_and_columns(z, g, kyh, kyl, kxh, kxl, mid):
    half, block = mid.shape[0], kyh.shape[0]
    for k in range(half // block):
        rows = pl.ds(g * half + k * block, block)
        zh, zl = split(z[rows, :])
        mid[k * block : (k + 1) * block, :] = dot3(kyh[...], kyl[...], zh, zl)
    mh, ml = split(mid[...])
    return dot3(mh, ml, kxh[...], kxl[...])


def log_halos(where, kz, halo, y, stats, z, scale, ny):
    has_left, has_right = where[0] > 0, where[1] > 0
    m_own = stats[2:3, 0:1]
    m_left = jnp.where(has_left, peak(halo[0]), m_own)
    m_right = jnp.where(has_right, peak(halo[1]), m_own)
    c = jnp.maximum(m_own, jnp.maximum(m_left, m_right))
    scale[...] = rows_of([c, stats[0:1, 0:1], stats[1:2, 0:1], m_left, m_right, c, c, c])
    own = tile(jnp.exp(m_own - c))
    c = tile(c)
    halo_planes(
        halo,
        kz,
        y,
        z,
        ny,
        lambda v: v * own,
        lambda v: jnp.where(has_left, jnp.exp(v - c), 0.0),
        lambda v: jnp.where(has_right, jnp.exp(v - c), 0.0),
    )


def potential_kernel(
    where, kz, near, far, y_in, stats, density_in, kyh, kyl, kxh, kxl, potential, to_near, to_far,
    halo, y, density, z, mid, scale, sems, *, ny
):
    core = where[2]
    arriving = halo_copies(near, far, halo, sems, core)
    late = [pltpu.make_async_copy(y_in, y, sems.at[2]), pltpu.make_async_copy(density_in, density, sems.at[3])]
    for copy in arriving + late:
        copy.start()
    for copy in arriving + late[:1]:
        copy.wait()
    log_halos(where, kz, halo, y, stats, z, scale, ny)
    half = mid.shape[0]
    late[1].wait()
    for g in range(2):
        rows = slice(g * half, (g + 1) * half)
        first = rows_and_columns(z, g, kyh, kyl, kxh, kxl, mid)
        potential[rows, :] = density[rows, :] - (jnp.log(first) + scale[0:1, 0:1])
    leaving = edge_copies(potential, to_near, to_far, sems, core)
    for copy in leaving:
        copy.start()
    for copy in leaving:
        copy.wait()


def second_kernel(
    where, kz, near, far, y, stats, kyh, kyl, kxh, kxl, out, scale, halo, z, mid, sems, *, ny
):
    arriving = halo_copies(near, far, halo, sems, where[2])
    for copy in arriving:
        copy.start()
    for copy in arriving:
        copy.wait()
    log_halos(where, kz, halo, y, stats, z, scale, ny)
    half = mid.shape[0]
    for g in range(2):
        out[g * half : (g + 1) * half, :] = rows_and_columns(z, g, kyh, kyl, kxh, kxl, mid)


def ratio_kernel(
    at, weight, second, scale, bary, cot, sum0, sum1, sum2, sum3, out, to_near, to_far, total, sums, sems
):
    c = scale[0:1, 0:1]
    block, columns = sums.shape[1:]
    count = sums.shape[0]
    arriving = [
        pltpu.make_async_copy(ref, sums.at[k], sems.at[k]) for k, ref in enumerate((sum0, sum1, sum2, sum3))
    ]
    for copy in arriving:
        copy.start()
    partial = jnp.zeros((8, 128), F32)
    f_lo = jnp.exp((scale[1:2, 0:1] - c) * 0.5)
    f_hi = jnp.exp((scale[2:3, 0:1] - c) * 0.5)
    for k, copy in enumerate(arriving):
        copy.wait()
        g = lax.rem(at[0] + k, count)
        rows = pl.ds(pl.multiple_of(g * block, block), block)
        summed = bary[rows, :] + sums[k]
        denominator = second[rows, :]
        share = summed * (jnp.log(denominator) + c)
        share = jnp.sum(share.reshape(block // 8, 8, columns), axis=0)
        for m in range(columns // 128):
            partial += share[:, m * 128 : (m + 1) * 128]
        f = jnp.where(2 * g < count, f_lo, f_hi)
        out[rows, :] = (weight[0] * summed - cot[rows, :]) / denominator * f * f
    leaving = edge_copies(out, to_near, to_far, sems, at[2])
    for copy in leaving:
        copy.start()
    lanes = lax.broadcasted_iota(jnp.int32, total.shape, 1)
    partial = jnp.sum(jnp.sum(partial, axis=0, keepdims=True), axis=1, keepdims=True)
    total[...] = jnp.where(lanes == at[1], partial, 0.0)
    for copy in leaving:
        copy.wait()


def gradient_kernel(
    where, kz, near, far, y, shifted, stats, kyh, kyl, kxh, kxl, out, halo, z, mid, result, sems, *, ny
):
    arriving = halo_copies(near, far, halo, sems, where[2])
    for copy in arriving:
        copy.start()
    c = stats[0:1, 0:1]
    f_left = tile(jnp.exp((c - stats[3:4, 0:1]) * 0.5))
    f_right = tile(jnp.exp((c - stats[4:5, 0:1]) * 0.5))
    has_left, has_right = where[0] > 0, where[1] > 0
    for copy in arriving:
        copy.wait()
    halo_planes(
        halo,
        kz,
        y,
        z,
        ny,
        lambda v: v,
        lambda v: jnp.where(has_left, v * f_left * f_left, 0.0),
        lambda v: jnp.where(has_right, v * f_right * f_right, 0.0),
    )
    half = mid.shape[0]
    leaving = []
    for g in range(2):
        rows = slice(g * half, (g + 1) * half)
        result[rows, :] = shifted[rows, :] * rows_and_columns(z, g, kyh, kyl, kxh, kxl, mid)
        leaving.append(pltpu.make_async_copy(result.at[rows], out.at[rows], sems.at[g]))
        leaving[-1].start()
    for copy in leaving:
        copy.wait()


def body(
    atom_log_density,
    prior_log_scaling,
    atom_cotangent_rows,
    barycenter_cotangent,
    weights,
    band,
    slot_atom_index,
):
    planes, ny, nx = barycenter_cotangent.shape
    slabs, atoms = lax.axis_size("slab"), lax.axis_size("atom")
    rows = planes * ny
    half = rows // 2
    block = GROUP * ny
    count = planes // GROUP
    slab_at, atom_at = lax.axis_index("slab"), lax.axis_index("atom")
    across = atoms // 2
    x_at = atom_at // 2

    smem = pl.BlockSpec(memory_space=pltpu.SMEM)
    vmem = pl.BlockSpec(memory_space=pltpu.VMEM)
    anywhere = pl.BlockSpec(memory_space=pl.ANY)
    hbm = pl.BlockSpec(memory_space=pltpu.HBM)
    params = pltpu.CompilerParams(vmem_limit_bytes=VMEM_LIMIT)

    def shape(*dims, dtype=F32):
        return jax.ShapeDtypeStruct(dims, dtype)

    def send(value, axis, pairs):
        return lax.ppermute(value, axis, pairs)

    in_order = lax.optimization_barrier
    cores = [(i, i ^ 1) for i in range(slabs)]
    chips = [(i, i + 1) for i in range(1, slabs - 1, 2)] + [(i + 1, i) for i in range(1, slabs - 1, 2)]
    core = slab_at % 2
    ahead = {
        k: [(2 * x + z, 2 * ((x + k) % across) + z) for x in range(across) for z in range(2)]
        for k in range(1, across)
    }
    swap = [(i, i ^ 1) for i in range(atoms)]

    cot = atom_cotangent_rows.reshape(rows, nx)

    def block_of(k):
        return lax.dynamic_slice_in_dim(cot, lax.rem(x_at + k, count) * block, block)

    blocks = [block_of(k) for k in range(1, across)]
    part = block_of(0)
    for k in range(1, across):
        part = part + send(blocks[k - 1], "atom", ahead[k])

    y_shape, x_shape = (block, block), (nx, nx)
    distance = jnp.arange(BAND_MAX + 1, dtype=jnp.int32)
    kz = jnp.exp((distance * distance).astype(F32) * (-2.0 / (BAND_MAX * BAND_MAX)))
    kz = jnp.where(distance <= band[2], kz, 0.0)
    tables = pl.pallas_call(
        functools.partial(tables_kernel, ny=ny),
        out_shape=[shape(*dims, dtype=BF16) for dims in (y_shape, y_shape, x_shape, x_shape)],
        in_specs=[smem],
        out_specs=[vmem] * 4,
        compiler_params=params,
        name="tables",
    )(band)
    prior = prior_log_scaling.reshape(rows, nx)
    to_near = lax.dynamic_slice_in_dim(prior, (1 - core) * half, half)
    to_far = lax.dynamic_slice_in_dim(prior, core * half, half)
    far = send(to_far, "slab", chips)
    near = send(to_near, "slab", cores)

    where = jnp.stack([slab_at > 0, slab_at < slabs - 1, core > 0]).astype(jnp.int32)
    slot = lax.dynamic_slice_in_dim(slot_atom_index, atom_at, 1)
    onehot = (slot[0] == jnp.arange(weights.shape[0], dtype=jnp.int32)).astype(F32)
    weight = jnp.sum(onehot * weights, keepdims=True)

    own_out = [shape(rows, nx), shape(8, 128)]
    own_log = pl.pallas_call(
        functools.partial(own_log_kernel, ny=ny),
        in_specs=[smem, vmem],
        out_specs=[vmem, vmem],
        out_shape=own_out,
        compiler_params=params,
        name="own_log",
    )
    whole, halo = pltpu.VMEM((rows, nx), F32), pltpu.VMEM((2, half, nx), F32)
    scratch = [pltpu.VMEM((rows, nx), F32), pltpu.VMEM((half, nx), F32)]
    scale = pltpu.VMEM((8, 128), F32)

    y, stats = own_log(kz, prior)
    y, part = in_order((y, part))
    swapped = send(part, "atom", swap)
    potential, to_near, to_far = pl.pallas_call(
        functools.partial(potential_kernel, ny=ny),
        in_specs=[smem, smem, hbm, hbm, hbm, vmem, hbm] + [vmem] * 4,
        out_specs=[vmem, anywhere, anywhere],
        out_shape=[shape(rows, nx), shape(half, nx), shape(half, nx)],
        scratch_shapes=[halo, whole, whole, *scratch, scale, pltpu.SemaphoreType.DMA((4,))],
        compiler_params=params,
        name="potential",
    )(where, kz, near, far, y, stats, atom_log_density.reshape(rows, nx), *tables)

    far = send(to_far, "slab", chips)
    near = send(to_near, "slab", cores)
    both = part + swapped
    own_at, both = in_order((potential, both))
    sums = [both] + [send(both, "atom", ahead[across - k]) for k in range(1, across)]
    y, stats = own_log(kz, own_at)
    second, stats = pl.pallas_call(
        functools.partial(second_kernel, ny=ny),
        in_specs=[smem, smem, anywhere, anywhere] + [vmem] * 6,
        out_specs=[vmem, vmem],
        out_shape=[shape(rows, nx), shape(8, 128)],
        scratch_shapes=[halo, *scratch, pltpu.SemaphoreType.DMA((2,))],
        compiler_params=params,
        name="second",
    )(where, kz, near, far, y, stats, *tables)
    ratio, to_near, to_far, total = pl.pallas_call(
        ratio_kernel,
        in_specs=[smem, smem] + [vmem] * 4 + [anywhere] * 4,
        out_specs=[vmem, anywhere, anywhere, vmem],
        out_shape=[shape(rows, nx), shape(half, nx), shape(half, nx), shape(8, 128)],
        scratch_shapes=[
            pltpu.VMEM((count, block, nx), F32),
            pltpu.SemaphoreType.DMA((count,)),
        ],
        compiler_params=params,
        name="ratio",
    )(
        jnp.stack([x_at, slot[0], core]),
        weight,
        second,
        stats,
        barycenter_cotangent.reshape(rows, nx),
        cot,
        *sums,
    )

    far = send(to_far, "slab", chips)
    near = send(to_near, "slab", cores)
    y, shifted = pl.pallas_call(
        functools.partial(own_linear_kernel, ny=ny),
        in_specs=[smem] + [vmem] * 3,
        out_specs=[vmem, vmem],
        out_shape=[shape(rows, nx), shape(rows, nx)],
        compiler_params=params,
        name="own_linear",
    )(kz, ratio, potential, stats)

    def add(value, axis, patterns):
        return sum([send(value, axis, pairs) for pairs in patterns], value)

    def flips(hop):
        return [(i, i ^ hop) for i in range(slabs)]

    value = add(total, "slab", [cores])
    value = add(value, "atom", [ahead[k] for k in range(1, across)])
    value, y = in_order((value, y))
    value = add(value, "slab", [[(i, (i + k) % slabs) for i in range(slabs)] for k in (8, 16, 24)])
    for hop in (2, 4):
        value = add(value, "slab", [flips(hop)])
    value, near, far = in_order((value, near, far))
    value = add(value, "atom", [swap])
    weight_grad = value[0, : weights.shape[0]] / (rows * nx * slabs)

    gradient = pl.pallas_call(
        functools.partial(gradient_kernel, ny=ny),
        in_specs=[smem, smem, anywhere, anywhere] + [vmem] * 7,
        out_specs=anywhere,
        out_shape=shape(rows, nx),
        scratch_shapes=[halo, *scratch, whole, pltpu.SemaphoreType.DMA((2,))],
        compiler_params=params,
        name="gradient",
    )(where, kz, near, far, y, shifted, stats, *tables)
    return gradient.reshape(atom_log_density.shape), weight_grad


def solution(mesh):
    return jax.shard_map(
        body,
        mesh=mesh,
        in_specs=(
            P("atom", "slab", None, None),
            P("atom", "slab", None, None),
            P("atom", "slab", None, None),
            P("slab", None, None),
            P(),
            P(),
            P(),
        ),
        out_specs=(P("atom", "slab", None, None), P()),
        check_vma=False,
    )
```

```python
import functools

import jax
import jax.numpy as jnp
from jax import lax
from jax.experimental import pallas as pl
from jax.experimental.pallas import tpu as pltpu
from jax.sharding import PartitionSpec as P

BAND_MAX = 8
GROUP = 4
F32 = jnp.float32
BF16 = jnp.bfloat16
VMEM_LIMIT = 16 * 1024 * 1024


def split(value):
    high = value.astype(BF16)
    return high, (value - high.astype(F32)).astype(BF16)


def dot(a, b):
    return jnp.dot(a, b, preferred_element_type=F32)


def dot3(ah, al, bh, bl):
    return dot(ah, bh) + (dot(al, bh) + dot(ah, bl))


def peak(value):
    return jnp.max(jnp.max(value, axis=0, keepdims=True), axis=1, keepdims=True)


def rows_of(values):
    return jnp.concatenate([jnp.broadcast_to(v, (1, 128)) for v in values], axis=0)


def tables_kernel(band, kyh, kyl, kxh, kxl, *, ny):
    def entries(sq, ok):
        return jnp.where(ok, jnp.exp(sq.astype(F32) * (-2.0 / (BAND_MAX * BAND_MAX))), 0.0)

    def offsets(shape):
        return lax.broadcasted_iota(jnp.int32, shape, 0), lax.broadcasted_iota(jnp.int32, shape, 1)

    row, col = offsets(kyh.shape)
    shift = ny.bit_length() - 1
    dy = row - col
    kyh[...], kyl[...] = split(entries(dy * dy, ((row >> shift) == (col >> shift)) & (jnp.abs(dy) <= band[1])))
    row, col = offsets(kxh.shape)
    dx = row - col
    kxh[...], kxl[...] = split(entries(dx * dx, jnp.abs(dx) <= band[0]))


def tile_loop(ny, nx, step):
    across = nx // 128

    def body_of(i, carry):
        row = pl.multiple_of(lax.div(i, across) * 8, 8)
        column = pl.multiple_of(lax.rem(i, across) * 128, 128)
        step(row, pl.ds(column, 128))
        return carry

    lax.fori_loop(0, ny // 8 * across, body_of, 0)


def own_planes(field, kz, y, ny, entry_lo, entry_hi):
    planes = field.shape[0] // ny
    taps = [kz[d] for d in range(BAND_MAX + 1)]

    def step(row, columns):
        e = [
            (entry_lo if 2 * q < planes else entry_hi)(field[pl.ds(q * ny + row, 8), columns])
            for q in range(planes)
        ]
        for p in range(planes):
            total = taps[0] * e[p]
            for d in range(1, BAND_MAX + 1):
                near = [e[q] for q in (p - d, p + d) if 0 <= q < planes]
                total += taps[d] * (near[0] if len(near) == 1 else near[0] + near[1])
            y[pl.ds(p * ny + row, 8), columns] = total

    tile_loop(ny, field.shape[1], step)


def halo_copies(near, far, halo, sems, core):
    return [
        pltpu.make_async_copy(near, halo.at[1 - core], sems.at[0]),
        pltpu.make_async_copy(far, halo.at[core], sems.at[1]),
    ]


def edge_copies(field, near, far, sems, core):
    half = near.shape[0]

    def rows(k):
        return pl.ds(pl.multiple_of(k * half, half), half)

    return [
        pltpu.make_async_copy(field.at[rows(1 - core)], near, sems.at[0]),
        pltpu.make_async_copy(field.at[rows(core)], far, sems.at[1]),
    ]


def halo_planes(halo, kz, y, z, ny, own, entry_left, entry_right):
    side = halo.shape[1] // ny
    taps = [kz[d] for d in range(BAND_MAX + 1)]

    def step(row, columns):
        e = [entry_left(halo[0, pl.ds(q * ny + row, 8), columns]) for q in range(side)]
        for p in range(side):
            rows = pl.ds(p * ny + row, 8)
            total = own(y[rows, columns])
            for q in range(max(0, p + side - BAND_MAX), side):
                total += taps[p + side - q] * e[q]
            z[rows, columns] = total
        e = [entry_right(halo[1, pl.ds(q * ny + row, 8), columns]) for q in range(side)]
        for p in range(side):
            rows = pl.ds((side + p) * ny + row, 8)
            total = own(y[rows, columns])
            for q in range(min(side, p + BAND_MAX - side + 1)):
                total += taps[side + q - p] * e[q]
            z[rows, columns] = total

    tile_loop(ny, halo.shape[2], step)


def tile(value):
    return jnp.broadcast_to(value, (8, 128))


def own_log_kernel(kz, field, y, stats, *, ny):
    half = field.shape[0] // 2
    m_lo, m_hi = peak(field[:half, :]), peak(field[half:, :])
    m = jnp.maximum(m_lo, m_hi)
    stats[...] = rows_of([m_lo, m_hi, m, m, m, m, m, m])
    m = tile(m)
    entry = lambda v: jnp.exp(v - m)
    own_planes(field, kz, y, ny, entry, entry)


def own_linear_kernel(kz, field, potential, stats, y, shifted, *, ny):
    c = stats[0:1, 0:1]
    shifted[...] = jnp.exp(potential[...] - c)
    f_lo = tile(jnp.exp((c - stats[1:2, 0:1]) * 0.5))
    f_hi = tile(jnp.exp((c - stats[2:3, 0:1]) * 0.5))
    own_planes(field, kz, y, ny, lambda v: v * f_lo * f_lo, lambda v: v * f_hi * f_hi)


def rows_and_columns(z, g, kyh, kyl, kxh, kxl, mid):
    half, block = mid.shape[0], kyh.shape[0]
    for k in range(half // block):
        rows = pl.ds(g * half + k * block, block)
        zh, zl = split(z[rows, :])
        mid[k * block : (k + 1) * block, :] = dot3(kyh[...], kyl[...], zh, zl)
    mh, ml = split(mid[...])
    return dot3(mh, ml, kxh[...], kxl[...])


def log_halos(where, kz, halo, y, stats, z, scale, ny):
    has_left, has_right = where[0] > 0, where[1] > 0
    m_own = stats[2:3, 0:1]
    m_left = jnp.where(has_left, peak(halo[0]), m_own)
    m_right = jnp.where(has_right, peak(halo[1]), m_own)
    c = jnp.maximum(m_own, jnp.maximum(m_left, m_right))
    scale[...] = rows_of([c, stats[0:1, 0:1], stats[1:2, 0:1], m_left, m_right, c, c, c])
    own = tile(jnp.exp(m_own - c))
    c = tile(c)
    halo_planes(
        halo,
        kz,
        y,
        z,
        ny,
        lambda v: v * own,
        lambda v: jnp.where(has_left, jnp.exp(v - c), 0.0),
        lambda v: jnp.where(has_right, jnp.exp(v - c), 0.0),
    )


def potential_kernel(
    where, kz, near, far, y_in, stats, density_in, kyh, kyl, kxh, kxl, potential, to_near, to_far,
    halo, y, density, z, mid, scale, sems, *, ny
):
    core = where[2]
    arriving = halo_copies(near, far, halo, sems, core)
    late = [pltpu.make_async_copy(y_in, y, sems.at[2]), pltpu.make_async_copy(density_in, density, sems.at[3])]
    for copy in arriving + late:
        copy.start()
    for copy in arriving + late[:1]:
        copy.wait()
    log_halos(where, kz, halo, y, stats, z, scale, ny)
    half = mid.shape[0]
    late[1].wait()
    for g in range(2):
        rows = slice(g * half, (g + 1) * half)
        first = rows_and_columns(z, g, kyh, kyl, kxh, kxl, mid)
        potential[rows, :] = density[rows, :] - (jnp.log(first) + scale[0:1, 0:1])
    leaving = edge_copies(potential, to_near, to_far, sems, core)
    for copy in leaving:
        copy.start()
    for copy in leaving:
        copy.wait()


def second_kernel(
    where, kz, near, far, y, stats, kyh, kyl, kxh, kxl, out, scale, halo, z, mid, sems, *, ny
):
    arriving = halo_copies(near, far, halo, sems, where[2])
    for copy in arriving:
        copy.start()
    for copy in arriving:
        copy.wait()
    log_halos(where, kz, halo, y, stats, z, scale, ny)
    half = mid.shape[0]
    for g in range(2):
        out[g * half : (g + 1) * half, :] = rows_and_columns(z, g, kyh, kyl, kxh, kxl, mid)


def ratio_kernel(
    at, weight, second, scale, bary, cot, sum0, sum1, sum2, sum3, out, to_near, to_far, total, sums, sems
):
    c = scale[0:1, 0:1]
    block, columns = sums.shape[1:]
    count = sums.shape[0]
    arriving = [
        pltpu.make_async_copy(ref, sums.at[k], sems.at[k]) for k, ref in enumerate((sum0, sum1, sum2, sum3))
    ]
    for copy in arriving:
        copy.start()
    partial = jnp.zeros((8, 128), F32)
    f_lo = jnp.exp((scale[1:2, 0:1] - c) * 0.5)
    f_hi = jnp.exp((scale[2:3, 0:1] - c) * 0.5)
    for k, copy in enumerate(arriving):
        copy.wait()
        g = lax.rem(at[0] + k, count)
        rows = pl.ds(pl.multiple_of(g * block, block), block)
        summed = bary[rows, :] + sums[k]
        denominator = second[rows, :]
        share = summed * (jnp.log(denominator) + c)
        share = jnp.sum(share.reshape(block // 8, 8, columns), axis=0)
        for m in range(columns // 128):
            partial += share[:, m * 128 : (m + 1) * 128]
        f = jnp.where(2 * g < count, f_lo, f_hi)
        out[rows, :] = (weight[0] * summed - cot[rows, :]) / denominator * f * f
    leaving = edge_copies(out, to_near, to_far, sems, at[2])
    for copy in leaving:
        copy.start()
    lanes = lax.broadcasted_iota(jnp.int32, total.shape, 1)
    partial = jnp.sum(jnp.sum(partial, axis=0, keepdims=True), axis=1, keepdims=True)
    total[...] = jnp.where(lanes == at[1], partial, 0.0)
    for copy in leaving:
        copy.wait()


def gradient_kernel(
    where, kz, near, far, y, shifted, stats, kyh, kyl, kxh, kxl, out, halo, z, mid, result, sems, *, ny
):
    arriving = halo_copies(near, far, halo, sems, where[2])
    for copy in arriving:
        copy.start()
    c = stats[0:1, 0:1]
    f_left = tile(jnp.exp((c - stats[3:4, 0:1]) * 0.5))
    f_right = tile(jnp.exp((c - stats[4:5, 0:1]) * 0.5))
    has_left, has_right = where[0] > 0, where[1] > 0
    for copy in arriving:
        copy.wait()
    halo_planes(
        halo,
        kz,
        y,
        z,
        ny,
        lambda v: v,
        lambda v: jnp.where(has_left, v * f_left * f_left, 0.0),
        lambda v: jnp.where(has_right, v * f_right * f_right, 0.0),
    )
    half = mid.shape[0]
    leaving = []
    for g in range(2):
        rows = slice(g * half, (g + 1) * half)
        result[rows, :] = shifted[rows, :] * rows_and_columns(z, g, kyh, kyl, kxh, kxl, mid)
        leaving.append(pltpu.make_async_copy(result.at[rows], out.at[rows], sems.at[g]))
        leaving[-1].start()
    for copy in leaving:
        copy.wait()


def body(
    atom_log_density,
    prior_log_scaling,
    atom_cotangent_rows,
    barycenter_cotangent,
    weights,
    band,
    slot_atom_index,
):
    planes, ny, nx = barycenter_cotangent.shape
    slabs, atoms = lax.axis_size("slab"), lax.axis_size("atom")
    rows = planes * ny
    half = rows // 2
    block = GROUP * ny
    count = planes // GROUP
    slab_at, atom_at = lax.axis_index("slab"), lax.axis_index("atom")
    across = atoms // 2
    x_at = atom_at // 2

    smem = pl.BlockSpec(memory_space=pltpu.SMEM)
    vmem = pl.BlockSpec(memory_space=pltpu.VMEM)
    anywhere = pl.BlockSpec(memory_space=pl.ANY)
    hbm = pl.BlockSpec(memory_space=pltpu.HBM)
    params = pltpu.CompilerParams(vmem_limit_bytes=VMEM_LIMIT)

    def shape(*dims, dtype=F32):
        return jax.ShapeDtypeStruct(dims, dtype)

    def send(value, axis, pairs):
        return lax.ppermute(value, axis, pairs)

    in_order = lax.optimization_barrier
    cores = [(i, i ^ 1) for i in range(slabs)]
    chips = [(i, i + 1) for i in range(1, slabs - 1, 2)] + [(i + 1, i) for i in range(1, slabs - 1, 2)]
    core = slab_at % 2
    ahead = {
        k: [(2 * x + z, 2 * ((x + k) % across) + z) for x in range(across) for z in range(2)]
        for k in range(1, across)
    }
    swap = [(i, i ^ 1) for i in range(atoms)]

    cot = atom_cotangent_rows.reshape(rows, nx)

    def block_of(k):
        return lax.dynamic_slice_in_dim(cot, lax.rem(x_at + k, count) * block, block)

    blocks = [block_of(k) for k in range(1, across)]
    part = block_of(0)
    for k in range(1, across):
        part = part + send(blocks[k - 1], "atom", ahead[k])

    y_shape, x_shape = (block, block), (nx, nx)
    distance = jnp.arange(BAND_MAX + 1, dtype=jnp.int32)
    kz = jnp.exp((distance * distance).astype(F32) * (-2.0 / (BAND_MAX * BAND_MAX)))
    kz = jnp.where(distance <= band[2], kz, 0.0)
    tables = pl.pallas_call(
        functools.partial(tables_kernel, ny=ny),
        out_shape=[shape(*dims, dtype=BF16) for dims in (y_shape, y_shape, x_shape, x_shape)],
        in_specs=[smem],
        out_specs=[vmem] * 4,
        compiler_params=params,
        name="tables",
    )(band)
    prior = prior_log_scaling.reshape(rows, nx)
    to_near = lax.dynamic_slice_in_dim(prior, (1 - core) * half, half)
    to_far = lax.dynamic_slice_in_dim(prior, core * half, half)
    far = send(to_far, "slab", chips)
    near = send(to_near, "slab", cores)

    where = jnp.stack([slab_at > 0, slab_at < slabs - 1, core > 0]).astype(jnp.int32)
    slot = lax.dynamic_slice_in_dim(slot_atom_index, atom_at, 1)
    onehot = (slot[0] == jnp.arange(weights.shape[0], dtype=jnp.int32)).astype(F32)
    weight = jnp.sum(onehot * weights, keepdims=True)

    own_out = [shape(rows, nx), shape(8, 128)]
    own_log = pl.pallas_call(
        functools.partial(own_log_kernel, ny=ny),
        in_specs=[smem, vmem],
        out_specs=[vmem, vmem],
        out_shape=own_out,
        compiler_params=params,
        name="own_log",
    )
    whole, halo = pltpu.VMEM((rows, nx), F32), pltpu.VMEM((2, half, nx), F32)
    scratch = [pltpu.VMEM((rows, nx), F32), pltpu.VMEM((half, nx), F32)]
    scale = pltpu.VMEM((8, 128), F32)

    y, stats = own_log(kz, prior)
    one, two = block * 32 // 256, block * 96 // 256
    swapped = [send(part[:one], "atom", swap)]
    following, swapped[0] = in_order((part[one:two], swapped[0]))
    swapped += [send(following, "atom", swap), send(part[two:], "atom", swap)]
    y, swapped[1] = in_order((y, swapped[1]))
    swapped = jnp.concatenate(swapped)
    potential, to_near, to_far = pl.pallas_call(
        functools.partial(potential_kernel, ny=ny),
        in_specs=[smem, smem, hbm, hbm, hbm, vmem, hbm] + [vmem] * 4,
        out_specs=[vmem, anywhere, anywhere],
        out_shape=[shape(rows, nx), shape(half, nx), shape(half, nx)],
        scratch_shapes=[halo, whole, whole, *scratch, scale, pltpu.SemaphoreType.DMA((4,))],
        compiler_params=params,
        name="potential",
    )(where, kz, near, far, y, stats, atom_log_density.reshape(rows, nx), *tables)

    far = send(to_far, "slab", chips)
    near = send(to_near, "slab", cores)
    both = part + swapped
    own_at, both = in_order((potential, both))
    sums = [both] + [send(both, "atom", ahead[across - k]) for k in range(1, across)]
    y, stats = own_log(kz, own_at)
    second, stats = pl.pallas_call(
        functools.partial(second_kernel, ny=ny),
        in_specs=[smem, smem, anywhere, anywhere] + [vmem] * 6,
        out_specs=[vmem, vmem],
        out_shape=[shape(rows, nx), shape(8, 128)],
        scratch_shapes=[halo, *scratch, pltpu.SemaphoreType.DMA((2,))],
        compiler_params=params,
        name="second",
    )(where, kz, near, far, y, stats, *tables)
    ratio, to_near, to_far, total = pl.pallas_call(
        ratio_kernel,
        in_specs=[smem, smem] + [vmem] * 4 + [anywhere] * 4,
        out_specs=[vmem, anywhere, anywhere, vmem],
        out_shape=[shape(rows, nx), shape(half, nx), shape(half, nx), shape(8, 128)],
        scratch_shapes=[
            pltpu.VMEM((count, block, nx), F32),
            pltpu.SemaphoreType.DMA((count,)),
        ],
        compiler_params=params,
        name="ratio",
    )(
        jnp.stack([x_at, slot[0], core]),
        weight,
        second,
        stats,
        barycenter_cotangent.reshape(rows, nx),
        cot,
        *sums,
    )

    far = send(to_far, "slab", chips)
    near = send(to_near, "slab", cores)
    y, shifted = pl.pallas_call(
        functools.partial(own_linear_kernel, ny=ny),
        in_specs=[smem] + [vmem] * 3,
        out_specs=[vmem, vmem],
        out_shape=[shape(rows, nx), shape(rows, nx)],
        compiler_params=params,
        name="own_linear",
    )(kz, ratio, potential, stats)

    def add(value, axis, patterns):
        return sum([send(value, axis, pairs) for pairs in patterns], value)

    def flips(hop):
        return [(i, i ^ hop) for i in range(slabs)]

    value = add(total, "slab", [cores])
    value = add(value, "atom", [ahead[k] for k in range(1, across)])
    value, y = in_order((value, y))
    value = add(value, "slab", [[(i, (i + k) % slabs) for i in range(slabs)] for k in (8, 16, 24)])
    for hop in (2, 4):
        value = add(value, "slab", [flips(hop)])
    value, near, far = in_order((value, near, far))
    value = add(value, "atom", [swap])
    weight_grad = value[0, : weights.shape[0]] / (rows * nx * slabs)

    gradient = pl.pallas_call(
        functools.partial(gradient_kernel, ny=ny),
        in_specs=[smem, smem, anywhere, anywhere] + [vmem] * 7,
        out_specs=anywhere,
        out_shape=shape(rows, nx),
        scratch_shapes=[halo, *scratch, whole, pltpu.SemaphoreType.DMA((2,))],
        compiler_params=params,
        name="gradient",
    )(where, kz, near, far, y, shifted, stats, *tables)
    return gradient.reshape(atom_log_density.shape), weight_grad


def solution(mesh):
    return jax.shard_map(
        body,
        mesh=mesh,
        in_specs=(
            P("atom", "slab", None, None),
            P("atom", "slab", None, None),
            P("atom", "slab", None, None),
            P("slab", None, None),
            P(),
            P(),
            P(),
        ),
        out_specs=(P("atom", "slab", None, None), P()),
        check_vma=False,
    )
```

```python
import functools

import jax
import jax.numpy as jnp
from jax import lax
from jax.experimental import pallas as pl
from jax.experimental.pallas import tpu as pltpu
from jax.sharding import PartitionSpec as P

BAND_MAX = 8
GROUP = 4
F32 = jnp.float32
BF16 = jnp.bfloat16
VMEM_LIMIT = 16 * 1024 * 1024


def split(value):
    high = value.astype(BF16)
    return high, (value - high.astype(F32)).astype(BF16)


def dot(a, b):
    return jnp.dot(a, b, preferred_element_type=F32)


def dot3(ah, al, bh, bl):
    return dot(ah, bh) + (dot(al, bh) + dot(ah, bl))


def peak(value):
    return jnp.max(jnp.max(value, axis=0, keepdims=True), axis=1, keepdims=True)


def rows_of(values):
    return jnp.concatenate([jnp.broadcast_to(v, (1, 128)) for v in values], axis=0)


def tables_kernel(band, kyh, kyl, kxh, kxl, *, ny):
    def entries(sq, ok):
        return jnp.where(ok, jnp.exp(sq.astype(F32) * (-2.0 / (BAND_MAX * BAND_MAX))), 0.0)

    def offsets(shape):
        return lax.broadcasted_iota(jnp.int32, shape, 0), lax.broadcasted_iota(jnp.int32, shape, 1)

    row, col = offsets(kyh.shape)
    shift = ny.bit_length() - 1
    dy = row - col
    kyh[...], kyl[...] = split(entries(dy * dy, ((row >> shift) == (col >> shift)) & (jnp.abs(dy) <= band[1])))
    row, col = offsets(kxh.shape)
    dx = row - col
    kxh[...], kxl[...] = split(entries(dx * dx, jnp.abs(dx) <= band[0]))


def tile_loop(ny, nx, step):
    across = nx // 128

    def body_of(i, carry):
        row = pl.multiple_of(lax.div(i, across) * 8, 8)
        column = pl.multiple_of(lax.rem(i, across) * 128, 128)
        step(row, pl.ds(column, 128))
        return carry

    lax.fori_loop(0, ny // 8 * across, body_of, 0)


def own_planes(field, kz, y, ny, entry_lo, entry_hi):
    planes = field.shape[0] // ny
    taps = [kz[d] for d in range(BAND_MAX + 1)]

    def step(row, columns):
        e = [
            (entry_lo if 2 * q < planes else entry_hi)(field[pl.ds(q * ny + row, 8), columns])
            for q in range(planes)
        ]
        for p in range(planes):
            total = taps[0] * e[p]
            for d in range(1, BAND_MAX + 1):
                near = [e[q] for q in (p - d, p + d) if 0 <= q < planes]
                total += taps[d] * (near[0] if len(near) == 1 else near[0] + near[1])
            y[pl.ds(p * ny + row, 8), columns] = total

    tile_loop(ny, field.shape[1], step)


def halo_copies(near, far, halo, sems, core):
    return [
        pltpu.make_async_copy(near, halo.at[1 - core], sems.at[0]),
        pltpu.make_async_copy(far, halo.at[core], sems.at[1]),
    ]


def edge_copies(field, near, far, sems, core):
    half = near.shape[0]

    def rows(k):
        return pl.ds(pl.multiple_of(k * half, half), half)

    return [
        pltpu.make_async_copy(field.at[rows(1 - core)], near, sems.at[0]),
        pltpu.make_async_copy(field.at[rows(core)], far, sems.at[1]),
    ]


def halo_planes(halo, kz, y, z, ny, own, entry_left, entry_right):
    side = halo.shape[1] // ny
    taps = [kz[d] for d in range(BAND_MAX + 1)]

    def step(row, columns):
        e = [entry_left(halo[0, pl.ds(q * ny + row, 8), columns]) for q in range(side)]
        for p in range(side):
            rows = pl.ds(p * ny + row, 8)
            total = own(y[rows, columns])
            for q in range(max(0, p + side - BAND_MAX), side):
                total += taps[p + side - q] * e[q]
            z[rows, columns] = total
        e = [entry_right(halo[1, pl.ds(q * ny + row, 8), columns]) for q in range(side)]
        for p in range(side):
            rows = pl.ds((side + p) * ny + row, 8)
            total = own(y[rows, columns])
            for q in range(min(side, p + BAND_MAX - side + 1)):
                total += taps[side + q - p] * e[q]
            z[rows, columns] = total

    tile_loop(ny, halo.shape[2], step)


def tile(value):
    return jnp.broadcast_to(value, (8, 128))


def own_log_kernel(kz, field, y, stats, *, ny):
    half = field.shape[0] // 2
    m_lo, m_hi = peak(field[:half, :]), peak(field[half:, :])
    m = jnp.maximum(m_lo, m_hi)
    stats[...] = rows_of([m_lo, m_hi, m, m, m, m, m, m])
    m = tile(m)
    entry = lambda v: jnp.exp(v - m)
    own_planes(field, kz, y, ny, entry, entry)


def own_linear_kernel(kz, field, potential, stats, y, shifted, *, ny):
    c = stats[0:1, 0:1]
    shifted[...] = jnp.exp(potential[...] - c)
    f_lo = tile(jnp.exp((c - stats[1:2, 0:1]) * 0.5))
    f_hi = tile(jnp.exp((c - stats[2:3, 0:1]) * 0.5))
    own_planes(field, kz, y, ny, lambda v: v * f_lo * f_lo, lambda v: v * f_hi * f_hi)


def rows_and_columns(z, g, kyh, kyl, kxh, kxl, mid):
    half, block = mid.shape[0], kyh.shape[0]
    for k in range(half // block):
        rows = pl.ds(g * half + k * block, block)
        zh, zl = split(z[rows, :])
        mid[k * block : (k + 1) * block, :] = dot3(kyh[...], kyl[...], zh, zl)
    mh, ml = split(mid[...])
    return dot3(mh, ml, kxh[...], kxl[...])


def log_halos(where, kz, halo, y, stats, z, scale, ny):
    has_left, has_right = where[0] > 0, where[1] > 0
    m_own = stats[2:3, 0:1]
    m_left = jnp.where(has_left, peak(halo[0]), m_own)
    m_right = jnp.where(has_right, peak(halo[1]), m_own)
    c = jnp.maximum(m_own, jnp.maximum(m_left, m_right))
    scale[...] = rows_of([c, stats[0:1, 0:1], stats[1:2, 0:1], m_left, m_right, c, c, c])
    own = tile(jnp.exp(m_own - c))
    c = tile(c)
    halo_planes(
        halo,
        kz,
        y,
        z,
        ny,
        lambda v: v * own,
        lambda v: jnp.where(has_left, jnp.exp(v - c), 0.0),
        lambda v: jnp.where(has_right, jnp.exp(v - c), 0.0),
    )


def potential_kernel(
    where, kz, near, far, more, y_in, stats, density_in, kyh, kyl, kxh, kxl, potential, to_near, to_far,
    halo, y, density, z, mid, scale, sems, *, ny
):
    core = where[2]
    piece = far.shape[0]
    arriving = [
        pltpu.make_async_copy(near, halo.at[1 - core], sems.at[0]),
        pltpu.make_async_copy(far, halo.at[core, pl.ds(0, piece)], sems.at[1]),
        pltpu.make_async_copy(more, halo.at[core, pl.ds(piece, piece)], sems.at[4]),
    ]
    late = [pltpu.make_async_copy(y_in, y, sems.at[2]), pltpu.make_async_copy(density_in, density, sems.at[3])]
    for copy in arriving + late:
        copy.start()
    for copy in arriving + late[:1]:
        copy.wait()
    log_halos(where, kz, halo, y, stats, z, scale, ny)
    half = mid.shape[0]
    late[1].wait()
    for g in range(2):
        rows = slice(g * half, (g + 1) * half)
        first = rows_and_columns(z, g, kyh, kyl, kxh, kxl, mid)
        potential[rows, :] = density[rows, :] - (jnp.log(first) + scale[0:1, 0:1])
    leaving = edge_copies(potential, to_near, to_far, sems, core)
    for copy in leaving:
        copy.start()
    for copy in leaving:
        copy.wait()


def second_kernel(
    where, kz, near, far, y, stats, kyh, kyl, kxh, kxl, out, scale, halo, z, mid, sems, *, ny
):
    arriving = halo_copies(near, far, halo, sems, where[2])
    for copy in arriving:
        copy.start()
    for copy in arriving:
        copy.wait()
    log_halos(where, kz, halo, y, stats, z, scale, ny)
    half = mid.shape[0]
    for g in range(2):
        out[g * half : (g + 1) * half, :] = rows_and_columns(z, g, kyh, kyl, kxh, kxl, mid)


def ratio_kernel(
    at, weight, second, scale, bary, cot, sum0, sum1, sum2, sum3, out, to_near, to_far, total, sums, sems
):
    c = scale[0:1, 0:1]
    block, columns = sums.shape[1:]
    count = sums.shape[0]
    arriving = [
        pltpu.make_async_copy(ref, sums.at[k], sems.at[k]) for k, ref in enumerate((sum0, sum1, sum2, sum3))
    ]
    for copy in arriving:
        copy.start()
    partial = jnp.zeros((8, 128), F32)
    f_lo = jnp.exp((scale[1:2, 0:1] - c) * 0.5)
    f_hi = jnp.exp((scale[2:3, 0:1] - c) * 0.5)
    for k, copy in enumerate(arriving):
        copy.wait()
        g = lax.rem(at[0] + k, count)
        rows = pl.ds(pl.multiple_of(g * block, block), block)
        summed = bary[rows, :] + sums[k]
        denominator = second[rows, :]
        share = summed * (jnp.log(denominator) + c)
        share = jnp.sum(share.reshape(block // 8, 8, columns), axis=0)
        for m in range(columns // 128):
            partial += share[:, m * 128 : (m + 1) * 128]
        f = jnp.where(2 * g < count, f_lo, f_hi)
        out[rows, :] = (weight[0] * summed - cot[rows, :]) / denominator * f * f
    leaving = edge_copies(out, to_near, to_far, sems, at[2])
    for copy in leaving:
        copy.start()
    lanes = lax.broadcasted_iota(jnp.int32, total.shape, 1)
    partial = jnp.sum(jnp.sum(partial, axis=0, keepdims=True), axis=1, keepdims=True)
    total[...] = jnp.where(lanes == at[1], partial, 0.0)
    for copy in leaving:
        copy.wait()


def gradient_kernel(
    where, kz, near, far, y, shifted, stats, kyh, kyl, kxh, kxl, out, halo, z, mid, result, sems, *, ny
):
    arriving = halo_copies(near, far, halo, sems, where[2])
    for copy in arriving:
        copy.start()
    c = stats[0:1, 0:1]
    f_left = tile(jnp.exp((c - stats[3:4, 0:1]) * 0.5))
    f_right = tile(jnp.exp((c - stats[4:5, 0:1]) * 0.5))
    has_left, has_right = where[0] > 0, where[1] > 0
    for copy in arriving:
        copy.wait()
    halo_planes(
        halo,
        kz,
        y,
        z,
        ny,
        lambda v: v,
        lambda v: jnp.where(has_left, v * f_left * f_left, 0.0),
        lambda v: jnp.where(has_right, v * f_right * f_right, 0.0),
    )
    half = mid.shape[0]
    leaving = []
    for g in range(2):
        rows = slice(g * half, (g + 1) * half)
        result[rows, :] = shifted[rows, :] * rows_and_columns(z, g, kyh, kyl, kxh, kxl, mid)
        leaving.append(pltpu.make_async_copy(result.at[rows], out.at[rows], sems.at[g]))
        leaving[-1].start()
    for copy in leaving:
        copy.wait()


def body(
    atom_log_density,
    prior_log_scaling,
    atom_cotangent_rows,
    barycenter_cotangent,
    weights,
    band,
    slot_atom_index,
):
    planes, ny, nx = barycenter_cotangent.shape
    slabs, atoms = lax.axis_size("slab"), lax.axis_size("atom")
    rows = planes * ny
    half = rows // 2
    block = GROUP * ny
    count = planes // GROUP
    slab_at, atom_at = lax.axis_index("slab"), lax.axis_index("atom")
    across = atoms // 2
    x_at = atom_at // 2

    smem = pl.BlockSpec(memory_space=pltpu.SMEM)
    vmem = pl.BlockSpec(memory_space=pltpu.VMEM)
    anywhere = pl.BlockSpec(memory_space=pl.ANY)
    hbm = pl.BlockSpec(memory_space=pltpu.HBM)
    params = pltpu.CompilerParams(vmem_limit_bytes=VMEM_LIMIT)

    def shape(*dims, dtype=F32):
        return jax.ShapeDtypeStruct(dims, dtype)

    def send(value, axis, pairs):
        return lax.ppermute(value, axis, pairs)

    in_order = lax.optimization_barrier
    cores = [(i, i ^ 1) for i in range(slabs)]
    chips = [(i, i + 1) for i in range(1, slabs - 1, 2)] + [(i + 1, i) for i in range(1, slabs - 1, 2)]
    core = slab_at % 2
    ahead = {
        k: [(2 * x + z, 2 * ((x + k) % across) + z) for x in range(across) for z in range(2)]
        for k in range(1, across)
    }
    swap = [(i, i ^ 1) for i in range(atoms)]

    cot = atom_cotangent_rows.reshape(rows, nx)

    def block_of(k):
        return lax.dynamic_slice_in_dim(cot, lax.rem(x_at + k, count) * block, block)

    blocks = [block_of(k) for k in range(1, across)]
    arrived = [send(blocks[k - 1], "atom", ahead[k]) for k in range(1, across)]

    y_shape, x_shape = (block, block), (nx, nx)
    distance = jnp.arange(BAND_MAX + 1, dtype=jnp.int32)
    kz = jnp.exp((distance * distance).astype(F32) * (-2.0 / (BAND_MAX * BAND_MAX)))
    kz = jnp.where(distance <= band[2], kz, 0.0)
    tables = pl.pallas_call(
        functools.partial(tables_kernel, ny=ny),
        out_shape=[shape(*dims, dtype=BF16) for dims in (y_shape, y_shape, x_shape, x_shape)],
        in_specs=[smem],
        out_specs=[vmem] * 4,
        compiler_params=params,
        name="tables",
    )(band)
    prior = prior_log_scaling.reshape(rows, nx)
    to_near = lax.dynamic_slice_in_dim(prior, (1 - core) * half, half)
    to_far = lax.dynamic_slice_in_dim(prior, core * half, half)
    far = [send(to_far[k : k + half // 2], "slab", chips) for k in (0, half // 2)]
    near = send(to_near, "slab", cores)

    where = jnp.stack([slab_at > 0, slab_at < slabs - 1, core > 0]).astype(jnp.int32)
    slot = lax.dynamic_slice_in_dim(slot_atom_index, atom_at, 1)
    onehot = (slot[0] == jnp.arange(weights.shape[0], dtype=jnp.int32)).astype(F32)
    weight = jnp.sum(onehot * weights, keepdims=True)

    own_out = [shape(rows, nx), shape(8, 128)]
    own_log = pl.pallas_call(
        functools.partial(own_log_kernel, ny=ny),
        in_specs=[smem, vmem],
        out_specs=[vmem, vmem],
        out_shape=own_out,
        compiler_params=params,
        name="own_log",
    )
    whole, halo = pltpu.VMEM((rows, nx), F32), pltpu.VMEM((2, half, nx), F32)
    scratch = [pltpu.VMEM((rows, nx), F32), pltpu.VMEM((half, nx), F32)]
    scale = pltpu.VMEM((8, 128), F32)

    y, stats = own_log(kz, prior)
    part = sum(arrived, block_of(0))
    y, part = in_order((y, part))
    swapped = send(part, "atom", swap)
    potential, to_near, to_far = pl.pallas_call(
        functools.partial(potential_kernel, ny=ny),
        in_specs=[smem, smem, hbm, hbm, hbm, hbm, vmem, hbm] + [vmem] * 4,
        out_specs=[vmem, anywhere, anywhere],
        out_shape=[shape(rows, nx), shape(half, nx), shape(half, nx)],
        scratch_shapes=[halo, whole, whole, *scratch, scale, pltpu.SemaphoreType.DMA((5,))],
        compiler_params=params,
        name="potential",
    )(where, kz, near, *far, y, stats, atom_log_density.reshape(rows, nx), *tables)

    far = send(to_far, "slab", chips)
    near = send(to_near, "slab", cores)
    both = part + swapped
    own_at, both = in_order((potential, both))
    sums = [both] + [send(both, "atom", ahead[across - k]) for k in range(1, across)]
    y, stats = own_log(kz, own_at)
    second, stats = pl.pallas_call(
        functools.partial(second_kernel, ny=ny),
        in_specs=[smem, smem, anywhere, anywhere] + [vmem] * 6,
        out_specs=[vmem, vmem],
        out_shape=[shape(rows, nx), shape(8, 128)],
        scratch_shapes=[halo, *scratch, pltpu.SemaphoreType.DMA((2,))],
        compiler_params=params,
        name="second",
    )(where, kz, near, far, y, stats, *tables)
    ratio, to_near, to_far, total = pl.pallas_call(
        ratio_kernel,
        in_specs=[smem, smem] + [vmem] * 4 + [anywhere] * 4,
        out_specs=[vmem, anywhere, anywhere, vmem],
        out_shape=[shape(rows, nx), shape(half, nx), shape(half, nx), shape(8, 128)],
        scratch_shapes=[
            pltpu.VMEM((count, block, nx), F32),
            pltpu.SemaphoreType.DMA((count,)),
        ],
        compiler_params=params,
        name="ratio",
    )(
        jnp.stack([x_at, slot[0], core]),
        weight,
        second,
        stats,
        barycenter_cotangent.reshape(rows, nx),
        cot,
        *sums,
    )

    far = send(to_far, "slab", chips)
    near = send(to_near, "slab", cores)
    y, shifted = pl.pallas_call(
        functools.partial(own_linear_kernel, ny=ny),
        in_specs=[smem] + [vmem] * 3,
        out_specs=[vmem, vmem],
        out_shape=[shape(rows, nx), shape(rows, nx)],
        compiler_params=params,
        name="own_linear",
    )(kz, ratio, potential, stats)

    def add(value, axis, patterns):
        return sum([send(value, axis, pairs) for pairs in patterns], value)

    def flips(hop):
        return [(i, i ^ hop) for i in range(slabs)]

    value = add(total, "slab", [cores])
    value = add(value, "atom", [ahead[k] for k in range(1, across)])
    value, y = in_order((value, y))
    value = add(value, "slab", [[(i, (i + k) % slabs) for i in range(slabs)] for k in (8, 16, 24)])
    for hop in (2, 4):
        value = add(value, "slab", [flips(hop)])
    value, near, far = in_order((value, near, far))
    value = add(value, "atom", [swap])
    weight_grad = value[0, : weights.shape[0]] / (rows * nx * slabs)

    gradient = pl.pallas_call(
        functools.partial(gradient_kernel, ny=ny),
        in_specs=[smem, smem, anywhere, anywhere] + [vmem] * 7,
        out_specs=anywhere,
        out_shape=shape(rows, nx),
        scratch_shapes=[halo, *scratch, whole, pltpu.SemaphoreType.DMA((2,))],
        compiler_params=params,
        name="gradient",
    )(where, kz, near, far, y, shifted, stats, *tables)
    return gradient.reshape(atom_log_density.shape), weight_grad


def solution(mesh):
    return jax.shard_map(
        body,
        mesh=mesh,
        in_specs=(
            P("atom", "slab", None, None),
            P("atom", "slab", None, None),
            P("atom", "slab", None, None),
            P("slab", None, None),
            P(),
            P(),
            P(),
        ),
        out_specs=(P("atom", "slab", None, None), P()),
        check_vma=False,
    )
```

```python
import functools

import jax
import jax.numpy as jnp
from jax import lax
from jax.experimental import pallas as pl
from jax.experimental.pallas import tpu as pltpu
from jax.sharding import PartitionSpec as P

BAND_MAX = 8
GROUP = 4
F32 = jnp.float32
BF16 = jnp.bfloat16
VMEM_LIMIT = 16 * 1024 * 1024


def split(value):
    high = value.astype(BF16)
    return high, (value - high.astype(F32)).astype(BF16)


def dot(a, b):
    return jnp.dot(a, b, preferred_element_type=F32)


def dot3(ah, al, bh, bl):
    return dot(ah, bh) + (dot(al, bh) + dot(ah, bl))


def peak(value):
    return jnp.max(jnp.max(value, axis=0, keepdims=True), axis=1, keepdims=True)


def rows_of(values):
    return jnp.concatenate([jnp.broadcast_to(v, (1, 128)) for v in values], axis=0)


def tables_kernel(band, kyh, kyl, kxh, kxl, *, ny):
    def entries(sq, ok):
        return jnp.where(ok, jnp.exp(sq.astype(F32) * (-2.0 / (BAND_MAX * BAND_MAX))), 0.0)

    def offsets(shape):
        return lax.broadcasted_iota(jnp.int32, shape, 0), lax.broadcasted_iota(jnp.int32, shape, 1)

    row, col = offsets(kyh.shape)
    shift = ny.bit_length() - 1
    dy = row - col
    kyh[...], kyl[...] = split(entries(dy * dy, ((row >> shift) == (col >> shift)) & (jnp.abs(dy) <= band[1])))
    row, col = offsets(kxh.shape)
    dx = row - col
    kxh[...], kxl[...] = split(entries(dx * dx, jnp.abs(dx) <= band[0]))


def tile_loop(ny, nx, step):
    across = nx // 128

    def body_of(i, carry):
        row = pl.multiple_of(lax.div(i, across) * 8, 8)
        column = pl.multiple_of(lax.rem(i, across) * 128, 128)
        step(row, pl.ds(column, 128))
        return carry

    lax.fori_loop(0, ny // 8 * across, body_of, 0)


def own_planes(field, kz, y, ny, entry_lo, entry_hi):
    planes = field.shape[0] // ny
    taps = [kz[d] for d in range(BAND_MAX + 1)]

    def step(row, columns):
        e = [
            (entry_lo if 2 * q < planes else entry_hi)(field[pl.ds(q * ny + row, 8), columns])
            for q in range(planes)
        ]
        for p in range(planes):
            total = taps[0] * e[p]
            for d in range(1, BAND_MAX + 1):
                near = [e[q] for q in (p - d, p + d) if 0 <= q < planes]
                total += taps[d] * (near[0] if len(near) == 1 else near[0] + near[1])
            y[pl.ds(p * ny + row, 8), columns] = total

    tile_loop(ny, field.shape[1], step)


def halo_copies(near, far, halo, sems, core):
    return [
        pltpu.make_async_copy(near, halo.at[1 - core], sems.at[0]),
        pltpu.make_async_copy(far, halo.at[core], sems.at[1]),
    ]


def edge_copies(field, near, far, sems, core):
    half = near.shape[0]

    def rows(k):
        return pl.ds(pl.multiple_of(k * half, half), half)

    return [
        pltpu.make_async_copy(field.at[rows(1 - core)], near, sems.at[0]),
        pltpu.make_async_copy(field.at[rows(core)], far, sems.at[1]),
    ]


def halo_planes(halo, kz, y, z, ny, own, entry_left, entry_right):
    side = halo.shape[1] // ny
    taps = [kz[d] for d in range(BAND_MAX + 1)]

    def step(row, columns):
        e = [entry_left(halo[0, pl.ds(q * ny + row, 8), columns]) for q in range(side)]
        for p in range(side):
            rows = pl.ds(p * ny + row, 8)
            total = own(y[rows, columns])
            for q in range(max(0, p + side - BAND_MAX), side):
                total += taps[p + side - q] * e[q]
            z[rows, columns] = total
        e = [entry_right(halo[1, pl.ds(q * ny + row, 8), columns]) for q in range(side)]
        for p in range(side):
            rows = pl.ds((side + p) * ny + row, 8)
            total = own(y[rows, columns])
            for q in range(min(side, p + BAND_MAX - side + 1)):
                total += taps[side + q - p] * e[q]
            z[rows, columns] = total

    tile_loop(ny, halo.shape[2], step)


def tile(value):
    return jnp.broadcast_to(value, (8, 128))


def own_log_kernel(kz, field, y, stats, *, ny):
    half = field.shape[0] // 2
    m_lo, m_hi = peak(field[:half, :]), peak(field[half:, :])
    m = jnp.maximum(m_lo, m_hi)
    stats[...] = rows_of([m_lo, m_hi, m, m, m, m, m, m])
    m = tile(m)
    entry = lambda v: jnp.exp(v - m)
    own_planes(field, kz, y, ny, entry, entry)


def own_linear_kernel(kz, field, potential, stats, y, shifted, *, ny):
    c = stats[0:1, 0:1]
    shifted[...] = jnp.exp(potential[...] - c)
    f_lo = tile(jnp.exp((c - stats[1:2, 0:1]) * 0.5))
    f_hi = tile(jnp.exp((c - stats[2:3, 0:1]) * 0.5))
    own_planes(field, kz, y, ny, lambda v: v * f_lo * f_lo, lambda v: v * f_hi * f_hi)


def rows_and_columns(z, g, kyh, kyl, kxh, kxl, mid):
    half, block = mid.shape[0], kyh.shape[0]
    for k in range(half // block):
        rows = pl.ds(g * half + k * block, block)
        zh, zl = split(z[rows, :])
        mid[k * block : (k + 1) * block, :] = dot3(kyh[...], kyl[...], zh, zl)
    mh, ml = split(mid[...])
    return dot3(mh, ml, kxh[...], kxl[...])


def log_halos(where, kz, halo, y, stats, z, scale, ny):
    has_left, has_right = where[0] > 0, where[1] > 0
    m_own = stats[2:3, 0:1]
    m_left = jnp.where(has_left, peak(halo[0]), m_own)
    m_right = jnp.where(has_right, peak(halo[1]), m_own)
    c = jnp.maximum(m_own, jnp.maximum(m_left, m_right))
    scale[...] = rows_of([c, stats[0:1, 0:1], stats[1:2, 0:1], m_left, m_right, c, c, c])
    own = tile(jnp.exp(m_own - c))
    c = tile(c)
    halo_planes(
        halo,
        kz,
        y,
        z,
        ny,
        lambda v: v * own,
        lambda v: jnp.where(has_left, jnp.exp(v - c), 0.0),
        lambda v: jnp.where(has_right, jnp.exp(v - c), 0.0),
    )


def potential_kernel(
    where, kz, near, far, more, y_in, stats, density_in, kyh, kyl, kxh, kxl, potential, to_near, to_far,
    halo, y, density, z, mid, scale, sems, *, ny
):
    core = where[2]
    piece = far.shape[0]
    arriving = [
        pltpu.make_async_copy(near, halo.at[1 - core], sems.at[0]),
        pltpu.make_async_copy(far, halo.at[core, pl.ds(0, piece)], sems.at[1]),
        pltpu.make_async_copy(more, halo.at[core, pl.ds(piece, piece)], sems.at[4]),
    ]
    late = [pltpu.make_async_copy(y_in, y, sems.at[2]), pltpu.make_async_copy(density_in, density, sems.at[3])]
    for copy in arriving + late:
        copy.start()
    for copy in arriving + late[:1]:
        copy.wait()
    log_halos(where, kz, halo, y, stats, z, scale, ny)
    half = mid.shape[0]
    late[1].wait()
    for g in range(2):
        rows = slice(g * half, (g + 1) * half)
        first = rows_and_columns(z, g, kyh, kyl, kxh, kxl, mid)
        potential[rows, :] = density[rows, :] - (jnp.log(first) + scale[0:1, 0:1])
    leaving = edge_copies(potential, to_near, to_far, sems, core)
    for copy in leaving:
        copy.start()
    for copy in leaving:
        copy.wait()


def second_kernel(
    where, kz, near, far, y, stats, kyh, kyl, kxh, kxl, out, scale, halo, z, mid, sems, *, ny
):
    arriving = halo_copies(near, far, halo, sems, where[2])
    for copy in arriving:
        copy.start()
    for copy in arriving:
        copy.wait()
    log_halos(where, kz, halo, y, stats, z, scale, ny)
    half = mid.shape[0]
    for g in range(2):
        out[g * half : (g + 1) * half, :] = rows_and_columns(z, g, kyh, kyl, kxh, kxl, mid)


def ratio_kernel(
    at, weight, second, scale, bary, cot, sum0, sum1, sum2, sum3, out, to_near, to_far, total, sums, sems
):
    c = scale[0:1, 0:1]
    block, columns = sums.shape[1:]
    count = sums.shape[0]
    arriving = [
        pltpu.make_async_copy(ref, sums.at[k], sems.at[k]) for k, ref in enumerate((sum0, sum1, sum2, sum3))
    ]
    for copy in arriving:
        copy.start()
    partial = jnp.zeros((8, 128), F32)
    f_lo = jnp.exp((scale[1:2, 0:1] - c) * 0.5)
    f_hi = jnp.exp((scale[2:3, 0:1] - c) * 0.5)
    for k, copy in enumerate(arriving):
        copy.wait()
        g = lax.rem(at[0] + k, count)
        rows = pl.ds(pl.multiple_of(g * block, block), block)
        summed = bary[rows, :] + sums[k]
        denominator = second[rows, :]
        share = summed * (jnp.log(denominator) + c)
        share = jnp.sum(share.reshape(block // 8, 8, columns), axis=0)
        for m in range(columns // 128):
            partial += share[:, m * 128 : (m + 1) * 128]
        f = jnp.where(2 * g < count, f_lo, f_hi)
        out[rows, :] = (weight[0] * summed - cot[rows, :]) / denominator * f * f
    leaving = edge_copies(out, to_near, to_far, sems, at[2])
    for copy in leaving:
        copy.start()
    lanes = lax.broadcasted_iota(jnp.int32, total.shape, 1)
    partial = jnp.sum(jnp.sum(partial, axis=0, keepdims=True), axis=1, keepdims=True)
    total[...] = jnp.where(lanes == at[1], partial, 0.0)
    for copy in leaving:
        copy.wait()


def gather_kernel(where, kz, near, far, y, stats, z, halo, sems, *, ny):
    arriving = halo_copies(near, far, halo, sems, where[2])
    for copy in arriving:
        copy.start()
    c = stats[0:1, 0:1]
    f_left = tile(jnp.exp((c - stats[3:4, 0:1]) * 0.5))
    f_right = tile(jnp.exp((c - stats[4:5, 0:1]) * 0.5))
    has_left, has_right = where[0] > 0, where[1] > 0
    for copy in arriving:
        copy.wait()
    halo_planes(
        halo,
        kz,
        y,
        z,
        ny,
        lambda v: v,
        lambda v: jnp.where(has_left, v * f_left * f_left, 0.0),
        lambda v: jnp.where(has_right, v * f_right * f_right, 0.0),
    )


def gradient_kernel(z, shifted, kyh, kyl, kxh, kxl, out, mid, result, sems):
    half = mid.shape[0]
    leaving = []
    for g in range(2):
        rows = slice(g * half, (g + 1) * half)
        result[rows, :] = shifted[rows, :] * rows_and_columns(z, g, kyh, kyl, kxh, kxl, mid)
        leaving.append(pltpu.make_async_copy(result.at[rows], out.at[rows], sems.at[g]))
        leaving[-1].start()
    for copy in leaving:
        copy.wait()


def body(
    atom_log_density,
    prior_log_scaling,
    atom_cotangent_rows,
    barycenter_cotangent,
    weights,
    band,
    slot_atom_index,
):
    planes, ny, nx = barycenter_cotangent.shape
    slabs, atoms = lax.axis_size("slab"), lax.axis_size("atom")
    rows = planes * ny
    half = rows // 2
    block = GROUP * ny
    count = planes // GROUP
    slab_at, atom_at = lax.axis_index("slab"), lax.axis_index("atom")
    across = atoms // 2
    x_at = atom_at // 2

    smem = pl.BlockSpec(memory_space=pltpu.SMEM)
    vmem = pl.BlockSpec(memory_space=pltpu.VMEM)
    anywhere = pl.BlockSpec(memory_space=pl.ANY)
    hbm = pl.BlockSpec(memory_space=pltpu.HBM)
    params = pltpu.CompilerParams(vmem_limit_bytes=VMEM_LIMIT)

    def shape(*dims, dtype=F32):
        return jax.ShapeDtypeStruct(dims, dtype)

    def send(value, axis, pairs):
        return lax.ppermute(value, axis, pairs)

    in_order = lax.optimization_barrier
    cores = [(i, i ^ 1) for i in range(slabs)]
    chips = [(i, i + 1) for i in range(1, slabs - 1, 2)] + [(i + 1, i) for i in range(1, slabs - 1, 2)]
    core = slab_at % 2
    ahead = {
        k: [(2 * x + z, 2 * ((x + k) % across) + z) for x in range(across) for z in range(2)]
        for k in range(1, across)
    }
    swap = [(i, i ^ 1) for i in range(atoms)]

    cot = atom_cotangent_rows.reshape(rows, nx)

    def block_of(k):
        return lax.dynamic_slice_in_dim(cot, lax.rem(x_at + k, count) * block, block)

    blocks = [block_of(k) for k in range(1, across)]
    arrived = [send(blocks[k - 1], "atom", ahead[k]) for k in range(1, across)]

    y_shape, x_shape = (block, block), (nx, nx)
    distance = jnp.arange(BAND_MAX + 1, dtype=jnp.int32)
    kz = jnp.exp((distance * distance).astype(F32) * (-2.0 / (BAND_MAX * BAND_MAX)))
    kz = jnp.where(distance <= band[2], kz, 0.0)
    tables = pl.pallas_call(
        functools.partial(tables_kernel, ny=ny),
        out_shape=[shape(*dims, dtype=BF16) for dims in (y_shape, y_shape, x_shape, x_shape)],
        in_specs=[smem],
        out_specs=[vmem] * 4,
        compiler_params=params,
        name="tables",
    )(band)
    prior = prior_log_scaling.reshape(rows, nx)
    to_near = lax.dynamic_slice_in_dim(prior, (1 - core) * half, half)
    to_far = lax.dynamic_slice_in_dim(prior, core * half, half)
    far = [send(to_far[k : k + half // 2], "slab", chips) for k in (0, half // 2)]
    near = send(to_near, "slab", cores)

    where = jnp.stack([slab_at > 0, slab_at < slabs - 1, core > 0]).astype(jnp.int32)
    slot = lax.dynamic_slice_in_dim(slot_atom_index, atom_at, 1)
    onehot = (slot[0] == jnp.arange(weights.shape[0], dtype=jnp.int32)).astype(F32)
    weight = jnp.sum(onehot * weights, keepdims=True)

    own_out = [shape(rows, nx), shape(8, 128)]
    own_log = pl.pallas_call(
        functools.partial(own_log_kernel, ny=ny),
        in_specs=[smem, vmem],
        out_specs=[vmem, vmem],
        out_shape=own_out,
        compiler_params=params,
        name="own_log",
    )
    whole, halo = pltpu.VMEM((rows, nx), F32), pltpu.VMEM((2, half, nx), F32)
    scratch = [pltpu.VMEM((rows, nx), F32), pltpu.VMEM((half, nx), F32)]
    scale = pltpu.VMEM((8, 128), F32)

    y, stats = own_log(kz, prior)
    part = sum(arrived, block_of(0))
    y, part = in_order((y, part))
    swapped = send(part, "atom", swap)
    potential, to_near, to_far = pl.pallas_call(
        functools.partial(potential_kernel, ny=ny),
        in_specs=[smem, smem, hbm, hbm, hbm, hbm, vmem, hbm] + [vmem] * 4,
        out_specs=[vmem, anywhere, anywhere],
        out_shape=[shape(rows, nx), shape(half, nx), shape(half, nx)],
        scratch_shapes=[halo, whole, whole, *scratch, scale, pltpu.SemaphoreType.DMA((5,))],
        compiler_params=params,
        name="potential",
    )(where, kz, near, *far, y, stats, atom_log_density.reshape(rows, nx), *tables)

    far = send(to_far, "slab", chips)
    near = send(to_near, "slab", cores)
    both = part + swapped
    own_at, both = in_order((potential, both))
    sums = [both] + [send(both, "atom", ahead[across - k]) for k in range(1, across)]
    y, stats = own_log(kz, own_at)
    second, stats = pl.pallas_call(
        functools.partial(second_kernel, ny=ny),
        in_specs=[smem, smem, anywhere, anywhere] + [vmem] * 6,
        out_specs=[vmem, vmem],
        out_shape=[shape(rows, nx), shape(8, 128)],
        scratch_shapes=[halo, *scratch, pltpu.SemaphoreType.DMA((2,))],
        compiler_params=params,
        name="second",
    )(where, kz, near, far, y, stats, *tables)
    ratio, to_near, to_far, total = pl.pallas_call(
        ratio_kernel,
        in_specs=[smem, smem] + [vmem] * 4 + [anywhere] * 4,
        out_specs=[vmem, anywhere, anywhere, vmem],
        out_shape=[shape(rows, nx), shape(half, nx), shape(half, nx), shape(8, 128)],
        scratch_shapes=[
            pltpu.VMEM((count, block, nx), F32),
            pltpu.SemaphoreType.DMA((count,)),
        ],
        compiler_params=params,
        name="ratio",
    )(
        jnp.stack([x_at, slot[0], core]),
        weight,
        second,
        stats,
        barycenter_cotangent.reshape(rows, nx),
        cot,
        *sums,
    )

    far = send(to_far, "slab", chips)
    near = send(to_near, "slab", cores)
    y, shifted = pl.pallas_call(
        functools.partial(own_linear_kernel, ny=ny),
        in_specs=[smem] + [vmem] * 3,
        out_specs=[vmem, vmem],
        out_shape=[shape(rows, nx), shape(rows, nx)],
        compiler_params=params,
        name="own_linear",
    )(kz, ratio, potential, stats)

    def add(value, axis, patterns):
        return sum([send(value, axis, pairs) for pairs in patterns], value)

    def flips(hop):
        return [(i, i ^ hop) for i in range(slabs)]

    value = add(total, "slab", [cores])
    value = add(value, "atom", [ahead[k] for k in range(1, across)])
    value, y = in_order((value, y))
    value = add(value, "slab", [[(i, (i + k) % slabs) for i in range(slabs)] for k in (8, 16, 24)])
    value = add(value, "slab", [flips(2)])
    value, near, far = in_order((value, near, far))
    z = pl.pallas_call(
        functools.partial(gather_kernel, ny=ny),
        in_specs=[smem, smem, anywhere, anywhere, vmem, vmem],
        out_specs=vmem,
        out_shape=shape(rows, nx),
        scratch_shapes=[halo, pltpu.SemaphoreType.DMA((2,))],
        compiler_params=params,
        name="gather",
    )(where, kz, near, far, y, stats)
    value = add(value, "slab", [flips(4)])
    value, z = in_order((value, z))
    value = add(value, "atom", [swap])
    weight_grad = value[0, : weights.shape[0]] / (rows * nx * slabs)

    gradient = pl.pallas_call(
        gradient_kernel,
        in_specs=[vmem] * 6,
        out_specs=anywhere,
        out_shape=shape(rows, nx),
        scratch_shapes=[scratch[1], whole, pltpu.SemaphoreType.DMA((2,))],
        compiler_params=params,
        name="gradient",
    )(z, shifted, *tables)
    return gradient.reshape(atom_log_density.shape), weight_grad


def solution(mesh):
    return jax.shard_map(
        body,
        mesh=mesh,
        in_specs=(
            P("atom", "slab", None, None),
            P("atom", "slab", None, None),
            P("atom", "slab", None, None),
            P("slab", None, None),
            P(),
            P(),
            P(),
        ),
        out_specs=(P("atom", "slab", None, None), P()),
        check_vma=False,
    )
```

```python
import functools

import jax
import jax.numpy as jnp
from jax import lax
from jax.experimental import pallas as pl
from jax.experimental.pallas import tpu as pltpu
from jax.sharding import PartitionSpec as P

BAND_MAX = 8
GROUP = 4
F32 = jnp.float32
BF16 = jnp.bfloat16
VMEM_LIMIT = 16 * 1024 * 1024


def split(value):
    high = value.astype(BF16)
    return high, (value - high.astype(F32)).astype(BF16)


def dot(a, b):
    return jnp.dot(a, b, preferred_element_type=F32)


def dot3(ah, al, bh, bl):
    return dot(ah, bh) + (dot(al, bh) + dot(ah, bl))


def peak(value):
    return jnp.max(jnp.max(value, axis=0, keepdims=True), axis=1, keepdims=True)


def rows_of(values):
    return jnp.concatenate([jnp.broadcast_to(v, (1, 128)) for v in values], axis=0)


def tables_kernel(band, kyh, kyl, kxh, kxl, *, ny):
    def entries(sq, ok):
        return jnp.where(ok, jnp.exp(sq.astype(F32) * (-2.0 / (BAND_MAX * BAND_MAX))), 0.0)

    def offsets(shape):
        return lax.broadcasted_iota(jnp.int32, shape, 0), lax.broadcasted_iota(jnp.int32, shape, 1)

    row, col = offsets(kyh.shape)
    shift = ny.bit_length() - 1
    dy = row - col
    kyh[...], kyl[...] = split(entries(dy * dy, ((row >> shift) == (col >> shift)) & (jnp.abs(dy) <= band[1])))
    row, col = offsets(kxh.shape)
    dx = row - col
    kxh[...], kxl[...] = split(entries(dx * dx, jnp.abs(dx) <= band[0]))


def tile_loop(ny, nx, step):
    across = nx // 128

    def body_of(i, carry):
        row = pl.multiple_of(lax.div(i, across) * 8, 8)
        column = pl.multiple_of(lax.rem(i, across) * 128, 128)
        step(row, pl.ds(column, 128))
        return carry

    lax.fori_loop(0, ny // 8 * across, body_of, 0)


def own_planes(field, kz, y, ny, entry_lo, entry_hi):
    planes = field.shape[0] // ny
    taps = [kz[d] for d in range(BAND_MAX + 1)]

    def step(row, columns):
        e = [
            (entry_lo if 2 * q < planes else entry_hi)(field[pl.ds(q * ny + row, 8), columns])
            for q in range(planes)
        ]
        for p in range(planes):
            total = taps[0] * e[p]
            for d in range(1, BAND_MAX + 1):
                near = [e[q] for q in (p - d, p + d) if 0 <= q < planes]
                total += taps[d] * (near[0] if len(near) == 1 else near[0] + near[1])
            y[pl.ds(p * ny + row, 8), columns] = total

    tile_loop(ny, field.shape[1], step)


def halo_copies(near, far, halo, sems, core):
    return [
        pltpu.make_async_copy(near, halo.at[1 - core], sems.at[0]),
        pltpu.make_async_copy(far, halo.at[core], sems.at[1]),
    ]


def edge_copies(field, near, far, sems, core):
    half = near.shape[0]

    def rows(k):
        return pl.ds(pl.multiple_of(k * half, half), half)

    return [
        pltpu.make_async_copy(field.at[rows(1 - core)], near, sems.at[0]),
        pltpu.make_async_copy(field.at[rows(core)], far, sems.at[1]),
    ]


def halo_planes(halo, kz, y, z, ny, own, entry_left, entry_right):
    side = halo.shape[1] // ny
    taps = [kz[d] for d in range(BAND_MAX + 1)]

    def step(row, columns):
        e = [entry_left(halo[0, pl.ds(q * ny + row, 8), columns]) for q in range(side)]
        for p in range(side):
            rows = pl.ds(p * ny + row, 8)
            total = own(y[rows, columns])
            for q in range(max(0, p + side - BAND_MAX), side):
                total += taps[p + side - q] * e[q]
            z[rows, columns] = total
        e = [entry_right(halo[1, pl.ds(q * ny + row, 8), columns]) for q in range(side)]
        for p in range(side):
            rows = pl.ds((side + p) * ny + row, 8)
            total = own(y[rows, columns])
            for q in range(min(side, p + BAND_MAX - side + 1)):
                total += taps[side + q - p] * e[q]
            z[rows, columns] = total

    tile_loop(ny, halo.shape[2], step)


def tile(value):
    return jnp.broadcast_to(value, (8, 128))


def own_log_kernel(kz, field, y, stats, *, ny):
    half = field.shape[0] // 2
    m_lo, m_hi = peak(field[:half, :]), peak(field[half:, :])
    m = jnp.maximum(m_lo, m_hi)
    stats[...] = rows_of([m_lo, m_hi, m, m, m, m, m, m])
    m = tile(m)
    entry = lambda v: jnp.exp(v - m)
    own_planes(field, kz, y, ny, entry, entry)


def own_linear_kernel(kz, field, potential, stats, y, shifted, *, ny):
    c = stats[0:1, 0:1]
    shifted[...] = jnp.exp(potential[...] - c)
    f_lo = tile(jnp.exp((c - stats[1:2, 0:1]) * 0.5))
    f_hi = tile(jnp.exp((c - stats[2:3, 0:1]) * 0.5))
    own_planes(field, kz, y, ny, lambda v: v * f_lo * f_lo, lambda v: v * f_hi * f_hi)


def rows_and_columns(z, g, kyh, kyl, kxh, kxl, mid):
    half, block = mid.shape[0], kyh.shape[0]
    for k in range(half // block):
        rows = pl.ds(g * half + k * block, block)
        zh, zl = split(z[rows, :])
        mid[k * block : (k + 1) * block, :] = dot3(kyh[...], kyl[...], zh, zl)
    mh, ml = split(mid[...])
    return dot3(mh, ml, kxh[...], kxl[...])


def log_halos(where, kz, halo, y, stats, z, scale, ny):
    has_left, has_right = where[0] > 0, where[1] > 0
    m_own = stats[2:3, 0:1]
    m_left = jnp.where(has_left, peak(halo[0]), m_own)
    m_right = jnp.where(has_right, peak(halo[1]), m_own)
    c = jnp.maximum(m_own, jnp.maximum(m_left, m_right))
    scale[...] = rows_of([c, stats[0:1, 0:1], stats[1:2, 0:1], m_left, m_right, c, c, c])
    own = tile(jnp.exp(m_own - c))
    c = tile(c)
    halo_planes(
        halo,
        kz,
        y,
        z,
        ny,
        lambda v: v * own,
        lambda v: jnp.where(has_left, jnp.exp(v - c), 0.0),
        lambda v: jnp.where(has_right, jnp.exp(v - c), 0.0),
    )


def potential_kernel(
    where, kz, near, far, more, y_in, stats, density_in, kyh, kyl, kxh, kxl, potential, to_near, to_far,
    halo, y, density, z, mid, scale, sems, *, ny
):
    core = where[2]
    piece = far.shape[0]
    arriving = [
        pltpu.make_async_copy(near, halo.at[1 - core], sems.at[0]),
        pltpu.make_async_copy(far, halo.at[core, pl.ds(0, piece)], sems.at[1]),
        pltpu.make_async_copy(more, halo.at[core, pl.ds(piece, piece)], sems.at[4]),
    ]
    late = [pltpu.make_async_copy(y_in, y, sems.at[2]), pltpu.make_async_copy(density_in, density, sems.at[3])]
    for copy in arriving + late:
        copy.start()
    for copy in arriving + late[:1]:
        copy.wait()
    log_halos(where, kz, halo, y, stats, z, scale, ny)
    half = mid.shape[0]
    late[1].wait()
    for g in range(2):
        rows = slice(g * half, (g + 1) * half)
        first = rows_and_columns(z, g, kyh, kyl, kxh, kxl, mid)
        potential[rows, :] = density[rows, :] - (jnp.log(first) + scale[0:1, 0:1])
    leaving = edge_copies(potential, to_near, to_far, sems, core)
    for copy in leaving:
        copy.start()
    for copy in leaving:
        copy.wait()


def second_kernel(
    where, kz, near, far, y, stats, kyh, kyl, kxh, kxl, out, scale, halo, z, mid, sems, *, ny
):
    arriving = halo_copies(near, far, halo, sems, where[2])
    for copy in arriving:
        copy.start()
    for copy in arriving:
        copy.wait()
    log_halos(where, kz, halo, y, stats, z, scale, ny)
    half = mid.shape[0]
    for g in range(2):
        out[g * half : (g + 1) * half, :] = rows_and_columns(z, g, kyh, kyl, kxh, kxl, mid)


def ratio_kernel(
    at, weight, second, scale, bary, cot, sum0, sum1, sum2, sum3, out, to_near, to_far, total, sums, sems
):
    c = scale[0:1, 0:1]
    block, columns = sums.shape[1:]
    count = sums.shape[0]
    arriving = [
        pltpu.make_async_copy(ref, sums.at[k], sems.at[k]) for k, ref in enumerate((sum0, sum1, sum2, sum3))
    ]
    for copy in arriving:
        copy.start()
    partial = jnp.zeros((8, 128), F32)
    f_lo = jnp.exp((scale[1:2, 0:1] - c) * 0.5)
    f_hi = jnp.exp((scale[2:3, 0:1] - c) * 0.5)
    for k, copy in enumerate(arriving):
        copy.wait()
        g = lax.rem(at[0] + k, count)
        rows = pl.ds(pl.multiple_of(g * block, block), block)
        summed = bary[rows, :] + sums[k]
        denominator = second[rows, :]
        share = summed * (jnp.log(denominator) + c)
        share = jnp.sum(share.reshape(block // 8, 8, columns), axis=0)
        for m in range(columns // 128):
            partial += share[:, m * 128 : (m + 1) * 128]
        f = jnp.where(2 * g < count, f_lo, f_hi)
        out[rows, :] = (weight[0] * summed - cot[rows, :]) / denominator * f * f
    leaving = edge_copies(out, to_near, to_far, sems, at[2])
    for copy in leaving:
        copy.start()
    lanes = lax.broadcasted_iota(jnp.int32, total.shape, 1)
    partial = jnp.sum(jnp.sum(partial, axis=0, keepdims=True), axis=1, keepdims=True)
    total[...] = jnp.where(lanes == at[1], partial, 0.0)
    for copy in leaving:
        copy.wait()


def gather_kernel(where, kz, near, far, y, stats, z, halo, sems, *, ny):
    arriving = halo_copies(near, far, halo, sems, where[2])
    for copy in arriving:
        copy.start()
    c = stats[0:1, 0:1]
    f_left = tile(jnp.exp((c - stats[3:4, 0:1]) * 0.5))
    f_right = tile(jnp.exp((c - stats[4:5, 0:1]) * 0.5))
    has_left, has_right = where[0] > 0, where[1] > 0
    for copy in arriving:
        copy.wait()
    halo_planes(
        halo,
        kz,
        y,
        z,
        ny,
        lambda v: v,
        lambda v: jnp.where(has_left, v * f_left * f_left, 0.0),
        lambda v: jnp.where(has_right, v * f_right * f_right, 0.0),
    )


def gradient_kernel(z, shifted, kyh, kyl, kxh, kxl, out, mid, result, sems):
    half = mid.shape[0]
    leaving = []
    for g in range(2):
        rows = slice(g * half, (g + 1) * half)
        result[rows, :] = shifted[rows, :] * rows_and_columns(z, g, kyh, kyl, kxh, kxl, mid)
        leaving.append(pltpu.make_async_copy(result.at[rows], out.at[rows], sems.at[g]))
        leaving[-1].start()
    for copy in leaving:
        copy.wait()


def body(
    atom_log_density,
    prior_log_scaling,
    atom_cotangent_rows,
    barycenter_cotangent,
    weights,
    band,
    slot_atom_index,
):
    planes, ny, nx = barycenter_cotangent.shape
    slabs, atoms = lax.axis_size("slab"), lax.axis_size("atom")
    rows = planes * ny
    half = rows // 2
    block = GROUP * ny
    count = planes // GROUP
    slab_at, atom_at = lax.axis_index("slab"), lax.axis_index("atom")
    across = atoms // 2
    x_at = atom_at // 2

    smem = pl.BlockSpec(memory_space=pltpu.SMEM)
    vmem = pl.BlockSpec(memory_space=pltpu.VMEM)
    anywhere = pl.BlockSpec(memory_space=pl.ANY)
    hbm = pl.BlockSpec(memory_space=pltpu.HBM)
    params = pltpu.CompilerParams(vmem_limit_bytes=VMEM_LIMIT)

    def shape(*dims, dtype=F32):
        return jax.ShapeDtypeStruct(dims, dtype)

    def send(value, axis, pairs):
        return lax.ppermute(value, axis, pairs)

    in_order = lax.optimization_barrier
    cores = [(i, i ^ 1) for i in range(slabs)]
    chips = [(i, i + 1) for i in range(1, slabs - 1, 2)] + [(i + 1, i) for i in range(1, slabs - 1, 2)]
    core = slab_at % 2
    ahead = {
        k: [(2 * x + z, 2 * ((x + k) % across) + z) for x in range(across) for z in range(2)]
        for k in range(1, across)
    }
    swap = [(i, i ^ 1) for i in range(atoms)]

    cot = atom_cotangent_rows.reshape(rows, nx)

    def block_of(k):
        return lax.dynamic_slice_in_dim(cot, lax.rem(x_at + k, count) * block, block)

    blocks = [block_of(k) for k in range(1, across)]
    arrived = [send(blocks[k - 1], "atom", ahead[k]) for k in range(1, across)]

    y_shape, x_shape = (block, block), (nx, nx)
    distance = jnp.arange(BAND_MAX + 1, dtype=jnp.int32)
    kz = jnp.exp((distance * distance).astype(F32) * (-2.0 / (BAND_MAX * BAND_MAX)))
    kz = jnp.where(distance <= band[2], kz, 0.0)
    tables = pl.pallas_call(
        functools.partial(tables_kernel, ny=ny),
        out_shape=[shape(*dims, dtype=BF16) for dims in (y_shape, y_shape, x_shape, x_shape)],
        in_specs=[smem],
        out_specs=[vmem] * 4,
        compiler_params=params,
        name="tables",
    )(band)
    prior = prior_log_scaling.reshape(rows, nx)
    to_near = lax.dynamic_slice_in_dim(prior, (1 - core) * half, half)
    to_far = lax.dynamic_slice_in_dim(prior, core * half, half)
    far = [send(to_far[k : k + half // 2], "slab", chips) for k in (0, half // 2)]
    near = send(to_near, "slab", cores)

    where = jnp.stack([slab_at > 0, slab_at < slabs - 1, core > 0]).astype(jnp.int32)
    slot = lax.dynamic_slice_in_dim(slot_atom_index, atom_at, 1)
    onehot = (slot[0] == jnp.arange(weights.shape[0], dtype=jnp.int32)).astype(F32)
    weight = jnp.sum(onehot * weights, keepdims=True)

    own_out = [shape(rows, nx), shape(8, 128)]
    own_log = pl.pallas_call(
        functools.partial(own_log_kernel, ny=ny),
        in_specs=[smem, vmem],
        out_specs=[vmem, vmem],
        out_shape=own_out,
        compiler_params=params,
        name="own_log",
    )
    whole, halo = pltpu.VMEM((rows, nx), F32), pltpu.VMEM((2, half, nx), F32)
    scratch = [pltpu.VMEM((rows, nx), F32), pltpu.VMEM((half, nx), F32)]
    scale = pltpu.VMEM((8, 128), F32)

    y, stats = own_log(kz, prior)
    part = sum(arrived, block_of(0))
    y, part = in_order((y, part))
    swapped = send(part, "atom", swap)
    potential, to_near, to_far = pl.pallas_call(
        functools.partial(potential_kernel, ny=ny),
        in_specs=[smem, smem, hbm, hbm, hbm, hbm, vmem, hbm] + [vmem] * 4,
        out_specs=[vmem, anywhere, anywhere],
        out_shape=[shape(rows, nx), shape(half, nx), shape(half, nx)],
        scratch_shapes=[halo, whole, whole, *scratch, scale, pltpu.SemaphoreType.DMA((5,))],
        compiler_params=params,
        name="potential",
    )(where, kz, near, *far, y, stats, atom_log_density.reshape(rows, nx), *tables)

    far = send(to_far, "slab", chips)
    near = send(to_near, "slab", cores)
    both = part + swapped
    own_at, both = in_order((potential, both))
    sums = [both] + [send(both, "atom", ahead[across - k]) for k in range(1, across)]
    y, stats = own_log(kz, own_at)
    second, stats = pl.pallas_call(
        functools.partial(second_kernel, ny=ny),
        in_specs=[smem, smem, anywhere, anywhere] + [vmem] * 6,
        out_specs=[vmem, vmem],
        out_shape=[shape(rows, nx), shape(8, 128)],
        scratch_shapes=[halo, *scratch, pltpu.SemaphoreType.DMA((2,))],
        compiler_params=params,
        name="second",
    )(where, kz, near, far, y, stats, *tables)
    ratio, to_near, to_far, total = pl.pallas_call(
        ratio_kernel,
        in_specs=[smem, smem] + [vmem] * 4 + [anywhere] * 4,
        out_specs=[vmem, anywhere, anywhere, vmem],
        out_shape=[shape(rows, nx), shape(half, nx), shape(half, nx), shape(8, 128)],
        scratch_shapes=[
            pltpu.VMEM((count, block, nx), F32),
            pltpu.SemaphoreType.DMA((count,)),
        ],
        compiler_params=params,
        name="ratio",
    )(
        jnp.stack([x_at, slot[0], core]),
        weight,
        second,
        stats,
        barycenter_cotangent.reshape(rows, nx),
        cot,
        *sums,
    )

    far = send(to_far, "slab", chips)
    near = send(to_near, "slab", cores)
    y, shifted = pl.pallas_call(
        functools.partial(own_linear_kernel, ny=ny),
        in_specs=[smem] + [vmem] * 3,
        out_specs=[vmem, vmem],
        out_shape=[shape(rows, nx), shape(rows, nx)],
        compiler_params=params,
        name="own_linear",
    )(kz, ratio, potential, stats)

    def add(value, axis, patterns):
        return sum([send(value, axis, pairs) for pairs in patterns], value)

    def flips(hop):
        return [(i, i ^ hop) for i in range(slabs)]

    value = add(total, "slab", [cores])
    value = add(value, "atom", [ahead[k] for k in range(1, across)])
    value, y = in_order((value, y))
    value = add(value, "slab", [[(i, (i + k) % slabs) for i in range(slabs)] for k in (8, 16, 24)])
    value = add(value, "slab", [flips(2)])
    value, near, y = in_order((value, near, y))
    z = pl.pallas_call(
        functools.partial(gather_kernel, ny=ny),
        in_specs=[smem, smem, anywhere, anywhere, vmem, vmem],
        out_specs=vmem,
        out_shape=shape(rows, nx),
        scratch_shapes=[halo, pltpu.SemaphoreType.DMA((2,))],
        compiler_params=params,
        name="gather",
    )(where, kz, near, far, y, stats)
    value = add(value, "slab", [flips(4)])
    value, z = in_order((value, z))
    value = add(value, "atom", [swap])
    weight_grad = value[0, : weights.shape[0]] / (rows * nx * slabs)

    gradient = pl.pallas_call(
        gradient_kernel,
        in_specs=[vmem] * 6,
        out_specs=anywhere,
        out_shape=shape(rows, nx),
        scratch_shapes=[scratch[1], whole, pltpu.SemaphoreType.DMA((2,))],
        compiler_params=params,
        name="gradient",
    )(z, shifted, *tables)
    return gradient.reshape(atom_log_density.shape), weight_grad


def solution(mesh):
    return jax.shard_map(
        body,
        mesh=mesh,
        in_specs=(
            P("atom", "slab", None, None),
            P("atom", "slab", None, None),
            P("atom", "slab", None, None),
            P("slab", None, None),
            P(),
            P(),
            P(),
        ),
        out_specs=(P("atom", "slab", None, None), P()),
        check_vma=False,
    )
```

```python
import functools

import jax
import jax.numpy as jnp
from jax import lax
from jax.experimental import pallas as pl
from jax.experimental.pallas import tpu as pltpu
from jax.sharding import PartitionSpec as P

BAND_MAX = 8
GROUP = 4
F32 = jnp.float32
BF16 = jnp.bfloat16
VMEM_LIMIT = 16 * 1024 * 1024


def split(value):
    high = value.astype(BF16)
    return high, (value - high.astype(F32)).astype(BF16)


def dot(a, b):
    return jnp.dot(a, b, preferred_element_type=F32)


def dot3(ah, al, bh, bl):
    return dot(ah, bh) + (dot(al, bh) + dot(ah, bl))


def peak(value):
    return jnp.max(jnp.max(value, axis=0, keepdims=True), axis=1, keepdims=True)


def rows_of(values):
    return jnp.concatenate([jnp.broadcast_to(v, (1, 128)) for v in values], axis=0)


def tables_kernel(band, kyh, kyl, kxh, kxl, *, ny):
    def entries(sq, ok):
        return jnp.where(ok, jnp.exp(sq.astype(F32) * (-2.0 / (BAND_MAX * BAND_MAX))), 0.0)

    def offsets(shape):
        return lax.broadcasted_iota(jnp.int32, shape, 0), lax.broadcasted_iota(jnp.int32, shape, 1)

    row, col = offsets(kyh.shape)
    shift = ny.bit_length() - 1
    dy = row - col
    kyh[...], kyl[...] = split(entries(dy * dy, ((row >> shift) == (col >> shift)) & (jnp.abs(dy) <= band[1])))
    row, col = offsets(kxh.shape)
    dx = row - col
    kxh[...], kxl[...] = split(entries(dx * dx, jnp.abs(dx) <= band[0]))


def tile_loop(ny, nx, step):
    across = nx // 128

    def body_of(i, carry):
        row = pl.multiple_of(lax.div(i, across) * 8, 8)
        column = pl.multiple_of(lax.rem(i, across) * 128, 128)
        step(row, pl.ds(column, 128))
        return carry

    lax.fori_loop(0, ny // 8 * across, body_of, 0)


def own_planes(field, kz, y, ny, entry_lo, entry_hi):
    planes = field.shape[0] // ny
    taps = [kz[d] for d in range(BAND_MAX + 1)]

    def step(row, columns):
        e = [
            (entry_lo if 2 * q < planes else entry_hi)(field[pl.ds(q * ny + row, 8), columns])
            for q in range(planes)
        ]
        for p in range(planes):
            total = taps[0] * e[p]
            for d in range(1, BAND_MAX + 1):
                near = [e[q] for q in (p - d, p + d) if 0 <= q < planes]
                total += taps[d] * (near[0] if len(near) == 1 else near[0] + near[1])
            y[pl.ds(p * ny + row, 8), columns] = total

    tile_loop(ny, field.shape[1], step)


def halo_copies(near, far, halo, sems, core):
    return [
        pltpu.make_async_copy(near, halo.at[1 - core], sems.at[0]),
        pltpu.make_async_copy(far, halo.at[core], sems.at[1]),
    ]


def edge_copies(field, near, far, sems, core):
    half = near.shape[0]

    def rows(k):
        return pl.ds(pl.multiple_of(k * half, half), half)

    return [
        pltpu.make_async_copy(field.at[rows(1 - core)], near, sems.at[0]),
        pltpu.make_async_copy(field.at[rows(core)], far, sems.at[1]),
    ]


def halo_planes(halo, kz, y, z, ny, own, entry_left, entry_right):
    side = halo.shape[1] // ny
    taps = [kz[d] for d in range(BAND_MAX + 1)]

    def step(row, columns):
        e = [entry_left(halo[0, pl.ds(q * ny + row, 8), columns]) for q in range(side)]
        for p in range(side):
            rows = pl.ds(p * ny + row, 8)
            total = own(y[rows, columns])
            for q in range(max(0, p + side - BAND_MAX), side):
                total += taps[p + side - q] * e[q]
            z[rows, columns] = total
        e = [entry_right(halo[1, pl.ds(q * ny + row, 8), columns]) for q in range(side)]
        for p in range(side):
            rows = pl.ds((side + p) * ny + row, 8)
            total = own(y[rows, columns])
            for q in range(min(side, p + BAND_MAX - side + 1)):
                total += taps[side + q - p] * e[q]
            z[rows, columns] = total

    tile_loop(ny, halo.shape[2], step)


def tile(value):
    return jnp.broadcast_to(value, (8, 128))


def own_log_kernel(kz, field, y, stats, *, ny):
    half = field.shape[0] // 2
    m_lo, m_hi = peak(field[:half, :]), peak(field[half:, :])
    m = jnp.maximum(m_lo, m_hi)
    stats[...] = rows_of([m_lo, m_hi, m, m, m, m, m, m])
    m = tile(m)
    entry = lambda v: jnp.exp(v - m)
    own_planes(field, kz, y, ny, entry, entry)


def own_linear_kernel(kz, field, potential, stats, y, shifted, *, ny):
    c = stats[0:1, 0:1]
    shifted[...] = jnp.exp(potential[...] - c)
    f_lo = tile(jnp.exp((c - stats[1:2, 0:1]) * 0.5))
    f_hi = tile(jnp.exp((c - stats[2:3, 0:1]) * 0.5))
    own_planes(field, kz, y, ny, lambda v: v * f_lo * f_lo, lambda v: v * f_hi * f_hi)


def rows_and_columns(z, g, kyh, kyl, kxh, kxl, mid):
    half, block = mid.shape[0], kyh.shape[0]
    for k in range(half // block):
        rows = pl.ds(g * half + k * block, block)
        zh, zl = split(z[rows, :])
        mid[k * block : (k + 1) * block, :] = dot3(kyh[...], kyl[...], zh, zl)
    mh, ml = split(mid[...])
    return dot3(mh, ml, kxh[...], kxl[...])


def log_halos(where, kz, halo, y, stats, z, scale, ny):
    has_left, has_right = where[0] > 0, where[1] > 0
    m_own = stats[2:3, 0:1]
    m_left = jnp.where(has_left, peak(halo[0]), m_own)
    m_right = jnp.where(has_right, peak(halo[1]), m_own)
    c = jnp.maximum(m_own, jnp.maximum(m_left, m_right))
    scale[...] = rows_of([c, stats[0:1, 0:1], stats[1:2, 0:1], m_left, m_right, c, c, c])
    own = tile(jnp.exp(m_own - c))
    c = tile(c)
    halo_planes(
        halo,
        kz,
        y,
        z,
        ny,
        lambda v: v * own,
        lambda v: jnp.where(has_left, jnp.exp(v - c), 0.0),
        lambda v: jnp.where(has_right, jnp.exp(v - c), 0.0),
    )


def potential_kernel(
    where, kz, near, far, more, y_in, stats, density_in, kyh, kyl, kxh, kxl, potential, to_near, to_far,
    halo, y, density, z, mid, scale, sems, *, ny
):
    core = where[2]
    piece = far.shape[0]
    arriving = [
        pltpu.make_async_copy(near, halo.at[1 - core], sems.at[0]),
        pltpu.make_async_copy(far, halo.at[core, pl.ds(0, piece)], sems.at[1]),
        pltpu.make_async_copy(more, halo.at[core, pl.ds(piece, piece)], sems.at[4]),
    ]
    late = [pltpu.make_async_copy(y_in, y, sems.at[2]), pltpu.make_async_copy(density_in, density, sems.at[3])]
    for copy in arriving + late:
        copy.start()
    for copy in arriving + late[:1]:
        copy.wait()
    log_halos(where, kz, halo, y, stats, z, scale, ny)
    half = mid.shape[0]
    late[1].wait()
    for g in range(2):
        rows = slice(g * half, (g + 1) * half)
        first = rows_and_columns(z, g, kyh, kyl, kxh, kxl, mid)
        potential[rows, :] = density[rows, :] - (jnp.log(first) + scale[0:1, 0:1])
    leaving = edge_copies(potential, to_near, to_far, sems, core)
    for copy in leaving:
        copy.start()
    for copy in leaving:
        copy.wait()


def second_kernel(
    where, kz, near, far, y, stats, kyh, kyl, kxh, kxl, out, scale, halo, z, mid, sems, *, ny
):
    arriving = halo_copies(near, far, halo, sems, where[2])
    for copy in arriving:
        copy.start()
    for copy in arriving:
        copy.wait()
    log_halos(where, kz, halo, y, stats, z, scale, ny)
    half = mid.shape[0]
    for g in range(2):
        out[g * half : (g + 1) * half, :] = rows_and_columns(z, g, kyh, kyl, kxh, kxl, mid)


def ratio_kernel(
    at, weight, second, scale, bary, cot, sum0, sum1, sum2, sum3, out, to_near, to_far, total, sums, sems
):
    c = scale[0:1, 0:1]
    block, columns = sums.shape[1:]
    count = sums.shape[0]
    arriving = [
        pltpu.make_async_copy(ref, sums.at[k], sems.at[k]) for k, ref in enumerate((sum0, sum1, sum2, sum3))
    ]
    for copy in arriving:
        copy.start()
    partial = jnp.zeros((8, 128), F32)
    f_lo = jnp.exp((scale[1:2, 0:1] - c) * 0.5)
    f_hi = jnp.exp((scale[2:3, 0:1] - c) * 0.5)
    for k, copy in enumerate(arriving):
        copy.wait()
        g = lax.rem(at[0] + k, count)
        rows = pl.ds(pl.multiple_of(g * block, block), block)
        summed = bary[rows, :] + sums[k]
        denominator = second[rows, :]
        share = summed * (jnp.log(denominator) + c)
        share = jnp.sum(share.reshape(block // 8, 8, columns), axis=0)
        for m in range(columns // 128):
            partial += share[:, m * 128 : (m + 1) * 128]
        f = jnp.where(2 * g < count, f_lo, f_hi)
        out[rows, :] = (weight[0] * summed - cot[rows, :]) / denominator * f * f
    leaving = edge_copies(out, to_near, to_far, sems, at[2])
    for copy in leaving:
        copy.start()
    lanes = lax.broadcasted_iota(jnp.int32, total.shape, 1)
    partial = jnp.sum(jnp.sum(partial, axis=0, keepdims=True), axis=1, keepdims=True)
    total[...] = jnp.where(lanes == at[1], partial, 0.0)
    for copy in leaving:
        copy.wait()


def gather_kernel(where, kz, near, far, y, stats, z, halo, sems, *, ny):
    arriving = halo_copies(near, far, halo, sems, where[2])
    for copy in arriving:
        copy.start()
    c = stats[0:1, 0:1]
    f_left = tile(jnp.exp((c - stats[3:4, 0:1]) * 0.5))
    f_right = tile(jnp.exp((c - stats[4:5, 0:1]) * 0.5))
    has_left, has_right = where[0] > 0, where[1] > 0
    for copy in arriving:
        copy.wait()
    halo_planes(
        halo,
        kz,
        y,
        z,
        ny,
        lambda v: v,
        lambda v: jnp.where(has_left, v * f_left * f_left, 0.0),
        lambda v: jnp.where(has_right, v * f_right * f_right, 0.0),
    )


def gradient_kernel(z, shifted, kyh, kyl, kxh, kxl, out, mid, result, sems):
    half = mid.shape[0]
    leaving = []
    for g in range(out.shape[0] // half):
        rows = slice(g * half, (g + 1) * half)
        result[rows, :] = shifted[rows, :] * rows_and_columns(z, g, kyh, kyl, kxh, kxl, mid)
        leaving.append(pltpu.make_async_copy(result.at[rows], out.at[rows], sems.at[g]))
        leaving[-1].start()
    for copy in leaving:
        copy.wait()


def body(
    atom_log_density,
    prior_log_scaling,
    atom_cotangent_rows,
    barycenter_cotangent,
    weights,
    band,
    slot_atom_index,
):
    planes, ny, nx = barycenter_cotangent.shape
    slabs, atoms = lax.axis_size("slab"), lax.axis_size("atom")
    rows = planes * ny
    half = rows // 2
    block = GROUP * ny
    count = planes // GROUP
    slab_at, atom_at = lax.axis_index("slab"), lax.axis_index("atom")
    across = atoms // 2
    x_at = atom_at // 2

    smem = pl.BlockSpec(memory_space=pltpu.SMEM)
    vmem = pl.BlockSpec(memory_space=pltpu.VMEM)
    anywhere = pl.BlockSpec(memory_space=pl.ANY)
    hbm = pl.BlockSpec(memory_space=pltpu.HBM)
    params = pltpu.CompilerParams(vmem_limit_bytes=VMEM_LIMIT)

    def shape(*dims, dtype=F32):
        return jax.ShapeDtypeStruct(dims, dtype)

    def send(value, axis, pairs):
        return lax.ppermute(value, axis, pairs)

    in_order = lax.optimization_barrier
    cores = [(i, i ^ 1) for i in range(slabs)]
    chips = [(i, i + 1) for i in range(1, slabs - 1, 2)] + [(i + 1, i) for i in range(1, slabs - 1, 2)]
    core = slab_at % 2
    ahead = {
        k: [(2 * x + z, 2 * ((x + k) % across) + z) for x in range(across) for z in range(2)]
        for k in range(1, across)
    }
    swap = [(i, i ^ 1) for i in range(atoms)]

    cot = atom_cotangent_rows.reshape(rows, nx)

    def block_of(k):
        return lax.dynamic_slice_in_dim(cot, lax.rem(x_at + k, count) * block, block)

    blocks = [block_of(k) for k in range(1, across)]
    arrived = [send(blocks[k - 1], "atom", ahead[k]) for k in range(1, across)]

    y_shape, x_shape = (block, block), (nx, nx)
    distance = jnp.arange(BAND_MAX + 1, dtype=jnp.int32)
    kz = jnp.exp((distance * distance).astype(F32) * (-2.0 / (BAND_MAX * BAND_MAX)))
    kz = jnp.where(distance <= band[2], kz, 0.0)
    tables = pl.pallas_call(
        functools.partial(tables_kernel, ny=ny),
        out_shape=[shape(*dims, dtype=BF16) for dims in (y_shape, y_shape, x_shape, x_shape)],
        in_specs=[smem],
        out_specs=[vmem] * 4,
        compiler_params=params,
        name="tables",
    )(band)
    prior = prior_log_scaling.reshape(rows, nx)
    to_near = lax.dynamic_slice_in_dim(prior, (1 - core) * half, half)
    to_far = lax.dynamic_slice_in_dim(prior, core * half, half)
    far = [send(to_far[k : k + half // 2], "slab", chips) for k in (0, half // 2)]
    near = send(to_near, "slab", cores)

    where = jnp.stack([slab_at > 0, slab_at < slabs - 1, core > 0]).astype(jnp.int32)
    slot = lax.dynamic_slice_in_dim(slot_atom_index, atom_at, 1)
    onehot = (slot[0] == jnp.arange(weights.shape[0], dtype=jnp.int32)).astype(F32)
    weight = jnp.sum(onehot * weights, keepdims=True)

    own_out = [shape(rows, nx), shape(8, 128)]
    own_log = pl.pallas_call(
        functools.partial(own_log_kernel, ny=ny),
        in_specs=[smem, vmem],
        out_specs=[vmem, vmem],
        out_shape=own_out,
        compiler_params=params,
        name="own_log",
    )
    whole, halo = pltpu.VMEM((rows, nx), F32), pltpu.VMEM((2, half, nx), F32)
    scratch = [pltpu.VMEM((rows, nx), F32), pltpu.VMEM((half, nx), F32)]
    scale = pltpu.VMEM((8, 128), F32)

    y, stats = own_log(kz, prior)
    part = sum(arrived, block_of(0))
    y, part = in_order((y, part))
    swapped = send(part, "atom", swap)
    potential, to_near, to_far = pl.pallas_call(
        functools.partial(potential_kernel, ny=ny),
        in_specs=[smem, smem, hbm, hbm, hbm, hbm, vmem, hbm] + [vmem] * 4,
        out_specs=[vmem, anywhere, anywhere],
        out_shape=[shape(rows, nx), shape(half, nx), shape(half, nx)],
        scratch_shapes=[halo, whole, whole, *scratch, scale, pltpu.SemaphoreType.DMA((5,))],
        compiler_params=params,
        name="potential",
    )(where, kz, near, *far, y, stats, atom_log_density.reshape(rows, nx), *tables)

    far = send(to_far, "slab", chips)
    near = send(to_near, "slab", cores)
    both = part + swapped
    own_at, both = in_order((potential, both))
    sums = [both] + [send(both, "atom", ahead[across - k]) for k in range(1, across)]
    y, stats = own_log(kz, own_at)
    second, stats = pl.pallas_call(
        functools.partial(second_kernel, ny=ny),
        in_specs=[smem, smem, anywhere, anywhere] + [vmem] * 6,
        out_specs=[vmem, vmem],
        out_shape=[shape(rows, nx), shape(8, 128)],
        scratch_shapes=[halo, *scratch, pltpu.SemaphoreType.DMA((2,))],
        compiler_params=params,
        name="second",
    )(where, kz, near, far, y, stats, *tables)
    ratio, to_near, to_far, total = pl.pallas_call(
        ratio_kernel,
        in_specs=[smem, smem] + [vmem] * 4 + [anywhere] * 4,
        out_specs=[vmem, anywhere, anywhere, vmem],
        out_shape=[shape(rows, nx), shape(half, nx), shape(half, nx), shape(8, 128)],
        scratch_shapes=[
            pltpu.VMEM((count, block, nx), F32),
            pltpu.SemaphoreType.DMA((count,)),
        ],
        compiler_params=params,
        name="ratio",
    )(
        jnp.stack([x_at, slot[0], core]),
        weight,
        second,
        stats,
        barycenter_cotangent.reshape(rows, nx),
        cot,
        *sums,
    )

    far = send(to_far, "slab", chips)
    near = send(to_near, "slab", cores)
    y, shifted = pl.pallas_call(
        functools.partial(own_linear_kernel, ny=ny),
        in_specs=[smem] + [vmem] * 3,
        out_specs=[vmem, vmem],
        out_shape=[shape(rows, nx), shape(rows, nx)],
        compiler_params=params,
        name="own_linear",
    )(kz, ratio, potential, stats)

    def add(value, axis, patterns):
        return sum([send(value, axis, pairs) for pairs in patterns], value)

    def flips(hop):
        return [(i, i ^ hop) for i in range(slabs)]

    value = add(total, "slab", [cores])
    value = add(value, "atom", [ahead[k] for k in range(1, across)])
    value, y = in_order((value, y))
    value = add(value, "slab", [[(i, (i + k) % slabs) for i in range(slabs)] for k in (8, 16, 24)])
    value = add(value, "slab", [flips(2)])
    value, near, y = in_order((value, near, y))
    z = pl.pallas_call(
        functools.partial(gather_kernel, ny=ny),
        in_specs=[smem, smem, anywhere, anywhere, vmem, vmem],
        out_specs=vmem,
        out_shape=shape(rows, nx),
        scratch_shapes=[halo, pltpu.SemaphoreType.DMA((2,))],
        compiler_params=params,
        name="gather",
    )(where, kz, near, far, y, stats)
    value = add(value, "slab", [flips(4)])
    value, z = in_order((value, z))
    value = add(value, "atom", [swap])
    weight_grad = value[0, : weights.shape[0]] / (rows * nx * slabs)

    gradient = pl.pallas_call(
        gradient_kernel,
        in_specs=[vmem] * 6,
        out_specs=anywhere,
        out_shape=shape(rows, nx),
        scratch_shapes=[pltpu.VMEM((block, nx), F32), whole, pltpu.SemaphoreType.DMA((count,))],
        compiler_params=params,
        name="gradient",
    )(z, shifted, *tables)
    return gradient.reshape(atom_log_density.shape), weight_grad


def solution(mesh):
    return jax.shard_map(
        body,
        mesh=mesh,
        in_specs=(
            P("atom", "slab", None, None),
            P("atom", "slab", None, None),
            P("atom", "slab", None, None),
            P("slab", None, None),
            P(),
            P(),
            P(),
        ),
        out_specs=(P("atom", "slab", None, None), P()),
        check_vma=False,
    )
```
